256 devices in a mesh: comp: 32 (over z, x), vocab: 8 (over y, core).
Axes of the slice: x: 4, y: 4, z: 8, core: 2. Of those that a mesh axis runs over, the one named last changes fastest.
Arguments:
- hidden: bfloat16 [2048, 2048], P('comp'), may hold values from -6 to 6
- routes: int32 [2048, 4], P('comp'), may hold values from 0 to 63, all different within a row; in each aligned block of 64 rows (0 to 63, 64 to 127, ...) at most 8 rows name the same one
- targets: int32 [2048], P('comp'), may hold values from 0 to 16383
- saved_lse: float32 [2048, 4], P('comp'), as said below
- target_logprob: float32 [2048, 4], P('comp'), may hold values from -8 to -4
- prior_weight: bfloat16 [2048, 64], P('vocab'), may hold values from -0.25 to 0.25
- projection: bfloat16 [64, 2048, 2048], P('comp', None, 'vocab'), as said below
- embedding: bfloat16 [2048, 16384], P(None, 'vocab'), as said below
Outputs:
- grad_hidden: float32 [2048, 2048], P('comp', 'vocab')
- grad_prior: float32 [2048, 64], P('vocab')
- grad_projection: bfloat16 [64, 2048, 2048], P('comp', None, 'vocab')
- grad_embedding: bfloat16 [2048, 16384], P('comp', 'vocab')
The draws below stay inside these ranges and needn't reach their ends.
Inputs may be any that keep to these rules, and one draw needn't show every extreme that they name: `routes`: in each aligned block of 64 rows (the tokens of one index of comp) the 4 entries of a row differ, and no component is named by more than 8 rows; some component reaches 8 in some block. `projection`: entries lie within 4 / sqrt(2048) of zero. `embedding`: entries lie within 6.5 / sqrt(2048) of zero. `saved_lse`: each entry lies between ln(16384) - 2.7 and ln(16384) - 0.9.
All inputs are finite; a program needn't handle non-finite values.
Results may differ from the reference program's by a relative error of at most 0.0056.
Values may be sent and summed in bfloat16 or wider, within the bound.
No kernel may reach another device: no remote copies, remote signals or barrier semaphores. Data moves between devices by JAX's collectives and lax.ppermute only.
A program may use at most 128 MiB of HBM per device.

```python
import math
import jax
import jax.numpy as jnp
import numpy as np
from jax import lax

D = 2048
TOP = 4
TOK_DEV = 64
VOCAB = 16384
COMPONENTS = 64
TOKENS = 2048
CAP = 8
N_COMP = 32


def draw_hidden(key, part):
    own_key = jax.random.fold_in(key, 12)
    values = jnp.clip(jax.random.normal(own_key, (TOKENS, D), jnp.float32), -6.0, 6.0)
    return values.astype(jnp.bfloat16)


def draw_projection(key, part):
    own_key = jax.random.fold_in(key, 22)
    factor = 1.0 / jnp.sqrt(jnp.float32(D))
    values = jnp.clip(jax.random.normal(own_key, (COMPONENTS, D, D), jnp.float32), -4.0, 4.0) * factor
    return values.astype(jnp.bfloat16)


def draw_embedding(key, part):
    own_key = jax.random.fold_in(key, 31)
    factor = 1.6 / jnp.sqrt(jnp.float32(D))
    values = jnp.clip(jax.random.normal(own_key, (D, VOCAB), jnp.float32), -4.0, 4.0) * factor
    return values.astype(jnp.bfloat16)


def draw_saved_lse(key, part):
    own_key = jax.random.fold_in(key, 41)
    center = jnp.log(jnp.float32(VOCAB)) + 0.5
    offset = jax.random.uniform(own_key, (TOKENS, TOP), jnp.float32, 1.6, 3.0)
    return (center - offset).astype(jnp.float32)


def plant(values, key, smallest, largest):
    longest = values.shape.index(max(values.shape))
    spots = []
    for shift in (0, 1):
        where = [jax.random.randint(jax.random.fold_in(key, axis), (), 0, length) for axis, length in enumerate(values.shape)]
        where[longest] = (where[longest] + shift) % values.shape[longest]
        spots.append(tuple(where))
    return values.at[spots[0]].set(smallest).at[spots[1]].set(largest)


def steps_of(stream_key, shape, pieces, least, top_value):
    def one(dim, parts):
        steps = jax.random.uniform(jax.random.fold_in(jax.random.fold_in(stream_key, 6), dim), (parts,), jnp.float32, least / len(pieces), top_value / len(pieces))
        return jnp.repeat(jnp.exp(steps), shape[dim] // parts).reshape((-1,) + (1,) * (len(shape) - dim - 1))

    gain = one(*pieces[0])
    for cut in pieces[1:]:
        gain = gain * one(*cut)
    return gain


def deal_out(rng, own, number, rows, number_of, top, limit, slope):
    ranking = jax.random.permutation(rng, number_of)
    heavy_load, common = portions_of(number_of, rows * top, limit, slope, True), portions_of(number_of, rows * top, limit, slope, False)
    places = jnp.arange(number_of)

    def named(tallies, rotation):
        used = int((tallies > 0).sum())
        fixed = max(1, used // 4)
        moved = fixed + (places - fixed + rotation * (used - fixed)) % max(1, number_of - fixed)
        return jnp.zeros((number_of,), jnp.int32).at[ranking[jnp.where(places < fixed, places, moved)]].set(jnp.asarray(tallies, jnp.int32))

    tallies = jnp.where(number % 4 == 0, named(heavy_load, number // 4), named(common, number - number // 4 - 1))
    mixed = jax.random.permutation(jax.random.fold_in(own, 3), number_of)
    giver, taker = mixed[0:number_of // 2 * 2:2], mixed[1:number_of // 2 * 2:2]
    margin = jnp.minimum(tallies[giver] - 1, limit - tallies[taker]) // 2
    margin = jnp.where((giver == ranking[0]) | (taker == ranking[0]) | (tallies[taker] == 0), 0, jnp.maximum(margin, 0))
    moved = jax.random.randint(jax.random.fold_in(own, 4), (number_of // 2,), 0, 1 << 20) % (margin + 1)
    tallies = tallies.at[giver].add(-moved).at[taker].add(moved)
    labels = jnp.searchsorted(jnp.cumsum(tallies), jnp.arange(rows * top), side="right").astype(jnp.int32)
    grid = labels.reshape(top, rows).T
    grid = grid[jax.random.permutation(jax.random.fold_in(own, 1), rows)]
    rotation = jax.random.randint(jax.random.fold_in(own, 2), (rows, 1), 0, top)
    return jnp.take_along_axis(grid, (jnp.arange(top)[None, :] + rotation) % top, axis=1)


def portions_of(count, total, bound, lean, full):
    weights = [(1 << 20) // math.isqrt(rank ** lean) + 1 for rank in range(1, count + 1)]
    largest = bound if full else min(bound, max(-(-total // count), total * weights[0] // sum(weights)))
    least = 1 if total - largest >= count - 1 else 0
    holding, surplus = [largest] + [least] * (count - 1), total - largest - least * (count - 1)
    while surplus > 0:
        candidates = [i for i in range(1, count) if holding[i] < largest] or [i for i in range(1, count) if holding[i] < bound]
        pool, left = sum([weights[i] for i in candidates]), surplus
        for i in candidates:
            more = min(bound - holding[i], max(1, left * weights[i] // pool), surplus)
            holding[i] = holding[i] + more
            surplus = surplus - more
    return np.array(holding)


def noise(stream_key, dims, scale, most, split=(), kind=jnp.bfloat16):
    drawn = jax.random.normal(stream_key, dims, jnp.float32) * scale
    if len(split) > 0:
        drawn = steps_of(stream_key, dims, split, -0.22, 0.18) * drawn
    return jnp.clip(drawn, min=-most, max=most).astype(kind)


def setup_inputs(seed: int = 0) -> dict:
    key_list = jax.random.split(jax.random.key(seed), 9)
    hidden = draw_hidden(jax.random.fold_in(key_list[8], 71), 0)
    routes_keys = jax.random.split(jax.random.fold_in(key_list[1], 1), TOKENS // TOK_DEV)
    routes_turns = jax.random.permutation(jax.random.fold_in(key_list[1], 3), TOKENS // TOK_DEV)
    routes = jax.vmap(lambda own, number: deal_out(jax.random.fold_in(key_list[1], 2), own, number, TOK_DEV, COMPONENTS, TOP, CAP, 2))(routes_keys, routes_turns).reshape((TOKENS, TOP))
    targets = plant(jax.random.randint(key_list[2], (TOKENS,), 0, VOCAB), jax.random.fold_in(key_list[2], 1), 0, VOCAB - 1).astype(jnp.int32)
    saved_lse = draw_saved_lse(jax.random.fold_in(key_list[8], 71), 0)
    target_logprob = jnp.clip(-8.0 + 4.0 * jax.random.uniform(key_list[4], (TOKENS, TOP), jnp.float32) ** steps_of(key_list[4], (TOKENS, TOP), ((0, 32),), -0.2, 0.2), -8.0, -4.0)
    prior_weight = noise(key_list[5], (D, COMPONENTS), (D // 4) ** -0.5, 0.25, ((0, 8),))
    projection = draw_projection(jax.random.fold_in(key_list[8], 71), 0)
    embedding = draw_embedding(jax.random.fold_in(key_list[8], 71), 0)
    return {"hidden": hidden, "routes": routes, "targets": targets, "saved_lse": saved_lse, "target_logprob": target_logprob, "prior_weight": prior_weight, "projection": projection, "embedding": embedding}


def reference(hidden, routes, targets, saved_lse, target_logprob, prior_weight, projection, embedding):
    highest = lax.Precision.HIGHEST
    prior_logits = jnp.dot(hidden, prior_weight, preferred_element_type=jnp.float32)
    selected = jnp.take_along_axis(prior_logits, routes, axis=1)
    gate_weights = jax.nn.softmax(selected, axis=-1)
    posterior = jax.nn.softmax(jax.nn.log_softmax(selected, axis=-1) + target_logprob, axis=-1)
    picked = (routes[:, :, None] == jnp.arange(COMPONENTS, dtype=jnp.int32)[None, None, :]).astype(jnp.float32)
    prior_grads = jnp.sum((gate_weights - posterior)[:, :, None] * picked, axis=1)
    grad_prior = jnp.dot(hidden.astype(jnp.float32).T, prior_grads, precision=highest)
    prior_back = jnp.dot(prior_grads, prior_weight.astype(jnp.float32).T, precision=highest)

    slot_rows = N_COMP * CAP
    pair_comp = routes.reshape(N_COMP, TOK_DEV * TOP).astype(jnp.int32)
    pair_onehot = (pair_comp[:, :, None] == jnp.arange(COMPONENTS, dtype=jnp.int32)[None, None, :]).astype(jnp.int32)
    earlier = (jnp.cumsum(pair_onehot, axis=1) - pair_onehot).astype(jnp.int32)
    pair_rank = jnp.sum(earlier * pair_onehot, axis=2).astype(jnp.int32)
    block_ids = jnp.arange(N_COMP, dtype=jnp.int32)[:, None]
    position = (pair_comp * slot_rows + block_ids * CAP + pair_rank).reshape(-1).astype(jnp.int32)
    pair_token = jnp.repeat(jnp.arange(TOKENS, dtype=jnp.int32), TOP)
    slot_total = COMPONENTS * slot_rows
    rows_all = jnp.zeros((slot_total, D), hidden.dtype).at[position].set(hidden[pair_token])
    post_all = jnp.zeros((slot_total,), jnp.float32).at[position].set(posterior.reshape(-1))
    lse_all = jnp.zeros((slot_total,), jnp.float32).at[position].set(saved_lse.reshape(-1))
    target_all = jnp.zeros((slot_total,), jnp.int32).at[position].set(targets[pair_token].astype(jnp.int32))
    vocab_ids = jnp.arange(VOCAB, dtype=jnp.int32)

    def component(running, inputs):
        slot_input, weight, post_rows, lse_rows, target_rows = inputs
        preact = jnp.dot(slot_input, weight, preferred_element_type=jnp.float32)
        tanh_value = jnp.tanh(preact)
        z_rows = tanh_value.astype(jnp.bfloat16)
        logits = jnp.dot(z_rows, embedding, preferred_element_type=jnp.float32)
        target_hit = (target_rows[:, None] == vocab_ids[None, :]).astype(jnp.float32)
        logit_grads = (post_rows[:, None] * (jnp.exp(logits - lse_rows[:, None]) - target_hit)).astype(jnp.bfloat16)
        feature_grads = lax.dot_general(logit_grads, embedding, (((1,), (1,)), ((), ())), preferred_element_type=jnp.float32)
        pre_grads = (feature_grads * (1.0 - tanh_value * tanh_value)).astype(jnp.bfloat16)
        grad_weight = lax.dot_general(slot_input, pre_grads, (((0,), (0,)), ((), ())), preferred_element_type=jnp.float32).astype(jnp.bfloat16)
        slot_grads = lax.dot_general(pre_grads, weight, (((1,), (1,)), ((), ())), preferred_element_type=jnp.float32)
        embed_part = lax.dot_general(z_rows, logit_grads, (((0,), (0,)), ((), ())), preferred_element_type=jnp.float32)
        return running + embed_part, (grad_weight, slot_grads)

    start_sum = jnp.zeros((D, VOCAB), jnp.float32)
    inputs = (rows_all.reshape(COMPONENTS, slot_rows, D), projection, post_all.reshape(COMPONENTS, slot_rows),
              lse_all.reshape(COMPONENTS, slot_rows), target_all.reshape(COMPONENTS, slot_rows))
    embed_sum, (grad_projection, slot_grads) = lax.scan(component, start_sum, inputs)
    pair_grads = slot_grads.reshape(slot_total, D)[position].reshape(TOKENS, TOP, D)
    grad_hidden = jnp.sum(pair_grads, axis=1) + prior_back
    return grad_hidden, grad_prior, grad_projection, embed_sum.astype(jnp.bfloat16)
```

```python
import jax
import jax.numpy as jnp
from jax import lax
from jax.sharding import Mesh
from jax.sharding import PartitionSpec as P

ZX = ("z", "x")
YC = ("y", "c")
ALL = ("z", "x", "y", "c")
BF = jnp.bfloat16
F32 = jnp.float32


def shifted(value, axis, by):
    n = lax.axis_size(axis)
    return lax.ppermute(value, axis, [(i, (i + by) % n) for i in range(n)])


def flipped(value, axis, bit):
    n = lax.axis_size(axis)
    return lax.ppermute(value, axis, [(i, i ^ bit) for i in range(n)])


def summed_by_flips(value, axes):
    for axis in axes:
        bit = 1
        while bit < lax.axis_size(axis):
            value = value + flipped(value, axis, bit)
            bit *= 2
    return value


def ring_sum(term, axis):
    n = lax.axis_size(axis)
    far = term(n // 2).astype(BF)
    half = far.shape[0] // 2
    up = shifted(far[:half], axis, 1)
    down = shifted(far[half:], axis, -1)
    for k in range(n // 2 - 1, 0, -1):
        ahead, behind = term(k), term(-k)
        if k == n // 2 - 1:
            ahead = jnp.concatenate([ahead[:half] + up, ahead[half:]], axis=0)
            behind = jnp.concatenate([behind[:half], behind[half:] + down], axis=0)
        else:
            ahead, behind = ahead + up, behind + down
        up = shifted(ahead.astype(BF), axis, 1)
        down = shifted(behind.astype(BF), axis, -1)
    return term(0) + up + down


def pick(value, index, dim):
    return lax.dynamic_index_in_dim(value, index, dim, keepdims=False)


def gathered(value):
    yi, ci = lax.axis_index("y"), lax.axis_index("c")
    half = value.shape[0] // 2
    below = shifted(value, "y", 1)
    above = shifted(value, "y", -1)
    far_low = shifted(below[:half], "y", 1)
    far_high = shifted(above[half:], "y", -1)
    far = jnp.concatenate([far_low, far_high], axis=0)
    mine = jnp.stack([value, above, far, below])
    other = flipped(mine, "c", 1)
    pairs = jnp.where(ci == 0, jnp.stack([mine, other], 1), jnp.stack([other, mine], 1))
    return lax.dynamic_slice_in_dim(jnp.concatenate([pairs, pairs], 0), (4 - yi) % 4, 4, 0)


def vocab_sum(part):
    yi, ci = lax.axis_index("y"), lax.axis_index("c")
    theirs = part(1 - ci)
    swapped = flipped(theirs.astype(BF), "c", 1)
    ours = part(ci)
    both = ours + swapped

    def term(k):
        return pick(both, (yi + k + 4) % 4, 0)

    return ring_sum(term, "y")


def shards(hidden, routes, targets, saved_lse, target_logprob, prior_weight, projection, embedding):
    highest = lax.Precision.HIGHEST
    tok_dev, _ = hidden.shape
    route_count = routes.shape[1]
    comp_dev, _, col_count = projection.shape
    voc_dev = embedding.shape[1]
    owners = lax.axis_size(ZX)
    experts_all = comp_dev * owners
    capacity = max(2, (2 * tok_dev * route_count + experts_all - 1) // experts_all)
    slot_count = owners * comp_dev * capacity
    slot_rows = owners * capacity
    zi, xi, yi, ci = (lax.axis_index(a) for a in ALL)
    vocab_index = yi * 2 + ci
    own_cols = lax.dynamic_slice_in_dim(hidden, vocab_index * col_count, col_count, 1)

    comp_ids = jnp.arange(experts_all, dtype=jnp.int32)
    pair_comp = routes.reshape(-1)
    pair_onehot = (pair_comp[:, None] == comp_ids[None, :]).astype(jnp.bfloat16)
    pair_total = pair_comp.shape[0]
    before = (
        jnp.arange(pair_total)[:, None] > jnp.arange(pair_total)[None, :]
    ).astype(jnp.bfloat16)
    earlier = jnp.dot(before, pair_onehot, preferred_element_type=F32)
    pair_rank = jnp.sum(earlier * pair_onehot.astype(F32), axis=1).astype(jnp.int32)
    pair_slot = pair_comp * capacity + pair_rank
    slot_ids = jnp.arange(slot_count, dtype=jnp.int32)
    dispatch_pairs = (slot_ids[:, None] == pair_slot[None, :]).astype(F32)
    dispatch_tokens = jnp.sum(dispatch_pairs.reshape(slot_count, tok_dev, route_count), axis=2).astype(BF)
    send_rows = jnp.dot(dispatch_tokens, own_cols, preferred_element_type=F32).astype(BF)
    got_rows = lax.all_to_all(
        send_rows.reshape(owners, comp_dev * capacity, col_count), ZX, 0, 0, tiled=True
    )

    partial_logits = jnp.dot(own_cols, prior_weight, preferred_element_type=F32)
    prior_logits = summed_by_flips(partial_logits, ("c", "y"))
    picked = (routes[:, :, None] == comp_ids[None, None, :]).astype(F32)
    selected = jnp.sum(picked * prior_logits[:, None, :], axis=2)
    gate_weights = jax.nn.softmax(selected, axis=-1)
    posterior = jax.nn.softmax(jax.nn.log_softmax(selected, axis=-1) + target_logprob, axis=-1)
    prior_grads = jnp.sum((gate_weights - posterior)[:, :, None] * picked, axis=1)
    pair_targets = jnp.repeat(targets, route_count).astype(F32)
    meta = jnp.stack([saved_lse.reshape(-1), posterior.reshape(-1), pair_targets], 0)
    send_meta = jnp.sum(dispatch_pairs[:, None, :] * meta[None, :, :], axis=2)
    send_meta = jnp.moveaxis(
        send_meta.reshape(owners, comp_dev * capacity, 3), 2, 1
    ).reshape(owners, -1)
    got_meta = lax.all_to_all(send_meta, ZX, 0, 0, tiled=True)
    got_meta = got_meta.reshape(owners, 3, comp_dev, capacity).transpose(1, 2, 0, 3)
    got_meta = got_meta.reshape(3, comp_dev * slot_rows)
    lse_rows, post_rows, target_rows = got_meta[0], got_meta[1], got_meta[2].astype(jnp.int32)

    rows_own = got_rows.reshape(owners, comp_dev, capacity, col_count).transpose(3, 1, 0, 2)
    rows_own = rows_own.reshape(col_count, comp_dev, slot_rows)
    rows_in = gathered(rows_own).reshape(-1, comp_dev, slot_rows)
    preact = jnp.einsum("dkr,kde->ekr", rows_in, projection, preferred_element_type=F32)
    tanh_value = jnp.tanh(preact)
    z_all = gathered(tanh_value.astype(BF)).reshape(-1, comp_dev * slot_rows)

    logits = jnp.einsum("dr,dv->rv", z_all, embedding, preferred_element_type=F32)
    vocab_ids = vocab_index * voc_dev + jnp.arange(voc_dev, dtype=jnp.int32)
    target_hit = (target_rows[:, None] == vocab_ids[None, :]).astype(F32)
    logit_grads = (
        post_rows[:, None] * (jnp.exp(logits - lse_rows[:, None]) - target_hit)
    ).astype(BF)
    logit_grads, z_all = lax.optimization_barrier((logit_grads, z_all))

    blocks = embedding.reshape(4, 2, col_count, voc_dev)

    def feature_part(c):
        return jnp.einsum("yev,rv->yer", pick(blocks, c, 1), logit_grads, preferred_element_type=F32)

    feature_grads = vocab_sum(feature_part).reshape(tanh_value.shape)
    pre_grads = (feature_grads * (1.0 - tanh_value * tanh_value)).astype(BF)
    grad_projection = jnp.einsum(
        "dkr,ekr->kde", rows_in, pre_grads, preferred_element_type=F32
    ).astype(BF)
    slot_blocks = projection.reshape(comp_dev, 4, 2, col_count, col_count)

    def slot_part(c):
        return jnp.einsum("ekr,kyde->ykrd", pre_grads, pick(slot_blocks, c, 2), preferred_element_type=F32)

    slot_grads = vocab_sum(slot_part).astype(BF)
    slot_grads = slot_grads.reshape(comp_dev, owners, capacity, col_count).transpose(1, 0, 2, 3)
    returned = lax.all_to_all(
        slot_grads.reshape(owners, comp_dev * capacity, col_count), ZX, 0, 0, tiled=True
    )
    route_grads = lax.dot_general(
        dispatch_tokens,
        returned.reshape(slot_count, col_count),
        (((0,), (0,)), ((), ())),
        preferred_element_type=F32,
    )
    prior_back = lax.dot_general(
        prior_grads, prior_weight.astype(F32), (((1,), (1,)), ((), ())), precision=highest
    )
    grad_hidden = route_grads + prior_back
    prior_local = lax.dot_general(
        own_cols.astype(F32), prior_grads, (((0,), (0,)), ((), ())), precision=highest
    )
    grad_prior = summed_by_flips(prior_local, ("x", "z"))

    words = voc_dev // 2
    z_major = z_all.reshape(8, 4 * 64, -1)
    x_major = z_all.reshape(8, 4, 64, -1)

    def z_term(k):
        return jnp.dot(
            pick(z_major, (zi + k + 8) % 8, 0), logit_grads[:, :words], preferred_element_type=F32
        )

    def x_term(k):
        rows = pick(x_major, (xi + k + 4) % 4, 1).reshape(8 * 64, -1)
        return jnp.dot(rows, logit_grads[:, words:], preferred_element_type=F32)

    z_first = ring_sum(z_term, "z").reshape(4, 64, words)
    x_first = ring_sum(x_term, "x").reshape(8, 64, words)
    z_then_x = ring_sum(lambda k: pick(z_first, (xi + k + 4) % 4, 0), "x")
    x_then_z = ring_sum(lambda k: pick(x_first, (zi + k + 8) % 8, 0), "z")
    grad_embedding = jnp.concatenate([z_then_x, x_then_z], axis=1).astype(BF)
    return (grad_hidden, grad_prior, grad_projection, grad_embedding)


def solution(mesh):
    finer = Mesh(mesh.devices.reshape(8, 4, 4, 2), ALL)
    in_specs = (
        P(ZX, None),
        P(ZX, None),
        P(ZX),
        P(ZX, None),
        P(ZX, None),
        P(YC, None),
        P(ZX, None, YC),
        P(None, YC),
    )
    out_specs = (P(ZX, YC), P(YC, None), P(ZX, None, YC), P(ZX, YC))
    return jax.shard_map(
        shards, mesh=finer, in_specs=in_specs, out_specs=out_specs, check_vma=False
    )
```

```python
import functools

import jax
import jax.numpy as jnp
from jax import lax
from jax.experimental import pallas as pl
from jax.experimental.pallas import tpu as pltpu
from jax.sharding import Mesh
from jax.sharding import PartitionSpec as P

ZX = ("z", "x")
YC = ("y", "c")
ALL = ("z", "x", "y", "c")
BF = jnp.bfloat16
F32 = jnp.float32
WHOLE = pl.BlockSpec(memory_space=pltpu.VMEM)
SCALARS = pl.BlockSpec(memory_space=pltpu.SMEM)


def shifted(value, axis, by):
    n = lax.axis_size(axis)
    return lax.ppermute(value, axis, [(i, (i + by) % n) for i in range(n)])


def flipped(value, axis, bit):
    n = lax.axis_size(axis)
    return lax.ppermute(value, axis, [(i, i ^ bit) for i in range(n)])


def summed_by_flips(value, axes):
    for axis in axes:
        bit = 1
        while bit < lax.axis_size(axis):
            value = value + flipped(value, axis, bit)
            bit *= 2
    return value


def ring_sum(term, axis):
    n = lax.axis_size(axis)
    far = term(n // 2)
    half = far.shape[0] // 2
    up = shifted(far[:half], axis, 1)
    down = shifted(far[half:], axis, -1)
    for k in range(n // 2 - 1, 0, -1):
        if k == n // 2 - 1:
            ahead, behind = term(k, first=up), term(-k, second=down)
        else:
            ahead, behind = term(k, whole=(up,)), term(-k, whole=(down,))
        up = shifted(ahead, axis, 1)
        down = shifted(behind, axis, -1)
    return term(0, whole=(up, down), last=True)


def plus(block, first=None, second=None, whole=(), last=False):
    half = block.shape[0] // 2
    if first is not None:
        block = jnp.concatenate([block[:half] + first, block[half:]], axis=0)
    if second is not None:
        block = jnp.concatenate([block[:half], block[half:] + second], axis=0)
    for other in whole:
        block = block + other
    return block if last else block.astype(BF)


def pick(value, index, dim):
    return lax.dynamic_index_in_dim(value, index, dim, keepdims=False)


def gathered(value):
    half = value.shape[0] // 2
    below = shifted(value, "y", 1)
    above = shifted(value, "y", -1)
    far_low = shifted(below[:half], "y", 1)
    far_high = shifted(above[half:], "y", -1)
    mine = (value, above, below, far_low, far_high)
    return mine + tuple(flipped(piece, "c", 1) for piece in mine)


def vocab_sum(part):
    yi, ci = lax.axis_index("y"), lax.axis_index("c")
    swapped = flipped(part(1 - ci).astype(BF), "c", 1)
    both = part(ci) + swapped

    def term(k, **arrived):
        return plus(pick(both, (yi + k + 4) % 4, 0), **arrived)

    return ring_sum(term, "y")


def piece_rows(refs, k, rows):
    for side in range(2):
        value, above, below, low, high = refs[5 * side : 5 * side + 5]
        span = slice(k * rows, (k + 1) * rows)
        yield 0, side, value[span, :]
        yield 1, side, above[span, :]
        yield 3, side, below[span, :]
        yield 2, side, (low, high)[k][...]


def block_start(pos, dist, side, cols):
    y = lax.rem(pos[0] + dist, 4)
    c = pos[1] if side == 0 else 1 - pos[1]
    return pl.multiple_of((y * 2 + c) * cols, cols)


def activation_kernel(pos, *refs):
    pieces, (proj, slope, z) = refs[:10], refs[10:]
    comps, _, cols = proj.shape
    rows = slope.shape[0] // comps
    for k in range(comps):
        total = jnp.zeros((rows, cols), F32)
        for dist, side, x in piece_rows(pieces, k, rows):
            w = proj[k, pl.ds(block_start(pos, dist, side, x.shape[1]), x.shape[1]), :]
            total += jnp.dot(x, w, preferred_element_type=F32)
        t = jnp.tanh(total)
        slope[k * rows : (k + 1) * rows, :] = 1.0 - t * t
        z[k * rows : (k + 1) * rows, :] = t.astype(BF)


def projection_kernel(pos, *refs):
    pieces, (pre, out) = refs[:10], refs[10:]
    comps = out.shape[0]
    rows = pre.shape[0] // comps
    for k in range(comps):
        g = pre[k * rows : (k + 1) * rows, :]
        for dist, side, x in piece_rows(pieces, k, rows):
            value = lax.dot_general(x, g, (((0,), (0,)), ((), ())), preferred_element_type=F32)
            out[k, pl.ds(block_start(pos, dist, side, x.shape[1]), x.shape[1]), :] = value.astype(BF)


def logit_kernel(pos, *refs):
    pieces, (lse, post, target, emb, lg, z_rows, z) = refs[:10], refs[10:]
    step = pl.program_id(0)
    rows, cols = pieces[0].shape
    half = rows // 2

    @pl.when(step == 0)
    def _():
        for k in range(2):
            for dist, side, x in piece_rows(pieces, k, half):
                start = block_start(pos, dist, side, cols)
                z[k * half : (k + 1) * half, pl.ds(start, cols)] = x
                z_rows[pl.ds(start, cols), k * half : (k + 1) * half] = x.T

    width = emb.shape[1]
    logits = jnp.dot(z[...], emb[...], preferred_element_type=F32)
    first = pos[2] + step * width
    words = first + lax.broadcasted_iota(jnp.int32, logits.shape, 1)
    hit = (target[...] == words).astype(F32)
    lg[...] = (post[...] * (jnp.exp(logits - lse[...]) - hit)).astype(BF)


def outer_kernel(first, second, whole, idx, z, lg, *refs):
    out = refs[-1]
    z = z[...].reshape(-1, z.shape[-1])
    value = jnp.dot(z, lg[...], preferred_element_type=F32)
    half = value.shape[0] // 2
    arrived = refs[:-1]
    if first:
        out[:half] = (value[:half] + arrived[0][...]).astype(out.dtype)
        out[half:] = value[half:].astype(out.dtype)
    elif second:
        out[:half] = value[:half].astype(out.dtype)
        out[half:] = (value[half:] + arrived[0][...]).astype(out.dtype)
    else:
        for other in arrived:
            value = value + other[...]
        out[...] = value.astype(out.dtype)


def outer_part(z_view, lg, index, side, first=None, second=None, whole=(), last=False):
    outer, _, inner, slots = z_view.shape
    words = lg.shape[1] // 2
    rows = outer * inner
    arrived = [a for a in (first, second, *whole) if a is not None]
    return pl.pallas_call(
        functools.partial(outer_kernel, first is not None, second is not None, len(whole)),
        grid_spec=pltpu.PrefetchScalarGridSpec(
            num_scalar_prefetch=1,
            grid=(1,),
            in_specs=[
                pl.BlockSpec((outer, 1, inner, slots), lambda i, n: (0, n[0], 0, 0)),
                pl.BlockSpec((slots, words), lambda i, n: (0, side)),
            ]
            + [pl.BlockSpec(a.shape, lambda i, n: (0, 0)) for a in arrived],
            out_specs=pl.BlockSpec((rows, words), lambda i, n: (0, 0)),
        ),
        out_shape=jax.ShapeDtypeStruct((rows, words), F32 if last else BF),
        compiler_params=pltpu.CompilerParams(vmem_limit_bytes=24 << 20),
        cost_estimate=pl.CostEstimate(
            flops=2 * rows * words * slots, bytes_accessed=6 * rows * words, transcendentals=0
        ),
    )(index.reshape(1).astype(jnp.int32), z_view, lg, *arrived)


def shards(hidden, routes, targets, saved_lse, target_logprob, prior_weight, projection, embedding):
    highest = lax.Precision.HIGHEST
    tok_dev, model_width = hidden.shape
    route_count = routes.shape[1]
    comp_dev, _, col_count = projection.shape
    voc_dev = embedding.shape[1]
    owners = lax.axis_size(ZX)
    experts_all = comp_dev * owners
    capacity = max(2, (2 * tok_dev * route_count + experts_all - 1) // experts_all)
    slot_count = owners * comp_dev * capacity
    slot_rows = owners * capacity
    slots = comp_dev * slot_rows
    zi, xi, yi, ci = (lax.axis_index(a) for a in ALL)
    vocab_index = yi * 2 + ci
    pos = jnp.stack([yi, ci, vocab_index * voc_dev]).astype(jnp.int32)
    own_cols = lax.dynamic_slice_in_dim(hidden, vocab_index * col_count, col_count, 1)

    comp_ids = jnp.arange(experts_all, dtype=jnp.int32)
    pair_comp = routes.reshape(-1)
    pair_onehot = (pair_comp[:, None] == comp_ids[None, :]).astype(BF)
    pair_total = pair_comp.shape[0]
    before = (jnp.arange(pair_total)[:, None] > jnp.arange(pair_total)[None, :]).astype(BF)
    earlier = jnp.dot(before, pair_onehot, preferred_element_type=F32)
    pair_rank = jnp.sum(earlier * pair_onehot.astype(F32), axis=1).astype(jnp.int32)
    pair_slot = pair_comp * capacity + pair_rank
    slot_ids = jnp.arange(slot_count, dtype=jnp.int32)
    dispatch_pairs = (slot_ids[:, None] == pair_slot[None, :]).astype(F32)
    dispatch_tokens = jnp.sum(dispatch_pairs.reshape(slot_count, tok_dev, route_count), axis=2).astype(BF)
    send_rows = jnp.dot(dispatch_tokens, own_cols, preferred_element_type=F32).astype(BF)
    got_rows = lax.all_to_all(
        send_rows.reshape(owners, comp_dev * capacity, col_count), ZX, 0, 0, tiled=True
    )

    partial_logits = jnp.dot(own_cols, prior_weight, preferred_element_type=F32)
    prior_logits = summed_by_flips(partial_logits, ("c", "y"))
    picked = (routes[:, :, None] == comp_ids[None, None, :]).astype(F32)
    selected = jnp.sum(picked * prior_logits[:, None, :], axis=2)
    gate_weights = jax.nn.softmax(selected, axis=-1)
    posterior = jax.nn.softmax(jax.nn.log_softmax(selected, axis=-1) + target_logprob, axis=-1)
    pair_grads = gate_weights - posterior
    prior_grads = jnp.sum(pair_grads[:, :, None] * picked, axis=1)
    pair_targets = jnp.repeat(targets, route_count).astype(F32)
    meta = [saved_lse.reshape(-1), posterior.reshape(-1), pair_targets, pair_grads.reshape(-1)]
    send_meta = jnp.stack(
        [jnp.sum(dispatch_pairs * m[None, :], axis=1).reshape(owners, -1) for m in meta], 1
    ).reshape(owners, -1)
    got_rows, send_meta = lax.optimization_barrier((got_rows, send_meta))
    got_meta = lax.all_to_all(send_meta, ZX, 0, 0, tiled=True)

    rows_own = got_rows.reshape(owners, comp_dev, capacity, col_count).transpose(1, 0, 2, 3)
    rows_own = rows_own.reshape(slots, col_count)
    rows_in = gathered(rows_own)
    slope, z_own = pl.pallas_call(
        activation_kernel,
        in_specs=[SCALARS] + [WHOLE] * 11,
        out_specs=[WHOLE, WHOLE],
        out_shape=[
            jax.ShapeDtypeStruct((slots, col_count), F32),
            jax.ShapeDtypeStruct((slots, col_count), BF),
        ],
        compiler_params=pltpu.CompilerParams(vmem_limit_bytes=24 << 20),
        cost_estimate=pl.CostEstimate(
            flops=2 * slots * model_width * col_count, bytes_accessed=6 << 20, transcendentals=slots * col_count
        ),
    )(pos, *rows_in, projection)
    z_own, got_meta = lax.optimization_barrier((z_own, got_meta))
    got_meta = got_meta.reshape(owners, 4, comp_dev, capacity).transpose(1, 2, 0, 3).reshape(4, slots, 1)
    lse_rows, post_rows, target_rows, grad_rows = (got_meta[i] for i in range(4))
    target_rows = target_rows.astype(jnp.int32)
    z_all = gathered(z_own)

    width = 256
    logit_grads, z_rows = pl.pallas_call(
        logit_kernel,
        grid=(voc_dev // width,),
        in_specs=[SCALARS]
        + [WHOLE] * 13
        + [pl.BlockSpec((model_width, width), lambda i: (0, i))],
        out_specs=[pl.BlockSpec((slots, width), lambda i: (0, i)), WHOLE],
        out_shape=[
            jax.ShapeDtypeStruct((slots, voc_dev), BF),
            jax.ShapeDtypeStruct((model_width, slots), BF),
        ],
        scratch_shapes=[pltpu.VMEM((slots, model_width), BF)],
        compiler_params=pltpu.CompilerParams(vmem_limit_bytes=32 << 20),
        cost_estimate=pl.CostEstimate(
            flops=2 * slots * model_width * voc_dev, bytes_accessed=16 << 20, transcendentals=slots * voc_dev
        ),
    )(pos, *z_all, lse_rows, post_rows, target_rows, embedding)

    z_major = z_rows.reshape(1, 8, 256, slots)
    x_major = z_rows.reshape(8, 4, 64, slots)

    def z_term(k, **arrived):
        return outer_part(z_major, logit_grads, (zi + k + 8) % 8, 0, **arrived)

    def x_term(k, **arrived):
        return outer_part(x_major, logit_grads, (xi + k + 4) % 4, 1, **arrived)

    blocks = embedding.reshape(4, 2, col_count, voc_dev)

    def feature_part(c):
        return jnp.einsum("rv,yev->yre", logit_grads, pick(blocks, c, 1), preferred_element_type=F32)

    feature_grads = vocab_sum(feature_part)
    pre_grads = (feature_grads * slope).astype(BF)
    slot_blocks = projection.reshape(comp_dev, 4, 2, col_count, col_count)

    def slot_part(c):
        return jnp.einsum(
            "kre,kyde->ykrd",
            pre_grads.reshape(comp_dev, slot_rows, col_count),
            pick(slot_blocks, c, 2),
            preferred_element_type=F32,
        ).reshape(4, slots, col_count)

    slot_grads = vocab_sum(slot_part).astype(BF)
    grad_projection = pl.pallas_call(
        projection_kernel,
        in_specs=[SCALARS] + [WHOLE] * 11,
        out_specs=WHOLE,
        out_shape=jax.ShapeDtypeStruct(projection.shape, BF),
        compiler_params=pltpu.CompilerParams(vmem_limit_bytes=24 << 20),
        cost_estimate=pl.CostEstimate(
            flops=2 * slots * model_width * col_count, bytes_accessed=4 << 20, transcendentals=0
        ),
    )(pos, *rows_in, pre_grads)

    prior_own = jnp.sum(
        (rows_own.astype(F32) * grad_rows).reshape(comp_dev, slot_rows, col_count), axis=1
    )
    high = prior_own.astype(BF)
    middle = (prior_own - high.astype(F32)).astype(BF)
    low = (prior_own - high.astype(F32) - middle.astype(F32)).astype(BF)
    pad = jnp.zeros((8 - 3 * comp_dev, col_count), BF)
    prior_pieces = jnp.concatenate([high, middle, low, pad], axis=0)
    slot_grads = slot_grads.reshape(comp_dev, owners, capacity, col_count).transpose(1, 0, 2, 3)
    slot_grads = slot_grads.reshape(owners, comp_dev * capacity, col_count)
    returned = lax.all_to_all(
        jnp.concatenate(
            [slot_grads, jnp.broadcast_to(prior_pieces, (owners, *prior_pieces.shape))], axis=1
        ),
        ZX,
        0,
        0,
        tiled=True,
    )
    per_owner = comp_dev * capacity
    route_grads = lax.dot_general(
        dispatch_tokens,
        returned[:, :per_owner].reshape(slot_count, col_count),
        (((0,), (0,)), ((), ())),
        preferred_element_type=F32,
    )
    pieces = returned[:, per_owner : per_owner + 3 * comp_dev].astype(F32)
    pieces = pieces.reshape(owners, 3, comp_dev, col_count)
    grad_prior = (pieces[:, 0] + (pieces[:, 1] + pieces[:, 2])).reshape(experts_all, col_count).T
    prior_back = lax.dot_general(
        prior_grads, prior_weight.astype(F32), (((1,), (1,)), ((), ())), precision=highest
    )
    grad_hidden = route_grads + prior_back

    words = voc_dev // 2
    z_first = ring_sum(z_term, "z").reshape(4, 64, words)
    x_first = ring_sum(x_term, "x").reshape(8, 64, words)

    def then_x(k, **arrived):
        return plus(pick(z_first, (xi + k + 4) % 4, 0), **arrived)

    def then_z(k, **arrived):
        return plus(pick(x_first, (zi + k + 8) % 8, 0), **arrived)

    grad_embedding = jnp.concatenate([ring_sum(then_x, "x"), ring_sum(then_z, "z")], axis=1).astype(BF)
    return (grad_hidden, grad_prior, grad_projection, grad_embedding)


def solution(mesh):
    finer = Mesh(mesh.devices.reshape(8, 4, 4, 2), ALL)
    in_specs = (
        P(ZX, None),
        P(ZX, None),
        P(ZX),
        P(ZX, None),
        P(ZX, None),
        P(YC, None),
        P(ZX, None, YC),
        P(None, YC),
    )
    out_specs = (P(ZX, YC), P(YC, None), P(ZX, None, YC), P(ZX, YC))
    return jax.shard_map(
        shards, mesh=finer, in_specs=in_specs, out_specs=out_specs, check_vma=False
    )
```

```python
import functools

import jax
import jax.numpy as jnp
from jax import lax
from jax.experimental import pallas as pl
from jax.experimental.pallas import tpu as pltpu
from jax.sharding import Mesh
from jax.sharding import PartitionSpec as P

ZX = ("z", "x")
YC = ("y", "c")
ALL = ("z", "x", "y", "c")
BF = jnp.bfloat16
F32 = jnp.float32
SCALARS = pl.BlockSpec(memory_space=pltpu.SMEM)


def shifted(value, axis, by):
    n = lax.axis_size(axis)
    return lax.ppermute(value, axis, [(i, (i + by) % n) for i in range(n)])


def flipped(value, axis, bit):
    n = lax.axis_size(axis)
    return lax.ppermute(value, axis, [(i, i ^ bit) for i in range(n)])


def ring_sum(term, axis):
    n = lax.axis_size(axis)
    far = term(n // 2)
    half = far.shape[0] // 2
    up = shifted(far[:half], axis, 1)
    down = shifted(far[half:], axis, -1)
    for k in range(n // 2 - 1, 0, -1):
        if k == n // 2 - 1:
            ahead, behind = term(k, first=up), term(-k, second=down)
        else:
            ahead, behind = term(k, whole=(up,)), term(-k, whole=(down,))
        up = shifted(ahead, axis, 1)
        down = shifted(behind, axis, -1)
    return term(0, whole=(up, down), last=True)


def pick(value, index, dim):
    return lax.dynamic_index_in_dim(value, index, dim, keepdims=False)


def gathered(value):
    half = value.shape[0] // 2
    below = shifted(value, "y", 1)
    above = shifted(value, "y", -1)
    far_low = shifted(below[:half], "y", 1)
    far_high = shifted(above[half:], "y", -1)
    near = jnp.stack([value, above, below])
    far = jnp.concatenate([far_low, far_high], axis=0)
    return near, far, flipped(near, "c", 1), flipped(far, "c", 1)


def exchanged(value, axis):
    return lax.all_to_all(value, axis, 0, 0, tiled=True)


def exchanged_sum(value, axis):
    return jnp.sum(exchanged(value.astype(BF), axis).astype(F32), axis=0)


def vocab_sum(part):
    ci = lax.axis_index("c")
    swapped = flipped(part(1 - ci).astype(BF), "c", 1)
    return exchanged_sum(part(ci) + swapped, "y")


def piece_rows(refs, k, rows):
    span = slice(k * rows, (k + 1) * rows)
    for side in range(2):
        near, far = refs[2 * side : 2 * side + 2]
        yield 0, side, near[0, span, :]
        yield 1, side, near[1, span, :]
        yield 3, side, near[2, span, :]
        yield 2, side, far[span, :]


def block_start(pos, dist, side, cols):
    y = lax.rem(pos[0] + dist, 4)
    c = pos[1] if side == 0 else 1 - pos[1]
    return pl.multiple_of((y * 2 + c) * cols, cols)


def posterior_of(prior, meta, me):
    ids = lax.broadcasted_iota(jnp.int32, prior.shape, 1).astype(F32) + 1.0
    route = [meta[:, 2 + j : 3 + j] for j in range(4)]
    lse = [meta[:, 6 + j : 7 + j] + (meta[:, 10 + j : 11 + j] + meta[:, 14 + j : 15 + j]) for j in range(4)]
    tlp = [meta[:, 18 + j : 19 + j] + (meta[:, 22 + j : 23 + j] + meta[:, 26 + j : 27 + j]) for j in range(4)]
    chosen = [jnp.sum(jnp.where(ids == route[j], prior, 0.0), axis=1, keepdims=True) for j in range(4)]

    def softmax(values):
        top = functools.reduce(jnp.maximum, values)
        powers = [jnp.exp(v - top) for v in values]
        total = sum(powers[1:], powers[0])
        return [p / total for p in powers], [v - top - jnp.log(total) for v in values]

    gate, log_gate = softmax(chosen)
    post, _ = softmax([log_gate[j] + tlp[j] for j in range(4)])
    mine = [(route[j] == me).astype(F32) for j in range(4)]

    def own(values):
        return sum([mine[j] * values[j] for j in range(1, 4)], mine[0] * values[0])

    target = meta[:, 0:1] * 128.0 + meta[:, 1:2]
    return own(lse), own(post), target, own([gate[j] - post[j] for j in range(4)])


def activation_kernel(pos, near, far, near_o, far_o, proj, prior, meta, slope, z, info, sums):
    comps, _, cols = proj.shape
    rows = slope.shape[0] // comps
    lane = lax.broadcasted_iota(jnp.int32, (rows, info.shape[1]), 1)
    for k in range(comps):
        span = slice(k * rows, (k + 1) * rows)
        total = jnp.zeros((rows, cols), F32)
        logits = jnp.zeros((rows, prior.shape[1]), F32)
        for dist, side, x in piece_rows((near, far, near_o, far_o), k, rows):
            width = x.shape[1]
            place = pl.ds(block_start(pos, dist, side, width), width)
            total += jnp.dot(x, proj[k, place, :], preferred_element_type=F32)
            logits += jnp.dot(x, prior[place, :], preferred_element_type=F32)
        t = jnp.tanh(total)
        slope[span, :] = 1.0 - t * t
        z[span, :] = t.astype(BF)
        me = (pos[3] * comps + k + 1).astype(F32)
        lse, post, target, grad = posterior_of(logits, meta[span, :].astype(F32), me)
        columns = jnp.where(lane == 0, lse, jnp.where(lane == 1, post, jnp.where(lane == 2, target, grad)))
        info[span, :] = columns
        sums[k : k + 1, :] = jnp.sum(near[0, span, :].astype(F32) * grad, axis=0, keepdims=True)


def projection_kernel(pos, near, far, near_o, far_o, pre, out):
    comps = out.shape[0]
    rows = pre.shape[0] // comps
    for k in range(comps):
        g = pre[k * rows : (k + 1) * rows, :]
        for dist, side, x in piece_rows((near, far, near_o, far_o), k, rows):
            value = lax.dot_general(x, g, (((0,), (0,)), ((), ())), preferred_element_type=F32)
            out[k, pl.ds(block_start(pos, dist, side, x.shape[1]), x.shape[1]), :] = value.astype(BF)


def logit_kernel(pos, near, far, near_o, far_o, info, emb, lg, z_rows, z):
    step = pl.program_id(0)
    rows, cols = far.shape

    @pl.when(step == 0)
    def _():
        for dist, side, x in piece_rows((near, far, near_o, far_o), 0, rows):
            start = block_start(pos, dist, side, cols)
            z[:, pl.ds(start, cols)] = x
            z_rows[pl.ds(start, cols), :] = x.T

    width = emb.shape[1]
    logits = jnp.dot(z[...], emb[...], preferred_element_type=F32)
    first = pos[2] + step * width
    words = first + lax.broadcasted_iota(jnp.int32, logits.shape, 1)
    hit = (info[:, 2:3].astype(jnp.int32) == words).astype(F32)
    lg[...] = (info[:, 1:2] * (jnp.exp(logits - info[:, 0:1]) - hit)).astype(BF)


def outer_kernel(first, second, whole, idx, z, lg, *refs):
    out = refs[-1]
    z = z[...].reshape(-1, z.shape[-1])
    value = jnp.dot(z, lg[...], preferred_element_type=F32)
    half = value.shape[0] // 2
    arrived = refs[:-1]
    if first:
        out[:half] = (value[:half] + arrived[0][...]).astype(out.dtype)
        out[half:] = value[half:].astype(out.dtype)
    elif second:
        out[:half] = value[:half].astype(out.dtype)
        out[half:] = (value[half:] + arrived[0][...]).astype(out.dtype)
    else:
        for other in arrived:
            value = value + other[...]
        out[...] = value.astype(out.dtype)


def outer_part(z_view, lg, index, side, first=None, second=None, whole=(), last=False):
    outer, _, inner, slots = z_view.shape
    words = lg.shape[1] // 2
    rows = outer * inner
    arrived = [a for a in (first, second, *whole) if a is not None]
    return pl.pallas_call(
        functools.partial(outer_kernel, first is not None, second is not None, len(whole)),
        grid_spec=pltpu.PrefetchScalarGridSpec(
            num_scalar_prefetch=1,
            grid=(1,),
            in_specs=[
                pl.BlockSpec((outer, 1, inner, slots), lambda i, n: (0, n[0], 0, 0)),
                pl.BlockSpec((slots, words), lambda i, n: (0, side)),
            ]
            + [pl.BlockSpec(a.shape, lambda i, n: (0, 0)) for a in arrived],
            out_specs=pl.BlockSpec((rows, words), lambda i, n: (0, 0)),
        ),
        out_shape=jax.ShapeDtypeStruct((rows, words), F32 if last else BF),
        compiler_params=pltpu.CompilerParams(vmem_limit_bytes=24 << 20),
        cost_estimate=pl.CostEstimate(
            flops=2 * rows * words * slots, bytes_accessed=6 * rows * words, transcendentals=0
        ),
    )(index.reshape(1).astype(jnp.int32), z_view, lg, *arrived)


def whole(a):
    return pl.BlockSpec(a.shape, lambda *_: (0,) * len(a.shape))


def shaped(shape, dtype):
    return jax.ShapeDtypeStruct(shape, dtype)


def in_three(value):
    high = lax.reduce_precision(value, 8, 7)
    middle = lax.reduce_precision(value - high, 8, 7)
    return high.astype(BF), middle.astype(BF), (value - high - middle).astype(BF)


def shards(hidden, routes, targets, saved_lse, target_logprob, prior_weight, projection, embedding):
    highest = lax.Precision.HIGHEST
    tok_dev, model_width = hidden.shape
    route_count = routes.shape[1]
    comp_dev, _, col_count = projection.shape
    voc_dev = embedding.shape[1]
    owners = lax.axis_size(ZX)
    experts_all = comp_dev * owners
    capacity = max(2, (2 * tok_dev * route_count + experts_all - 1) // experts_all)
    slot_count = owners * comp_dev * capacity
    slot_rows = owners * capacity
    slots = comp_dev * slot_rows
    zi, xi, yi, ci = (lax.axis_index(a) for a in ALL)
    vocab_index = yi * 2 + ci
    pos = jnp.stack([yi, ci, vocab_index * voc_dev, zi * 4 + xi]).astype(jnp.int32)
    own_cols = lax.dynamic_slice_in_dim(hidden, vocab_index * col_count, col_count, 1)

    comp_ids = jnp.arange(experts_all, dtype=jnp.int32)
    pair_comp = routes.reshape(-1)
    pair_onehot = (pair_comp[:, None] == comp_ids[None, :]).astype(BF)
    pair_total = pair_comp.shape[0]
    before = (jnp.arange(pair_total)[:, None] > jnp.arange(pair_total)[None, :]).astype(BF)
    earlier = jnp.dot(before, pair_onehot, preferred_element_type=F32)
    pair_rank = jnp.sum(earlier * pair_onehot.astype(F32), axis=1).astype(jnp.int32)
    pair_slot = (pair_comp * capacity + pair_rank).reshape(tok_dev, route_count)
    slot_ids = jnp.arange(slot_count, dtype=jnp.int32)
    dispatch_tokens = sum(
        (slot_ids[:, None] == pair_slot[:, j][None, :]).astype(F32) for j in range(route_count)
    ).astype(BF)
    numbers = jnp.concatenate(
        [
            (targets[:, None] // 128).astype(BF),
            (targets[:, None] % 128).astype(BF),
            (routes + 1).astype(BF),
            *in_three(saved_lse),
            *in_three(target_logprob),
            jnp.zeros((tok_dev, 128 - 2 - 7 * route_count), BF),
        ],
        axis=1,
    )
    per_owner = comp_dev * capacity
    send_rows = jnp.dot(
        dispatch_tokens, jnp.concatenate([own_cols, numbers], axis=1), preferred_element_type=F32
    ).astype(BF)
    got_rows = exchanged(send_rows.reshape(owners, per_owner, -1), ZX)

    prior_all = exchanged(jnp.broadcast_to(prior_weight, (8, *prior_weight.shape)), YC)
    prior_all = prior_all.reshape(model_width, experts_all)
    prior_logits = jnp.dot(hidden, prior_all, preferred_element_type=F32)
    picked = (routes[:, :, None] == comp_ids[None, None, :]).astype(F32)
    selected = jnp.sum(picked * prior_logits[:, None, :], axis=2)
    gate_weights = jax.nn.softmax(selected, axis=-1)
    posterior = jax.nn.softmax(jax.nn.log_softmax(selected, axis=-1) + target_logprob, axis=-1)
    prior_grads = jnp.sum((gate_weights - posterior)[:, :, None] * picked, axis=1)
    prior_back = lax.dot_general(
        prior_grads, prior_weight.astype(F32), (((1,), (1,)), ((), ())), precision=highest
    )
    got_rows, prior_all, prior_back = lax.optimization_barrier((got_rows, prior_all, prior_back))

    got_rows = got_rows.reshape(owners, comp_dev, capacity, -1).transpose(1, 0, 2, 3)
    got_rows = got_rows.reshape(slots, -1)
    rows_in = gathered(got_rows[:, :col_count])
    numbers_in = got_rows[:, col_count:]
    operands = (*rows_in, projection, prior_all, numbers_in)
    results = [
        shaped((slots, col_count), F32),
        shaped((slots, col_count), BF),
        shaped((slots, 128), F32),
        shaped((8, col_count), F32),
    ]
    slope, z_own, info, prior_own = pl.pallas_call(
        activation_kernel,
        grid=(1,),
        in_specs=[SCALARS] + [whole(a) for a in operands],
        out_specs=[whole(r) for r in results],
        out_shape=results,
        compiler_params=pltpu.CompilerParams(vmem_limit_bytes=32 << 20),
        cost_estimate=pl.CostEstimate(
            flops=2 * slots * model_width * col_count, bytes_accessed=6 << 20, transcendentals=slots * col_count
        ),
    )(pos, *operands)
    z_all = gathered(z_own)

    width = 256
    z_shape = shaped((model_width, slots), BF)
    logit_grads, z_rows = pl.pallas_call(
        logit_kernel,
        grid=(voc_dev // width,),
        in_specs=[SCALARS]
        + [whole(a) for a in (*z_all, info)]
        + [pl.BlockSpec((model_width, width), lambda i: (0, i))],
        out_specs=[pl.BlockSpec((slots, width), lambda i: (0, i)), whole(z_shape)],
        out_shape=[shaped((slots, voc_dev), BF), z_shape],
        scratch_shapes=[pltpu.VMEM((slots, model_width), BF)],
        compiler_params=pltpu.CompilerParams(vmem_limit_bytes=32 << 20),
        cost_estimate=pl.CostEstimate(
            flops=2 * slots * model_width * voc_dev, bytes_accessed=16 << 20, transcendentals=slots * voc_dev
        ),
    )(pos, *z_all, info, embedding)

    words = voc_dev // 2
    z_major = z_rows.reshape(1, 8, 256, slots)
    x_major = z_rows.reshape(8, 4, 64, slots)

    def z_term(k, **arrived):
        return outer_part(z_major, logit_grads, (zi + k + 8) % 8, 0, **arrived)

    x_blocks = pl.pallas_call(
        lambda zr, lg, out: outer_kernel(False, False, 0, None, zr, lg, out.at[0]),
        grid=(4,),
        in_specs=[
            pl.BlockSpec((8, 1, 64, slots), lambda i: (0, i, 0, 0)),
            pl.BlockSpec((slots, words), lambda i: (0, 1)),
        ],
        out_specs=pl.BlockSpec((1, 512, words), lambda i: (i, 0, 0)),
        out_shape=shaped((4, 512, words), BF),
        compiler_params=pltpu.CompilerParams(vmem_limit_bytes=24 << 20),
        cost_estimate=pl.CostEstimate(
            flops=2 * slots * model_width * words, bytes_accessed=7 << 20, transcendentals=0
        ),
    )(x_major, logit_grads)

    blocks = embedding.reshape(4, 2, col_count, voc_dev)

    def feature_part(c):
        return jnp.einsum("rv,yev->yre", logit_grads, pick(blocks, c, 1), preferred_element_type=F32)

    pre_grads = (vocab_sum(feature_part) * slope).astype(BF)
    slot_blocks = projection.reshape(comp_dev, 4, 2, col_count, col_count)

    def slot_part(c):
        return jnp.einsum(
            "kre,kyde->ykrd",
            pre_grads.reshape(comp_dev, slot_rows, col_count),
            pick(slot_blocks, c, 2),
            preferred_element_type=F32,
        ).reshape(4, slots, col_count)

    slot_grads = vocab_sum(slot_part).astype(BF)
    out_shape = shaped(projection.shape, BF)
    grad_projection = pl.pallas_call(
        projection_kernel,
        grid=(1,),
        in_specs=[SCALARS] + [whole(a) for a in (*rows_in, pre_grads)],
        out_specs=whole(out_shape),
        out_shape=out_shape,
        compiler_params=pltpu.CompilerParams(vmem_limit_bytes=24 << 20),
        cost_estimate=pl.CostEstimate(
            flops=2 * slots * model_width * col_count, bytes_accessed=4 << 20, transcendentals=0
        ),
    )(pos, *rows_in, pre_grads)

    pad = jnp.zeros((8 - 3 * comp_dev, col_count), BF)
    prior_pieces = jnp.concatenate([*in_three(prior_own[:comp_dev]), pad], axis=0)
    slot_grads = slot_grads.reshape(comp_dev, owners, capacity, col_count).transpose(1, 0, 2, 3)
    slot_grads = slot_grads.reshape(owners, per_owner, col_count)
    returned = exchanged(
        jnp.concatenate(
            [slot_grads, jnp.broadcast_to(prior_pieces, (owners, *prior_pieces.shape))], axis=1
        ),
        ZX,
    )
    route_grads = lax.dot_general(
        dispatch_tokens,
        returned[:, :per_owner].reshape(slot_count, col_count),
        (((0,), (0,)), ((), ())),
        preferred_element_type=F32,
    )
    pieces = returned[:, per_owner : per_owner + 3 * comp_dev].astype(F32)
    pieces = pieces.reshape(owners, 3, comp_dev, col_count)
    grad_prior = (pieces[:, 0] + (pieces[:, 1] + pieces[:, 2])).reshape(experts_all, col_count).T
    grad_hidden = route_grads + prior_back

    x_first = exchanged_sum(x_blocks, "x").reshape(8, 64, words)
    x_then_z = exchanged_sum(x_first, "z")
    z_first = ring_sum(z_term, "z").reshape(4, 64, words)
    z_then_x = exchanged_sum(z_first, "x")
    grad_embedding = jnp.concatenate([z_then_x, x_then_z], axis=1).astype(BF)
    return (grad_hidden, grad_prior, grad_projection, grad_embedding)


def solution(mesh):
    finer = Mesh(mesh.devices.reshape(8, 4, 4, 2), ALL)
    in_specs = (
        P(ZX, None),
        P(ZX, None),
        P(ZX),
        P(ZX, None),
        P(ZX, None),
        P(YC, None),
        P(ZX, None, YC),
        P(None, YC),
    )
    out_specs = (P(ZX, YC), P(YC, None), P(ZX, None, YC), P(ZX, YC))
    return jax.shard_map(
        shards, mesh=finer, in_specs=in_specs, out_specs=out_specs, check_vma=False
    )
```

```python
import functools

import jax
import jax.numpy as jnp
from jax import lax
from jax.experimental import pallas as pl
from jax.experimental.pallas import tpu as pltpu
from jax.sharding import Mesh
from jax.sharding import PartitionSpec as P

ZX = ("z", "x")
YC = ("y", "c")
ALL = ("z", "x", "y", "c")
BF = jnp.bfloat16
F32 = jnp.float32
LIMIT = 48 << 20
SCALARS = pl.BlockSpec(memory_space=pltpu.SMEM)


def shifted(value, axis, by):
    n = lax.axis_size(axis)
    return lax.ppermute(value, axis, [(i, (i + by) % n) for i in range(n)])


def flipped(value, axis, bit):
    n = lax.axis_size(axis)
    return lax.ppermute(value, axis, [(i, i ^ bit) for i in range(n)])


def ring_sum(term, axis, gate=None, halves=True):
    n = lax.axis_size(axis)
    far = term(n // 2)
    half = far.shape[0] // 2 if halves else far.shape[0]
    up = shifted(far[:half], axis, 1)
    down = shifted(far[half:], axis, -1) if halves else ()
    if gate is not None:
        up, down, _ = lax.optimization_barrier((up, down, gate))
    for k in range(n // 2 - 1, 0, -1):
        if k < n // 2 - 1:
            ahead, behind = term(k, whole=(up,)), term(-k, whole=(down,))
        elif halves:
            ahead, behind = term(k, first=up), term(-k, second=down)
        else:
            ahead, behind = term(k, whole=(up,)), term(-k)
        up = shifted(ahead, axis, 1)
        down = shifted(behind, axis, -1)
    return term(0, whole=(up, down), last=True)


def pick(value, index, dim):
    return lax.dynamic_index_in_dim(value, index, dim, keepdims=False)


def gathered(value):
    half = value.shape[0] // 2
    below = shifted(value, "y", 1)
    above = shifted(value, "y", -1)
    far_low = shifted(below[:half], "y", 1)
    far_high = shifted(above[half:], "y", -1)
    near = jnp.stack([value, above, below])
    far = jnp.concatenate([far_low, far_high], axis=0)
    return near, far, flipped(near, "c", 1), flipped(far, "c", 1)


def exchanged(value, axis):
    return lax.all_to_all(value, axis, 0, 0, tiled=True)


def exchanged_sum(value, axis):
    return jnp.sum(exchanged(value.astype(BF), axis).astype(F32), axis=0)


def piece_rows(refs, k, rows):
    span = slice(k * rows, (k + 1) * rows)
    for side in range(2):
        near, far = refs[2 * side : 2 * side + 2]
        yield 0, side, near[0, span, :]
        yield 1, side, near[1, span, :]
        yield 3, side, near[2, span, :]
        yield 2, side, far[span, :]


def half_rows(refs, k, rows, cols):
    for side in range(2):
        for y in range(refs[side].shape[1] // cols):
            yield y, side, refs[side][k * rows : (k + 1) * rows, y * cols : (y + 1) * cols]


def core_start(pos, y, side, cols):
    c = pos[1] if side == 0 else 1 - pos[1]
    return pl.multiple_of((y * 2 + c) * cols, cols)


def block_start(pos, dist, side, cols):
    y = lax.rem(pos[0] + dist, 4)
    c = pos[1] if side == 0 else 1 - pos[1]
    return pl.multiple_of((y * 2 + c) * cols, cols)


def posterior_of(prior, meta, me):
    ids = lax.broadcasted_iota(jnp.int32, prior.shape, 0).astype(F32) + 1.0
    route = [meta[2 + j : 3 + j] for j in range(4)]
    lse = [meta[6 + j : 7 + j] + (meta[10 + j : 11 + j] + meta[14 + j : 15 + j]) for j in range(4)]
    tlp = [meta[18 + j : 19 + j] + (meta[22 + j : 23 + j] + meta[26 + j : 27 + j]) for j in range(4)]
    chosen = [jnp.sum(jnp.where(ids == route[j], prior, 0.0), axis=0, keepdims=True) for j in range(4)]

    def softmax(values):
        top = functools.reduce(jnp.maximum, values)
        powers = [jnp.exp(v - top) for v in values]
        total = sum(powers[1:], powers[0])
        return [p / total for p in powers], [v - top - jnp.log(total) for v in values]

    gate, log_gate = softmax(chosen)
    post, _ = softmax([log_gate[j] + tlp[j] for j in range(4)])
    mine = [(route[j] == me).astype(F32) for j in range(4)]

    def own(values):
        return sum([mine[j] * values[j] for j in range(1, 4)], mine[0] * values[0])

    target = meta[0:1] * 128.0 + meta[1:2]
    return own(lse), own(post), target, own([gate[j] - post[j] for j in range(4)])


def activation_kernel(pos, mine, other, proj, prior, meta, own, slope, z, info, sums):
    comps, _, cols = proj.shape
    rows = slope.shape[0] // comps
    row = lax.broadcasted_iota(jnp.int32, (info.shape[1], rows), 0)
    for k in range(comps):
        span = slice(k * rows, (k + 1) * rows)
        total = jnp.zeros((rows, cols), F32)
        logits = jnp.zeros((rows, prior.shape[1]), F32)
        for y, side, x in half_rows((mine, other), k, rows, cols):
            place = pl.ds(core_start(pos, y, side, cols), cols)
            total += jnp.dot(x, proj[k, place, :], preferred_element_type=F32)
            logits += jnp.dot(x, prior[place, :], preferred_element_type=F32)
        t = jnp.tanh(total)
        slope[span, :] = 1.0 - t * t
        z[span, :] = t.astype(BF)
        me = (pos[3] * comps + k + 1).astype(F32)
        lse, post, target, grad = posterior_of(logits.T, meta[span, :].astype(F32).T, me)
        columns = jnp.where(row == 0, lse, jnp.where(row == 1, post, jnp.where(row == 2, target, grad))).T
        info[span, :] = columns
        sums[k : k + 1, :] = jnp.sum(own[span, :].astype(F32) * columns[:, 3:4], axis=0, keepdims=True)


def projection_kernel(pos, mine, other, pre, out):
    comps, _, cols = out.shape
    rows = pre.shape[0] // comps
    for k in range(comps):
        g = pre[k * rows : (k + 1) * rows, :]
        for y, side, x in half_rows((mine, other), k, rows, cols):
            value = lax.dot_general(x, g, (((0,), (0,)), ((), ())), preferred_element_type=F32)
            out[k, pl.ds(core_start(pos, y, side, cols), cols), :] = value.astype(BF)


def logit_kernel(pos, near, far, near_o, far_o, info, emb, lg, z_rows, z):
    step = pl.program_id(0)
    rows, cols = far.shape

    @pl.when(step == 0)
    def _():
        for dist, side, x in piece_rows((near, far, near_o, far_o), 0, rows):
            start = block_start(pos, dist, side, cols)
            z[:, pl.ds(start, cols)] = x
            z_rows[pl.ds(start, cols), :] = x.T

    width = emb.shape[1]
    logits = jnp.dot(z[...], emb[...], preferred_element_type=F32)
    first = pos[2] + step * width
    words = first + lax.broadcasted_iota(jnp.int32, logits.shape, 1)
    hit = (info[:, 2:3].astype(jnp.int32) == words).astype(F32)
    lg[...] = (info[:, 1:2] * (jnp.exp(logits - info[:, 0:1]) - hit)).astype(BF)


def feature_kernel(added, core, lg, emb, *refs):
    value = lax.dot_general(lg[...], emb[0], (((1,), (1,)), ((), ())), preferred_element_type=F32)
    if added:
        value = value + refs[0][0]
    refs[-1][0] = value.astype(BF)


def feature_part(lg, emb, core, added=None):
    slots, words = lg.shape
    out = pl.BlockSpec((1, slots, 256), lambda i, n: (i, 0, 0))
    more = [] if added is None else [added]
    return pl.pallas_call(
        functools.partial(feature_kernel, added is not None),
        grid_spec=pltpu.PrefetchScalarGridSpec(
            num_scalar_prefetch=1,
            grid=(4,),
            in_specs=[
                pl.BlockSpec((slots, words), lambda i, n: (0, 0)),
                pl.BlockSpec((1, 256, words), lambda i, n: (2 * i + n[0], 0, 0)),
            ]
            + [out] * len(more),
            out_specs=out,
        ),
        out_shape=jax.ShapeDtypeStruct((4, slots, 256), BF),
        compiler_params=pltpu.CompilerParams(vmem_limit_bytes=LIMIT),
        cost_estimate=pl.CostEstimate(
            flops=2 * slots * words * 1024, bytes_accessed=7 << 20, transcendentals=0
        ),
    )(core.reshape(1).astype(jnp.int32), lg, emb.reshape(8, 256, words), *more)


def slot_kernel(first, core, *refs):
    if first:
        got, slope, proj, pre, out = refs

        @pl.when(pl.program_id(0) == 0)
        def _():
            total = got[0].astype(F32) + got[1].astype(F32)
            total = total + (got[2].astype(F32) + got[3].astype(F32))
            pre[...] = (total * slope[...]).astype(BF)

    else:
        pre, proj, added, out = refs
    comps = proj.shape[0]
    rows = pre.shape[0] // comps
    for k in range(comps):
        span = slice(k * rows, (k + 1) * rows)
        value = lax.dot_general(
            pre[span, :], proj[k, 0], (((1,), (1,)), ((), ())), preferred_element_type=F32
        )
        if not first:
            value = value + added[0, span, :]
        out[0, span, :] = value.astype(BF)


def slot_part(proj, core, got=None, slope=None, pre=None, added=None):
    comps, _, cols = proj.shape
    slots = (slope if pre is None else pre).shape[0]
    out = pl.BlockSpec((1, slots, cols), lambda i, n: (i, 0, 0))
    rows = pl.BlockSpec((slots, cols), lambda i, n: (0, 0))
    weights = pl.BlockSpec((comps, 1, cols, cols), lambda i, n: (0, 2 * i + n[0], 0, 0))
    view = proj.reshape(comps, 8, cols, cols)
    shape, pre_shape = jax.ShapeDtypeStruct((4, slots, cols), BF), jax.ShapeDtypeStruct((slots, cols), BF)
    if pre is None:
        operands = (got, slope, view)
        specs = [pl.BlockSpec((4, slots, cols), lambda i, n: (0, 0, 0)), rows, weights]
        outs, shapes = [rows, out], [pre_shape, shape]
    else:
        operands, specs, outs, shapes = (pre, view, added), [rows, weights, out], out, shape
    return pl.pallas_call(
        functools.partial(slot_kernel, pre is None),
        grid_spec=pltpu.PrefetchScalarGridSpec(
            num_scalar_prefetch=1, grid=(4,), in_specs=specs, out_specs=outs
        ),
        out_shape=shapes,
        compiler_params=pltpu.CompilerParams(vmem_limit_bytes=LIMIT),
        cost_estimate=pl.CostEstimate(
            flops=2 * slots * cols * 1024, bytes_accessed=3 << 20, transcendentals=0
        ),
    )(core.reshape(1).astype(jnp.int32), *operands)


def outer_kernel(first, second, whole, idx, z, lg, *refs):
    out = refs[-1]
    z = z[...].reshape(-1, z.shape[-1])
    value = jnp.dot(z, lg[...], preferred_element_type=F32)
    half = value.shape[0] // 2
    arrived = refs[:-1]
    if first:
        out[:half] = (value[:half] + arrived[0][...]).astype(out.dtype)
        out[half:] = value[half:].astype(out.dtype)
    elif second:
        out[:half] = value[:half].astype(out.dtype)
        out[half:] = (value[half:] + arrived[0][...]).astype(out.dtype)
    else:
        for other in arrived:
            value = value + other[...]
        out[...] = value.astype(out.dtype)


def outer_part(z_view, lg, index, first_col, cols, first=None, second=None, whole=(), last=False):
    outer, _, inner, slots = z_view.shape
    rows = outer * inner
    width = 256
    skip = first_col // width
    arrived = [a for a in (first, second, *whole) if a is not None]
    return pl.pallas_call(
        functools.partial(outer_kernel, first is not None, second is not None, len(whole)),
        grid_spec=pltpu.PrefetchScalarGridSpec(
            num_scalar_prefetch=1,
            grid=(cols // width,),
            in_specs=[
                pl.BlockSpec((outer, 1, inner, slots), lambda i, n: (0, n[0], 0, 0)),
                pl.BlockSpec((slots, width), lambda i, n: (0, skip + i)),
            ]
            + [pl.BlockSpec((a.shape[0], width), lambda i, n: (0, i)) for a in arrived],
            out_specs=pl.BlockSpec((rows, width), lambda i, n: (0, i)),
        ),
        out_shape=jax.ShapeDtypeStruct((rows, cols), F32 if last else BF),
        compiler_params=pltpu.CompilerParams(vmem_limit_bytes=LIMIT),
        cost_estimate=pl.CostEstimate(
            flops=2 * rows * cols * slots, bytes_accessed=6 * rows * cols, transcendentals=0
        ),
    )(index.reshape(1).astype(jnp.int32), z_view, lg, *arrived)


def whole(a):
    return pl.BlockSpec(a.shape, lambda *_: (0,) * len(a.shape))


def shaped(shape, dtype):
    return jax.ShapeDtypeStruct(shape, dtype)


def in_three(value):
    high = lax.reduce_precision(value, 8, 7)
    middle = lax.reduce_precision(value - high, 8, 7)
    return high.astype(BF), middle.astype(BF), (value - high - middle).astype(BF)


def shards(hidden, routes, targets, saved_lse, target_logprob, prior_weight, projection, embedding):
    highest = lax.Precision.HIGHEST
    tok_dev, model_width = hidden.shape
    route_count = routes.shape[1]
    comp_dev, _, col_count = projection.shape
    voc_dev = embedding.shape[1]
    owners = lax.axis_size(ZX)
    experts_all = comp_dev * owners
    capacity = max(2, (2 * tok_dev * route_count + experts_all - 1) // experts_all)
    slot_count = owners * comp_dev * capacity
    slot_rows = owners * capacity
    slots = comp_dev * slot_rows
    zi, xi, yi, ci = (lax.axis_index(a) for a in ALL)
    vocab_index = yi * 2 + ci
    pos = jnp.stack([yi, ci, vocab_index * voc_dev, zi * 4 + xi]).astype(jnp.int32)
    core_cols = pick(hidden.reshape(tok_dev, 4, 2, col_count), ci, 2).reshape(tok_dev, 4 * col_count)

    comp_ids = jnp.arange(experts_all, dtype=jnp.int32)
    pair_comp = routes.reshape(-1)
    pair_onehot = (pair_comp[:, None] == comp_ids[None, :]).astype(BF)
    pair_total = pair_comp.shape[0]
    before = (jnp.arange(pair_total)[:, None] > jnp.arange(pair_total)[None, :]).astype(BF)
    earlier = jnp.dot(before, pair_onehot, preferred_element_type=F32)
    pair_rank = jnp.sum(earlier * pair_onehot.astype(F32), axis=1).astype(jnp.int32)
    pair_slot = (pair_comp * capacity + pair_rank).reshape(tok_dev, route_count)
    slot_ids = jnp.arange(slot_count, dtype=jnp.int32)
    dispatch_tokens = sum(
        (slot_ids[:, None] == pair_slot[:, j][None, :]).astype(F32) for j in range(route_count)
    ).astype(BF)
    numbers = jnp.concatenate(
        [
            (targets[:, None] // 128).astype(BF),
            (targets[:, None] % 128).astype(BF),
            (routes + 1).astype(BF),
            *in_three(saved_lse),
            *in_three(target_logprob),
            jnp.zeros((tok_dev, 128 - 2 - 7 * route_count), BF),
        ],
        axis=1,
    )
    per_owner = comp_dev * capacity
    send_rows = jnp.dot(
        dispatch_tokens, jnp.concatenate([core_cols, numbers], axis=1), preferred_element_type=F32
    ).astype(BF)
    got_rows = exchanged(send_rows.reshape(owners, per_owner, -1), ZX)

    got_rows, prior_weight = lax.optimization_barrier((got_rows, prior_weight))
    prior_all = exchanged(jnp.broadcast_to(prior_weight, (8, *prior_weight.shape)), YC)
    prior_all = prior_all.reshape(model_width, experts_all)
    prior_logits = jnp.dot(hidden, prior_all, preferred_element_type=F32)
    picked = (routes[:, :, None] == comp_ids[None, None, :]).astype(F32)
    selected = jnp.sum(picked * prior_logits[:, None, :], axis=2)
    gate_weights = jax.nn.softmax(selected, axis=-1)
    posterior = jax.nn.softmax(jax.nn.log_softmax(selected, axis=-1) + target_logprob, axis=-1)
    prior_grads = jnp.sum((gate_weights - posterior)[:, :, None] * picked, axis=1)
    prior_back = lax.dot_general(
        prior_grads, prior_weight.astype(F32), (((1,), (1,)), ((), ())), precision=highest
    )

    got_rows = got_rows.reshape(owners, comp_dev, capacity, -1).transpose(1, 0, 2, 3)
    got_rows = got_rows.reshape(slots, -1)
    core_rows = got_rows[:, : 4 * col_count]
    rows_in = (core_rows, flipped(core_rows, "c", 1))
    rows_own = lax.dynamic_slice_in_dim(core_rows, yi * col_count, col_count, 1)
    numbers_in = got_rows[:, 4 * col_count :]
    prior_wide = jnp.pad(prior_all, ((0, 0), (0, 128 - experts_all)))
    operands = (*rows_in, projection, prior_wide, numbers_in, rows_own)
    results = [
        shaped((slots, col_count), F32),
        shaped((slots, col_count), BF),
        shaped((slots, 128), F32),
        shaped((8, col_count), F32),
    ]
    slope, z_own, info, prior_own = pl.pallas_call(
        activation_kernel,
        grid=(1,),
        in_specs=[SCALARS] + [whole(a) for a in operands],
        out_specs=[whole(r) for r in results],
        out_shape=results,
        compiler_params=pltpu.CompilerParams(vmem_limit_bytes=LIMIT),
        cost_estimate=pl.CostEstimate(
            flops=2 * slots * model_width * col_count, bytes_accessed=6 << 20, transcendentals=slots * col_count
        ),
    )(pos, *operands)
    z_all = gathered(z_own)

    width = 256
    z_shape = shaped((model_width, slots), BF)
    logit_grads, z_rows = pl.pallas_call(
        logit_kernel,
        grid=(voc_dev // width,),
        in_specs=[SCALARS]
        + [whole(a) for a in (*z_all, info)]
        + [pl.BlockSpec((model_width, width), lambda i: (0, i))],
        out_specs=[pl.BlockSpec((slots, width), lambda i: (0, i)), whole(z_shape)],
        out_shape=[shaped((slots, voc_dev), BF), z_shape],
        scratch_shapes=[pltpu.VMEM((slots, model_width), BF)],
        compiler_params=pltpu.CompilerParams(vmem_limit_bytes=LIMIT),
        cost_estimate=pl.CostEstimate(
            flops=2 * slots * model_width * voc_dev, bytes_accessed=16 << 20, transcendentals=slots * voc_dev
        ),
    )(pos, *z_all, info, embedding)

    words = 1024
    rest = voc_dev - words
    x_major = z_rows.reshape(8, 4, 64, slots)

    def x_term(k, **arrived):
        return outer_part(x_major, logit_grads, (xi + k + 4) % 4, words, rest, **arrived)

    z_blocks = pl.pallas_call(
        lambda zr, lg, out: outer_kernel(False, False, 0, None, zr, lg, out),
        grid=(4,),
        in_specs=[
            pl.BlockSpec((512, slots), lambda i: (i, 0)),
            pl.BlockSpec((slots, words), lambda i: (0, 0)),
        ],
        out_specs=pl.BlockSpec((512, words), lambda i: (i, 0)),
        out_shape=shaped((model_width, words), BF),
        compiler_params=pltpu.CompilerParams(vmem_limit_bytes=LIMIT),
        cost_estimate=pl.CostEstimate(
            flops=2 * slots * model_width * words, bytes_accessed=7 << 20, transcendentals=0
        ),
    )(z_rows, logit_grads)
    z_first = lax.psum_scatter(z_blocks, "z", scatter_dimension=0, tiled=True)

    feature_theirs = flipped(feature_part(logit_grads, embedding, 1 - ci), "c", 1)
    feature_both = feature_part(logit_grads, embedding, ci, feature_theirs)
    feature_got = exchanged(feature_both, "y")
    pre_grads, slot_theirs = slot_part(projection, 1 - ci, got=feature_got, slope=slope)
    slot_both = slot_part(projection, ci, pre=pre_grads, added=flipped(slot_theirs, "c", 1))
    slot_grads = exchanged_sum(slot_both, "y").astype(BF)
    out_shape = shaped(projection.shape, BF)
    grad_projection = pl.pallas_call(
        projection_kernel,
        grid=(1,),
        in_specs=[SCALARS] + [whole(a) for a in (*rows_in, pre_grads)],
        out_specs=whole(out_shape),
        out_shape=out_shape,
        compiler_params=pltpu.CompilerParams(vmem_limit_bytes=LIMIT),
        cost_estimate=pl.CostEstimate(
            flops=2 * slots * model_width * col_count, bytes_accessed=4 << 20, transcendentals=0
        ),
    )(pos, *rows_in, pre_grads)

    pad = jnp.zeros((8 - 3 * comp_dev, col_count), BF)
    prior_pieces = jnp.concatenate([*in_three(prior_own[:comp_dev]), pad], axis=0)
    slot_grads = slot_grads.reshape(comp_dev, owners, capacity, col_count).transpose(1, 0, 2, 3)
    slot_grads = slot_grads.reshape(owners, per_owner, col_count)
    returned = exchanged(
        jnp.concatenate(
            [slot_grads, jnp.broadcast_to(prior_pieces, (owners, *prior_pieces.shape))], axis=1
        ),
        ZX,
    )
    route_grads = lax.dot_general(
        dispatch_tokens,
        returned[:, :per_owner].reshape(slot_count, col_count),
        (((0,), (0,)), ((), ())),
        preferred_element_type=F32,
    )
    pieces = returned[:, per_owner : per_owner + 3 * comp_dev].astype(F32)
    pieces = pieces.reshape(owners, 3, comp_dev, col_count)
    grad_prior = (pieces[:, 0] + (pieces[:, 1] + pieces[:, 2])).reshape(experts_all, col_count).T
    grad_hidden = route_grads + prior_back

    x_first = ring_sum(x_term, "x", feature_got).reshape(8, 64, rest)

    def then_z(k, whole=(), last=False):
        block = pick(x_first, (zi + k + 8) % 8, 0)
        for other in whole:
            block = block + other
        return block if last else block.astype(BF)

    x_then_z = ring_sum(then_z, "z", halves=False).astype(BF)
    z_then_x = exchanged_sum(z_first.reshape(4, 64, words), "x").astype(BF)
    grad_embedding = jnp.concatenate([z_then_x, x_then_z], axis=1)
    return (grad_hidden, grad_prior, grad_projection, grad_embedding)


def solution(mesh):
    finer = Mesh(mesh.devices.reshape(8, 4, 4, 2), ALL)
    in_specs = (
        P(ZX, None),
        P(ZX, None),
        P(ZX),
        P(ZX, None),
        P(ZX, None),
        P(YC, None),
        P(ZX, None, YC),
        P(None, YC),
    )
    out_specs = (P(ZX, YC), P(YC, None), P(ZX, None, YC), P(ZX, YC))
    return jax.shard_map(
        shards, mesh=finer, in_specs=in_specs, out_specs=out_specs, check_vma=False
    )
```

```python
import functools

import jax
import jax.numpy as jnp
from jax import lax
from jax.experimental import pallas as pl
from jax.experimental.pallas import tpu as pltpu
from jax.sharding import Mesh
from jax.sharding import PartitionSpec as P

ZX = ("z", "x")
YC = ("y", "c")
ALL = ("z", "x", "y", "c")
BF = jnp.bfloat16
F32 = jnp.float32
LIMIT = 48 << 20
SCALARS = pl.BlockSpec(memory_space=pltpu.SMEM)


def shifted(value, axis, by):
    n = lax.axis_size(axis)
    return lax.ppermute(value, axis, [(i, (i + by) % n) for i in range(n)])


def flipped(value, axis, bit):
    n = lax.axis_size(axis)
    return lax.ppermute(value, axis, [(i, i ^ bit) for i in range(n)])


def ring_sum(term, axis):
    n = lax.axis_size(axis)
    up, down = shifted(term(n // 2), axis, 1), None
    for k in range(n // 2 - 1, 0, -1):
        ahead, behind = term(k, whole=(up,)), term(-k, whole=() if down is None else (down,))
        up = shifted(ahead, axis, 1)
        down = shifted(behind, axis, -1)
    return term(0, whole=(up, down), last=True)


def pick(value, index, dim):
    return lax.dynamic_index_in_dim(value, index, dim, keepdims=False)


def gathered(value):
    half = value.shape[0] // 2
    below = shifted(value, "y", 1)
    above = shifted(value, "y", -1)
    far_low = shifted(below[:half], "y", 1)
    far_high = shifted(above[half:], "y", -1)
    near = jnp.stack([value, above, below])
    far = jnp.concatenate([far_low, far_high], axis=0)
    return near, far, flipped(near, "c", 1), flipped(far, "c", 1)


def exchanged(value, axis):
    return lax.all_to_all(value, axis, 0, 0, tiled=True)


def exchanged_sum(value, axis):
    return jnp.sum(exchanged(value.astype(BF), axis).astype(F32), axis=0)


def piece_rows(refs, k, rows):
    span = slice(k * rows, (k + 1) * rows)
    for side in range(2):
        near, far = refs[2 * side : 2 * side + 2]
        yield 0, side, near[0, span, :]
        yield 1, side, near[1, span, :]
        yield 3, side, near[2, span, :]
        yield 2, side, far[span, :]


def half_rows(refs, k, rows, cols):
    for side in range(2):
        for y in range(4):
            yield y, side, refs[side][k * rows : (k + 1) * rows, y * cols : (y + 1) * cols]


def core_start(pos, y, side, cols):
    c = pos[1] if side == 0 else 1 - pos[1]
    return pl.multiple_of((y * 2 + c) * cols, cols)


def block_start(pos, dist, side, cols):
    y = lax.rem(pos[0] + dist, 4)
    c = pos[1] if side == 0 else 1 - pos[1]
    return pl.multiple_of((y * 2 + c) * cols, cols)


def prep_kernel(pos, hidden, routes, targets, lse, tlp, send, table):
    tokens = hidden.shape[0]
    slots = table.shape[0]
    cap = slots // tokens
    ids = lax.broadcasted_iota(jnp.int32, (tokens, tokens), 1)
    chosen = [ids == routes[:, j : j + 1] for j in range(4)]
    mask = sum([c.astype(F32) for c in chosen[1:]], chosen[0].astype(F32))
    rows = lax.broadcasted_iota(jnp.int32, (tokens, tokens), 0)
    earlier = (rows > ids).astype(BF)
    rank = jnp.dot(earlier, mask.astype(BF), preferred_element_type=F32)
    place = (mask * (rank + 1.0)).astype(BF)
    slot = lax.broadcasted_iota(jnp.int32, (slots, tokens), 0)
    comp = lax.broadcasted_iota(jnp.int32, (slots, tokens), 1)
    spread = (lax.div(slot, cap) == comp).astype(BF)
    number = lax.dot_general(spread, place, (((1,), (1,)), ((), ())), preferred_element_type=F32)
    hits = (number == (lax.rem(slot, cap) + 1).astype(F32)).astype(BF)
    table[...] = hits
    lane = lax.broadcasted_iota(jnp.int32, (tokens, 128), 1)
    numbers = jnp.zeros((tokens, 128), F32)

    def put(numbers, at, column):
        return jnp.where(lane == at, column, numbers)

    t = targets[...]
    numbers = put(numbers, 0, lax.div(t, 128).astype(F32))
    numbers = put(numbers, 1, lax.rem(t, 128).astype(F32))
    for j in range(4):
        numbers = put(numbers, 2 + j, (routes[:, j : j + 1] + 1).astype(F32))
        for base, ref in ((6, lse), (18, tlp)):
            value = ref[:, j : j + 1]
            high = value.astype(BF).astype(F32)
            middle = (value - high).astype(BF).astype(F32)
            numbers = put(numbers, base + j, high)
            numbers = put(numbers, base + 4 + j, middle)
            numbers = put(numbers, base + 8 + j, value - high - middle)
    for y in range(4):
        columns = hidden[:, pl.ds(core_start(pos, y, 0, 256), 256)]
        rows_out = jnp.dot(hits, columns, preferred_element_type=F32)
        send[:, y * 256 : (y + 1) * 256] = rows_out.astype(BF)
    send[:, 1024:] = jnp.dot(hits, numbers.astype(BF), preferred_element_type=F32).astype(BF)


def posterior_of(prior, meta, me):
    ids = lax.broadcasted_iota(jnp.int32, prior.shape, 0).astype(F32) + 1.0
    route = [meta[2 + j : 3 + j] for j in range(4)]
    lse = [meta[6 + j : 7 + j] + (meta[10 + j : 11 + j] + meta[14 + j : 15 + j]) for j in range(4)]
    tlp = [meta[18 + j : 19 + j] + (meta[22 + j : 23 + j] + meta[26 + j : 27 + j]) for j in range(4)]
    chosen = [jnp.sum(jnp.where(ids == route[j], prior, 0.0), axis=0, keepdims=True) for j in range(4)]

    def softmax(values):
        top = functools.reduce(jnp.maximum, values)
        powers = [jnp.exp(v - top) for v in values]
        total = sum(powers[1:], powers[0])
        return [p / total for p in powers], [v - top - jnp.log(total) for v in values]

    gate, log_gate = softmax(chosen)
    post, _ = softmax([log_gate[j] + tlp[j] for j in range(4)])
    mine = [(route[j] == me).astype(F32) for j in range(4)]

    def own(values):
        return sum([mine[j] * values[j] for j in range(1, 4)], mine[0] * values[0])

    target = meta[0:1] * 128.0 + meta[1:2]
    return own(lse), own(post), target, own([gate[j] - post[j] for j in range(4)])


def activation_kernel(pos, mine, other, proj, prior, slope, z, info, sums):
    comps, _, cols = proj.shape
    rows = slope.shape[0] // comps
    row = lax.broadcasted_iota(jnp.int32, (info.shape[1], rows), 0)
    for k in range(comps):
        span = slice(k * rows, (k + 1) * rows)
        total = jnp.zeros((rows, cols), F32)
        logits = jnp.zeros((rows, prior.shape[1]), F32)
        for y, side, x in half_rows((mine, other), k, rows, cols):
            place = pl.ds(core_start(pos, y, side, cols), cols)
            total += jnp.dot(x, proj[k, place, :], preferred_element_type=F32)
            logits += jnp.dot(x, prior[place, :], preferred_element_type=F32)
        t = jnp.tanh(total)
        slope[span, :] = 1.0 - t * t
        z[span, :] = t.astype(BF)
        me = (pos[3] * comps + k + 1).astype(F32)
        lse, post, target, grad = posterior_of(logits.T, mine[span, 4 * cols :].astype(F32).T, me)
        columns = jnp.where(row == 0, lse, jnp.where(row == 1, post, jnp.where(row == 2, target, grad))).T
        info[span, :] = columns
        sums[k : k + 1, :] = jnp.sum(mine[span, pl.ds(pl.multiple_of(pos[0] * cols, cols), cols)].astype(F32) * columns[:, 3:4], axis=0, keepdims=True)


def projection_kernel(pos, mine, other, pre, out):
    comps, _, cols = out.shape
    rows = pre.shape[0] // comps
    for k in range(comps):
        g = pre[k * rows : (k + 1) * rows, :]
        for y, side, x in half_rows((mine, other), k, rows, cols):
            value = lax.dot_general(x, g, (((0,), (0,)), ((), ())), preferred_element_type=F32)
            out[k, pl.ds(core_start(pos, y, side, cols), cols), :] = value.astype(BF)


def logit_kernel(pos, near, far, near_o, far_o, info, emb, lg, z_rows, z):
    step = pl.program_id(0)
    rows, cols = far.shape

    @pl.when(step == 0)
    def _():
        for dist, side, x in piece_rows((near, far, near_o, far_o), 0, rows):
            start = block_start(pos, dist, side, cols)
            z[:, pl.ds(start, cols)] = x
            z_rows[pl.ds(start, cols), :] = x.T

    width = emb.shape[1]
    logits = jnp.dot(z[...], emb[...], preferred_element_type=F32)
    first = pos[2] + step * width
    words = first + lax.broadcasted_iota(jnp.int32, logits.shape, 1)
    hit = (info[:, 2:3].astype(jnp.int32) == words).astype(F32)
    lg[...] = (info[:, 1:2] * (jnp.exp(logits - info[:, 0:1]) - hit)).astype(BF)


def feature_kernel(added, core, lg, emb, *refs):
    value = lax.dot_general(lg[...], emb[0], (((1,), (1,)), ((), ())), preferred_element_type=F32)
    if added:
        value = value + refs[0][0]
    refs[-1][0] = value.astype(BF)


def feature_part(lg, emb, core, added=None):
    slots, words = lg.shape
    out = pl.BlockSpec((1, slots, 256), lambda i, n: (i, 0, 0))
    more = [] if added is None else [added]
    return pl.pallas_call(
        functools.partial(feature_kernel, added is not None),
        grid_spec=pltpu.PrefetchScalarGridSpec(
            num_scalar_prefetch=1,
            grid=(4,),
            in_specs=[
                pl.BlockSpec((slots, words), lambda i, n: (0, 0)),
                pl.BlockSpec((1, 256, words), lambda i, n: (2 * i + n[0], 0, 0)),
            ]
            + [out] * len(more),
            out_specs=out,
        ),
        out_shape=jax.ShapeDtypeStruct((4, slots, 256), BF),
        compiler_params=pltpu.CompilerParams(vmem_limit_bytes=LIMIT),
        cost_estimate=pl.CostEstimate(
            flops=2 * slots * words * 1024, bytes_accessed=7 << 20, transcendentals=0
        ),
    )(core.reshape(1).astype(jnp.int32), lg, emb.reshape(8, 256, words), *more)


def slot_kernel(first, core, *refs):
    if first:
        got, slope, proj, pre, out = refs

        @pl.when(pl.program_id(0) == 0)
        def _():
            total = got[0].astype(F32) + got[1].astype(F32)
            total = total + (got[2].astype(F32) + got[3].astype(F32))
            pre[...] = (total * slope[...]).astype(BF)

    else:
        pre, proj, added, out = refs
    comps = proj.shape[0]
    rows = pre.shape[0] // comps
    for k in range(comps):
        span = slice(k * rows, (k + 1) * rows)
        value = lax.dot_general(
            pre[span, :], proj[k, 0], (((1,), (1,)), ((), ())), preferred_element_type=F32
        )
        if not first:
            value = value + added[0, span, :]
        out[0, span, :] = value.astype(BF)


def slot_part(proj, core, got=None, slope=None, pre=None, added=None):
    comps, _, cols = proj.shape
    slots = (slope if pre is None else pre).shape[0]
    out = pl.BlockSpec((1, slots, cols), lambda i, n: (i, 0, 0))
    rows = pl.BlockSpec((slots, cols), lambda i, n: (0, 0))
    weights = pl.BlockSpec((comps, 1, cols, cols), lambda i, n: (0, 2 * i + n[0], 0, 0))
    view = proj.reshape(comps, 8, cols, cols)
    shape, pre_shape = jax.ShapeDtypeStruct((4, slots, cols), BF), jax.ShapeDtypeStruct((slots, cols), BF)
    if pre is None:
        operands = (got, slope, view)
        specs = [pl.BlockSpec((4, slots, cols), lambda i, n: (0, 0, 0)), rows, weights]
        outs, shapes = [rows, out], [pre_shape, shape]
    else:
        operands, specs, outs, shapes = (pre, view, added), [rows, weights, out], out, shape
    return pl.pallas_call(
        functools.partial(slot_kernel, pre is None),
        grid_spec=pltpu.PrefetchScalarGridSpec(
            num_scalar_prefetch=1, grid=(4,), in_specs=specs, out_specs=outs
        ),
        out_shape=shapes,
        compiler_params=pltpu.CompilerParams(vmem_limit_bytes=LIMIT),
        cost_estimate=pl.CostEstimate(
            flops=2 * slots * cols * 1024, bytes_accessed=3 << 20, transcendentals=0
        ),
    )(core.reshape(1).astype(jnp.int32), *operands)


def outer_kernel(first, second, whole, idx, z, lg, *refs):
    out = refs[-1]
    z = z[...].reshape(-1, z.shape[-1])
    value = jnp.dot(z, lg[...], preferred_element_type=F32)
    half = value.shape[0] // 2
    arrived = refs[:-1]
    if first:
        out[:half] = (value[:half] + arrived[0][...]).astype(out.dtype)
        out[half:] = value[half:].astype(out.dtype)
    elif second:
        out[:half] = value[:half].astype(out.dtype)
        out[half:] = (value[half:] + arrived[0][...]).astype(out.dtype)
    else:
        for other in arrived:
            value = value + other[...]
        out[...] = value.astype(out.dtype)


def outer_part(z_view, lg, index, first_col, cols, first=None, second=None, whole=(), last=False):
    outer, _, inner, slots = z_view.shape
    rows = outer * inner
    width = 256
    skip = first_col // width
    arrived = [a for a in (first, second, *whole) if a is not None]
    return pl.pallas_call(
        functools.partial(outer_kernel, first is not None, second is not None, len(whole)),
        grid_spec=pltpu.PrefetchScalarGridSpec(
            num_scalar_prefetch=1,
            grid=(cols // width,),
            in_specs=[
                pl.BlockSpec((outer, 1, inner, slots), lambda i, n: (0, n[0], 0, 0)),
                pl.BlockSpec((slots, width), lambda i, n: (0, skip + i)),
            ]
            + [pl.BlockSpec((a.shape[0], width), lambda i, n: (0, i)) for a in arrived],
            out_specs=pl.BlockSpec((rows, width), lambda i, n: (0, i)),
        ),
        out_shape=jax.ShapeDtypeStruct((rows, cols), F32 if last else BF),
        compiler_params=pltpu.CompilerParams(vmem_limit_bytes=LIMIT),
        cost_estimate=pl.CostEstimate(
            flops=2 * rows * cols * slots, bytes_accessed=6 * rows * cols, transcendentals=0
        ),
    )(index.reshape(1).astype(jnp.int32), z_view, lg, *arrived)


def whole(a):
    return pl.BlockSpec(a.shape, lambda *_: (0,) * len(a.shape))


def shaped(shape, dtype):
    return jax.ShapeDtypeStruct(shape, dtype)


def in_three(value):
    high = lax.reduce_precision(value, 8, 7)
    middle = lax.reduce_precision(value - high, 8, 7)
    return high.astype(BF), middle.astype(BF), (value - high - middle).astype(BF)


def shards(hidden, routes, targets, saved_lse, target_logprob, prior_weight, projection, embedding):
    highest = lax.Precision.HIGHEST
    tok_dev, model_width = hidden.shape
    route_count = routes.shape[1]
    comp_dev, _, col_count = projection.shape
    voc_dev = embedding.shape[1]
    owners = lax.axis_size(ZX)
    experts_all = comp_dev * owners
    capacity = max(2, (2 * tok_dev * route_count + experts_all - 1) // experts_all)
    slot_count = owners * comp_dev * capacity
    slot_rows = owners * capacity
    slots = comp_dev * slot_rows
    zi, xi, yi, ci = (lax.axis_index(a) for a in ALL)
    vocab_index = yi * 2 + ci
    pos = jnp.stack([yi, ci, vocab_index * voc_dev, zi * 4 + xi]).astype(jnp.int32)
    comp_ids = jnp.arange(experts_all, dtype=jnp.int32)
    per_owner = comp_dev * capacity
    sent_width = 4 * col_count + 128
    operands = (hidden, routes, targets[:, None], saved_lse, target_logprob)
    results = [shaped((slot_count, sent_width), BF), shaped((slot_count, tok_dev), BF)]
    send_rows, dispatch_tokens = pl.pallas_call(
        prep_kernel,
        grid=(1,),
        in_specs=[SCALARS] + [whole(a) for a in operands],
        out_specs=[whole(r) for r in results],
        out_shape=results,
        compiler_params=pltpu.CompilerParams(vmem_limit_bytes=LIMIT),
        cost_estimate=pl.CostEstimate(
            flops=2 * slot_count * tok_dev * sent_width, bytes_accessed=2 << 20, transcendentals=0
        ),
    )(pos, *operands)
    got_rows = exchanged(send_rows.reshape(owners, per_owner, sent_width), ZX)

    pair = jnp.stack([prior_weight, flipped(prior_weight, "c", 1)])
    pair = jnp.where(ci == 0, pair, pair[::-1])
    two = jnp.stack([pair, flipped(pair, "y", 1)])
    two = jnp.where(yi % 2 == 0, two, two[::-1])
    four = jnp.stack([two, flipped(two, "y", 2)])
    four = jnp.where(yi < 2, four, four[::-1])
    prior_all = four.reshape(model_width, experts_all)
    prior_wide = jnp.pad(prior_all, ((0, 0), (0, 128 - experts_all)))
    prior_logits = jnp.dot(hidden, prior_all, preferred_element_type=F32)
    picked = (routes[:, :, None] == comp_ids[None, None, :]).astype(F32)
    selected = jnp.sum(picked * prior_logits[:, None, :], axis=2)
    gate_weights = jax.nn.softmax(selected, axis=-1)
    posterior = jax.nn.softmax(jax.nn.log_softmax(selected, axis=-1) + target_logprob, axis=-1)
    prior_grads = jnp.sum((gate_weights - posterior)[:, :, None] * picked, axis=1)
    prior_back = lax.dot_general(
        prior_grads, prior_weight.astype(F32), (((1,), (1,)), ((), ())), precision=highest
    )
    got_rows, prior_wide, prior_back = lax.optimization_barrier((got_rows, prior_wide, prior_back))

    got_rows = got_rows.reshape(owners, comp_dev, capacity, -1).transpose(1, 0, 2, 3)
    got_rows = got_rows.reshape(slots, -1)
    rows_in = (got_rows, flipped(got_rows, "c", 1))
    operands = (*rows_in, projection, prior_wide)
    results = [
        shaped((slots, col_count), F32),
        shaped((slots, col_count), BF),
        shaped((slots, 128), F32),
        shaped((8, col_count), F32),
    ]
    slope, z_own, info, prior_own = pl.pallas_call(
        activation_kernel,
        grid=(1,),
        in_specs=[SCALARS] + [whole(a) for a in operands],
        out_specs=[whole(r) for r in results],
        out_shape=results,
        compiler_params=pltpu.CompilerParams(vmem_limit_bytes=LIMIT),
        cost_estimate=pl.CostEstimate(
            flops=2 * slots * model_width * col_count, bytes_accessed=6 << 20, transcendentals=slots * col_count
        ),
    )(pos, *operands)
    z_all = gathered(z_own)

    width = 512
    z_shape = shaped((model_width, slots), BF)
    logit_grads, z_rows = pl.pallas_call(
        logit_kernel,
        grid=(voc_dev // width,),
        in_specs=[SCALARS]
        + [whole(a) for a in (*z_all, info)]
        + [pl.BlockSpec((model_width, width), lambda i: (0, i))],
        out_specs=[pl.BlockSpec((slots, width), lambda i: (0, i)), whole(z_shape)],
        out_shape=[shaped((slots, voc_dev), BF), z_shape],
        scratch_shapes=[pltpu.VMEM((slots, model_width), BF)],
        compiler_params=pltpu.CompilerParams(vmem_limit_bytes=LIMIT),
        cost_estimate=pl.CostEstimate(
            flops=2 * slots * model_width * voc_dev, bytes_accessed=16 << 20, transcendentals=slots * voc_dev
        ),
    )(pos, *z_all, info, embedding)

    words = 1280
    rest = voc_dev - words
    x_major = z_rows.reshape(8, 4, 64, slots)

    def x_term(k, **arrived):
        return outer_part(x_major, logit_grads, (xi + k + 4) % 4, words, rest, **arrived)

    z_blocks = pl.pallas_call(
        lambda zr, lg, out: outer_kernel(False, False, 0, None, zr, lg, out),
        grid=(4,),
        in_specs=[
            pl.BlockSpec((512, slots), lambda i: (i, 0)),
            pl.BlockSpec((slots, words), lambda i: (0, 0)),
        ],
        out_specs=pl.BlockSpec((512, words), lambda i: (i, 0)),
        out_shape=shaped((model_width, words), BF),
        compiler_params=pltpu.CompilerParams(vmem_limit_bytes=LIMIT),
        cost_estimate=pl.CostEstimate(
            flops=2 * slots * model_width * words, bytes_accessed=7 << 20, transcendentals=0
        ),
    )(z_rows, logit_grads)
    z_first = lax.psum_scatter(z_blocks, "z", scatter_dimension=0, tiled=True)

    x_far = x_term(2)
    half = x_far.shape[0] // 2
    up, down = shifted(x_far[:half], "x", 1), shifted(x_far[half:], "x", -1)
    tied, x_far = lax.optimization_barrier((logit_grads, x_far))
    feature_theirs = flipped(feature_part(tied, embedding, 1 - ci), "c", 1)
    feature_both = feature_part(tied, embedding, ci, feature_theirs)
    feature_both, up, down = lax.optimization_barrier((feature_both, up, down))
    feature_got = exchanged(feature_both, "y")
    pre_grads, slot_theirs = slot_part(projection, 1 - ci, got=feature_got, slope=slope)
    slot_theirs, up, down = lax.optimization_barrier((slot_theirs, up, down))
    ahead, behind = x_term(1, first=up), x_term(-1, second=down)
    up, down = shifted(ahead, "x", 1), shifted(behind, "x", -1)
    slot_both = slot_part(projection, ci, pre=pre_grads, added=flipped(slot_theirs, "c", 1))
    slot_got = exchanged(slot_both, "y")
    slot_got, up, down = lax.optimization_barrier((slot_got, up, down))
    x_first = x_term(0, whole=(up, down), last=True).reshape(8, 64, rest)
    slot_grads = jnp.sum(slot_got.astype(F32), axis=0).astype(BF)
    out_shape = shaped(projection.shape, BF)
    grad_projection = pl.pallas_call(
        projection_kernel,
        grid=(1,),
        in_specs=[SCALARS] + [whole(a) for a in (*rows_in, pre_grads)],
        out_specs=whole(out_shape),
        out_shape=out_shape,
        compiler_params=pltpu.CompilerParams(vmem_limit_bytes=LIMIT),
        cost_estimate=pl.CostEstimate(
            flops=2 * slots * model_width * col_count, bytes_accessed=4 << 20, transcendentals=0
        ),
    )(pos, *rows_in, pre_grads)

    pad = jnp.zeros((8 - 3 * comp_dev, col_count), BF)
    prior_pieces = jnp.concatenate([*in_three(prior_own[:comp_dev]), pad], axis=0)
    slot_grads = slot_grads.reshape(comp_dev, owners, capacity, col_count).transpose(1, 0, 2, 3)
    slot_grads = slot_grads.reshape(owners, per_owner, col_count)
    returned = exchanged(
        jnp.concatenate(
            [slot_grads, jnp.broadcast_to(prior_pieces, (owners, *prior_pieces.shape))], axis=1
        ),
        ZX,
    )
    route_grads = lax.dot_general(
        dispatch_tokens,
        returned[:, :per_owner].reshape(slot_count, col_count),
        (((0,), (0,)), ((), ())),
        preferred_element_type=F32,
    )
    pieces = returned[:, per_owner : per_owner + 3 * comp_dev].astype(F32)
    pieces = pieces.reshape(owners, 3, comp_dev, col_count)
    grad_prior = (pieces[:, 0] + (pieces[:, 1] + pieces[:, 2])).reshape(experts_all, col_count).T
    grad_hidden = route_grads + prior_back

    def then_z(k, whole=(), last=False):
        block = pick(x_first, (zi + k + 8) % 8, 0)
        for other in whole:
            block = block + other
        return block if last else block.astype(BF)

    x_then_z = ring_sum(then_z, "z").astype(BF)
    z_then_x = exchanged_sum(z_first.reshape(4, 64, words), "x").astype(BF)
    grad_embedding = jnp.concatenate([z_then_x, x_then_z], axis=1)
    return (grad_hidden, grad_prior, grad_projection, grad_embedding)


def solution(mesh):
    finer = Mesh(mesh.devices.reshape(8, 4, 4, 2), ALL)
    in_specs = (
        P(ZX, None),
        P(ZX, None),
        P(ZX),
        P(ZX, None),
        P(ZX, None),
        P(YC, None),
        P(ZX, None, YC),
        P(None, YC),
    )
    out_specs = (P(ZX, YC), P(YC, None), P(ZX, None, YC), P(ZX, YC))
    return jax.shard_map(
        shards, mesh=finer, in_specs=in_specs, out_specs=out_specs, check_vma=False
    )
```

```python
import functools

import jax
import jax.numpy as jnp
from jax import lax
from jax.experimental import pallas as pl
from jax.experimental.pallas import tpu as pltpu
from jax.sharding import Mesh
from jax.sharding import PartitionSpec as P

ZX = ("z", "x")
YC = ("y", "c")
ALL = ("z", "x", "y", "c")
BF = jnp.bfloat16
F32 = jnp.float32
LIMIT = 48 << 20
SCALARS = pl.BlockSpec(memory_space=pltpu.SMEM)


def shifted(value, axis, by):
    n = lax.axis_size(axis)
    return lax.ppermute(value, axis, [(i, (i + by) % n) for i in range(n)])


def flipped(value, axis, bit):
    n = lax.axis_size(axis)
    return lax.ppermute(value, axis, [(i, i ^ bit) for i in range(n)])


def pick(value, index, dim):
    return lax.dynamic_index_in_dim(value, index, dim, keepdims=False)


def gathered(value):
    half = value.shape[0] // 2
    below = shifted(value, "y", 1)
    above = shifted(value, "y", -1)
    far_low = shifted(below[:half], "y", 1)
    far_high = shifted(above[half:], "y", -1)
    near = jnp.stack([value, above, below])
    far = jnp.concatenate([far_low, far_high], axis=0)
    return near, far, flipped(near, "c", 1), flipped(far, "c", 1)


def exchanged(value, axis):
    return lax.all_to_all(value, axis, 0, 0, tiled=True)


def piece_rows(refs, k, rows):
    span = slice(k * rows, (k + 1) * rows)
    for side in range(2):
        near, far = refs[2 * side : 2 * side + 2]
        yield 0, side, near[0, span, :]
        yield 1, side, near[1, span, :]
        yield 3, side, near[2, span, :]
        yield 2, side, far[span, :]


def half_rows(refs, k, rows, cols):
    for side in range(2):
        for y in range(4):
            yield y, side, refs[side][k * rows : (k + 1) * rows, y * cols : (y + 1) * cols]


def core_start(pos, y, side, cols):
    c = pos[1] if side == 0 else 1 - pos[1]
    return pl.multiple_of((y * 2 + c) * cols, cols)


def block_start(pos, dist, side, cols):
    y = lax.rem(pos[0] + dist, 4)
    c = pos[1] if side == 0 else 1 - pos[1]
    return pl.multiple_of((y * 2 + c) * cols, cols)


def prep_kernel(pos, hidden, routes, targets, lse, tlp, send, table):
    tokens = hidden.shape[0]
    slots = table.shape[0]
    cap = slots // tokens
    ids = lax.broadcasted_iota(jnp.int32, (tokens, tokens), 0)
    token = lax.broadcasted_iota(jnp.int32, (tokens, tokens), 1)
    chosen = [(ids == routes[j : j + 1, :]).astype(F32) for j in range(4)]
    mask = chosen[0] + chosen[1] + (chosen[2] + chosen[3])
    rank = jnp.dot(mask.astype(BF), (ids < token).astype(BF), preferred_element_type=F32)
    place = (mask * (rank + 1.0)).astype(BF)
    slot = lax.broadcasted_iota(jnp.int32, (slots, tokens), 0)
    comp = lax.broadcasted_iota(jnp.int32, (slots, tokens), 1)
    spread = (lax.div(slot, cap) == comp).astype(BF)
    number = jnp.dot(spread, place, preferred_element_type=F32)
    hits = (number == (lax.rem(slot, cap) + 1).astype(F32)).astype(BF)
    table[...] = hits
    at = lax.broadcasted_iota(jnp.int32, (128, tokens), 0)
    t = targets[...]
    numbers = jnp.where(at == 0, lax.div(t, 128).astype(F32), jnp.where(at == 1, lax.rem(t, 128).astype(F32), 0.0))
    for j in range(4):
        numbers = jnp.where(at == 2 + j, (routes[j : j + 1, :] + 1).astype(F32), numbers)
        for base, ref in ((6, lse), (18, tlp)):
            value = ref[j : j + 1, :]
            high = value.astype(BF).astype(F32)
            middle = (value - high).astype(BF).astype(F32)
            numbers = jnp.where(at == base + j, high, numbers)
            numbers = jnp.where(at == base + 4 + j, middle, numbers)
            numbers = jnp.where(at == base + 8 + j, value - high - middle, numbers)
    for y in range(4):
        columns = hidden[:, pl.ds(core_start(pos, y, 0, 256), 256)]
        rows_out = jnp.dot(hits, columns, preferred_element_type=F32)
        send[:, y * 256 : (y + 1) * 256] = rows_out.astype(BF)
    picked = lax.dot_general(
        hits, numbers.astype(BF), (((1,), (1,)), ((), ())), preferred_element_type=F32
    )
    send[:, 1024:] = picked.astype(BF)


def posterior_of(prior, meta, me):
    ids = lax.broadcasted_iota(jnp.int32, prior.shape, 0).astype(F32) + 1.0
    route = [meta[2 + j : 3 + j] for j in range(4)]
    lse = [meta[6 + j : 7 + j] + (meta[10 + j : 11 + j] + meta[14 + j : 15 + j]) for j in range(4)]
    tlp = [meta[18 + j : 19 + j] + (meta[22 + j : 23 + j] + meta[26 + j : 27 + j]) for j in range(4)]
    chosen = [jnp.sum(jnp.where(ids == route[j], prior, 0.0), axis=0, keepdims=True) for j in range(4)]

    def softmax(values):
        top = functools.reduce(jnp.maximum, values)
        powers = [jnp.exp(v - top) for v in values]
        total = sum(powers[1:], powers[0])
        return [p / total for p in powers], [v - top - jnp.log(total) for v in values]

    gate, log_gate = softmax(chosen)
    post, _ = softmax([log_gate[j] + tlp[j] for j in range(4)])
    mine = [(route[j] == me).astype(F32) for j in range(4)]

    def own(values):
        return sum([mine[j] * values[j] for j in range(1, 4)], mine[0] * values[0])

    target = meta[0:1] * 128.0 + meta[1:2]
    return own(lse), own(post), target, own([gate[j] - post[j] for j in range(4)])


def activation_kernel(pos, mine, other, proj, prior, slope, z, info, sums):
    comps, _, cols = proj.shape
    rows = slope.shape[0] // comps
    row = lax.broadcasted_iota(jnp.int32, (info.shape[1], rows), 0)
    for k in range(comps):
        span = slice(k * rows, (k + 1) * rows)
        total = jnp.zeros((rows, cols), F32)
        logits = jnp.zeros((rows, prior.shape[1]), F32)
        for y, side, x in half_rows((mine, other), k, rows, cols):
            place = pl.ds(core_start(pos, y, side, cols), cols)
            total += jnp.dot(x, proj[k, place, :], preferred_element_type=F32)
            logits += jnp.dot(x, prior[place, :], preferred_element_type=F32)
        t = jnp.tanh(total)
        slope[span, :] = 1.0 - t * t
        z[span, :] = t.astype(BF)
        me = (pos[3] * comps + k + 1).astype(F32)
        lse, post, target, grad = posterior_of(logits.T, mine[span, 4 * cols :].astype(F32).T, me)
        columns = jnp.where(row == 0, lse, jnp.where(row == 1, post, jnp.where(row == 2, target, grad))).T
        info[span, :] = columns
        sums[k : k + 1, :] = jnp.sum(mine[span, pl.ds(pl.multiple_of(pos[0] * cols, cols), cols)].astype(F32) * columns[:, 3:4], axis=0, keepdims=True)


def projection_kernel(pos, mine, other, pre, out):
    comps, _, cols = out.shape
    rows = pre.shape[0] // comps
    for k in range(comps):
        g = pre[k * rows : (k + 1) * rows, :]
        for y, side, x in half_rows((mine, other), k, rows, cols):
            value = lax.dot_general(x, g, (((0,), (0,)), ((), ())), preferred_element_type=F32)
            out[k, pl.ds(core_start(pos, y, side, cols), cols), :] = value.astype(BF)


def logit_kernel(assemble, pos, *refs):
    if assemble:
        near, far, near_o, far_o, info, emb, lg, blocks, z, z_rows = refs
        rows, cols = far.shape

        @pl.when(pl.program_id(0) == 0)
        def _():
            for dist, side, x in piece_rows((near, far, near_o, far_o), 0, rows):
                start = block_start(pos, dist, side, cols)
                z[:, pl.ds(start, cols)] = x
                z_rows[pl.ds(start, cols), :] = x.T

    else:
        z, z_rows, info, emb, lg, blocks = refs
    step = pl.program_id(0)
    width = emb.shape[1]
    logits = jnp.dot(z[...], emb[...], preferred_element_type=F32)
    first = pos[2] + step * width + (0 if assemble else pos[4])
    words = first + lax.broadcasted_iota(jnp.int32, logits.shape, 1)
    hit = (info[:, 2:3].astype(jnp.int32) == words).astype(F32)
    grads = (info[:, 1:2] * (jnp.exp(logits - info[:, 0:1]) - hit)).astype(BF)
    lg[...] = grads
    half = blocks.shape[0] // 4
    for i in range(4):
        span = slice(i * half, (i + 1) * half)
        blocks[span, :] = jnp.dot(z_rows[span, :], grads, preferred_element_type=F32).astype(BF)


def feature_kernel(added, core, lg_low, lg_high, emb, *refs):
    low = lg_low.shape[1]
    over_words = (((1,), (1,)), ((), ()))
    value = lax.dot_general(lg_low[...], emb[0, :, :low], over_words, preferred_element_type=F32)
    value += lax.dot_general(lg_high[...], emb[0, :, low:], over_words, preferred_element_type=F32)
    if added:
        value = value + refs[0][0]
    refs[-1][0] = value.astype(BF)


def feature_part(lgs, emb, core, added=None):
    slots, words = lgs[0].shape[0], emb.shape[1]
    out = pl.BlockSpec((1, slots, 256), lambda i, n: (i, 0, 0))
    more = [] if added is None else [added]
    return pl.pallas_call(
        functools.partial(feature_kernel, added is not None),
        grid_spec=pltpu.PrefetchScalarGridSpec(
            num_scalar_prefetch=1,
            grid=(4,),
            in_specs=[pl.BlockSpec(lg.shape, lambda i, n: (0, 0)) for lg in lgs]
            + [pl.BlockSpec((1, 256, words), lambda i, n: (2 * i + n[0], 0, 0))]
            + [out] * len(more),
            out_specs=out,
        ),
        out_shape=jax.ShapeDtypeStruct((4, slots, 256), BF),
        compiler_params=pltpu.CompilerParams(vmem_limit_bytes=LIMIT),
        cost_estimate=pl.CostEstimate(
            flops=2 * slots * words * 1024, bytes_accessed=7 << 20, transcendentals=0
        ),
    )(core.reshape(1).astype(jnp.int32), *lgs, emb.reshape(8, 256, words), *more)


def slot_kernel(first, core, *refs):
    if first:
        got, slope, proj, pre, out = refs

        @pl.when(pl.program_id(0) == 0)
        def _():
            total = got[0].astype(F32) + got[1].astype(F32)
            total = total + (got[2].astype(F32) + got[3].astype(F32))
            pre[...] = (total * slope[...]).astype(BF)

    else:
        pre, proj, added, out = refs
    comps = proj.shape[0]
    rows = pre.shape[0] // comps
    for k in range(comps):
        span = slice(k * rows, (k + 1) * rows)
        value = lax.dot_general(
            pre[span, :], proj[k, 0], (((1,), (1,)), ((), ())), preferred_element_type=F32
        )
        if not first:
            value = value + added[0, span, :]
        out[0, span, :] = value.astype(BF)


def slot_part(proj, core, got=None, slope=None, pre=None, added=None):
    comps, _, cols = proj.shape
    slots = (slope if pre is None else pre).shape[0]
    out = pl.BlockSpec((1, slots, cols), lambda i, n: (i, 0, 0))
    rows = pl.BlockSpec((slots, cols), lambda i, n: (0, 0))
    weights = pl.BlockSpec((comps, 1, cols, cols), lambda i, n: (0, 2 * i + n[0], 0, 0))
    view = proj.reshape(comps, 8, cols, cols)
    shape, pre_shape = jax.ShapeDtypeStruct((4, slots, cols), BF), jax.ShapeDtypeStruct((slots, cols), BF)
    if pre is None:
        operands = (got, slope, view)
        specs = [pl.BlockSpec((4, slots, cols), lambda i, n: (0, 0, 0)), rows, weights]
        outs, shapes = [rows, out], [pre_shape, shape]
    else:
        operands, specs, outs, shapes = (pre, view, added), [rows, weights, out], out, shape
    return pl.pallas_call(
        functools.partial(slot_kernel, pre is None),
        grid_spec=pltpu.PrefetchScalarGridSpec(
            num_scalar_prefetch=1, grid=(4,), in_specs=specs, out_specs=outs
        ),
        out_shape=shapes,
        compiler_params=pltpu.CompilerParams(vmem_limit_bytes=LIMIT),
        cost_estimate=pl.CostEstimate(
            flops=2 * slots * cols * 1024, bytes_accessed=3 << 20, transcendentals=0
        ),
    )(core.reshape(1).astype(jnp.int32), *operands)


def whole(a):
    return pl.BlockSpec(a.shape, lambda *_: (0,) * len(a.shape))


def shaped(shape, dtype):
    return jax.ShapeDtypeStruct(shape, dtype)


def in_three(value):
    high = lax.reduce_precision(value, 8, 7)
    middle = lax.reduce_precision(value - high, 8, 7)
    return high.astype(BF), middle.astype(BF), (value - high - middle).astype(BF)


def shards(hidden, routes, targets, saved_lse, target_logprob, prior_weight, projection, embedding):
    highest = lax.Precision.HIGHEST
    tok_dev, model_width = hidden.shape
    route_count = routes.shape[1]
    comp_dev, _, col_count = projection.shape
    voc_dev = embedding.shape[1]
    owners = lax.axis_size(ZX)
    experts_all = comp_dev * owners
    capacity = max(2, (2 * tok_dev * route_count + experts_all - 1) // experts_all)
    slot_count = owners * comp_dev * capacity
    slot_rows = owners * capacity
    slots = comp_dev * slot_rows
    zi, xi, yi, ci = (lax.axis_index(a) for a in ALL)
    vocab_index = yi * 2 + ci
    low_words = voc_dev // 2
    pos = jnp.stack([yi, ci, vocab_index * voc_dev, zi * 4 + xi, jnp.int32(low_words)]).astype(jnp.int32)
    comp_ids = jnp.arange(experts_all, dtype=jnp.int32)
    per_owner = comp_dev * capacity
    sent_width = 4 * col_count + 128
    operands = (hidden, routes.T, targets[None, :], saved_lse.T, target_logprob.T)
    results = [shaped((slot_count, sent_width), BF), shaped((slot_count, tok_dev), BF)]
    send_rows, dispatch_tokens = pl.pallas_call(
        prep_kernel,
        grid=(1,),
        in_specs=[SCALARS] + [whole(a) for a in operands],
        out_specs=[whole(r) for r in results],
        out_shape=results,
        compiler_params=pltpu.CompilerParams(vmem_limit_bytes=LIMIT),
        cost_estimate=pl.CostEstimate(
            flops=2 * slot_count * tok_dev * sent_width, bytes_accessed=2 << 20, transcendentals=0
        ),
    )(pos, *operands)
    got_rows = exchanged(send_rows.reshape(owners, per_owner, sent_width), ZX)

    pair = jnp.stack([prior_weight, flipped(prior_weight, "c", 1)])
    pair = jnp.where(ci == 0, pair, pair[::-1])
    two = jnp.stack([pair, flipped(pair, "y", 1)])
    two = jnp.where(yi % 2 == 0, two, two[::-1])
    four = jnp.stack([two, flipped(two, "y", 2)])
    four = jnp.where(yi < 2, four, four[::-1])
    prior_all = four.reshape(model_width, experts_all)
    prior_wide = jnp.pad(prior_all, ((0, 0), (0, 128 - experts_all)))
    prior_logits = jnp.dot(hidden, prior_all, preferred_element_type=F32)
    picked = (routes[:, :, None] == comp_ids[None, None, :]).astype(F32)
    selected = jnp.sum(picked * prior_logits[:, None, :], axis=2)
    gate_weights = jax.nn.softmax(selected, axis=-1)
    posterior = jax.nn.softmax(jax.nn.log_softmax(selected, axis=-1) + target_logprob, axis=-1)
    prior_grads = jnp.sum((gate_weights - posterior)[:, :, None] * picked, axis=1)
    prior_back = lax.dot_general(
        prior_grads, prior_weight.astype(F32), (((1,), (1,)), ((), ())), precision=highest
    )
    got_rows, prior_wide, prior_back = lax.optimization_barrier((got_rows, prior_wide, prior_back))

    got_rows = got_rows.reshape(owners, comp_dev, capacity, -1).transpose(1, 0, 2, 3)
    got_rows = got_rows.reshape(slots, -1)
    rows_in = (got_rows, flipped(got_rows, "c", 1))
    operands = (*rows_in, projection, prior_wide)
    results = [
        shaped((slots, col_count), F32),
        shaped((slots, col_count), BF),
        shaped((slots, 128), F32),
        shaped((8, col_count), F32),
    ]
    slope, z_own, info, prior_own = pl.pallas_call(
        activation_kernel,
        grid=(1,),
        in_specs=[SCALARS] + [whole(a) for a in operands],
        out_specs=[whole(r) for r in results],
        out_shape=results,
        compiler_params=pltpu.CompilerParams(vmem_limit_bytes=LIMIT),
        cost_estimate=pl.CostEstimate(
            flops=2 * slots * model_width * col_count, bytes_accessed=6 << 20, transcendentals=slots * col_count
        ),
    )(pos, *operands)
    z_all = gathered(z_own)

    width = 512
    z_shapes = [shaped((slots, model_width), BF), shaped((model_width, slots), BF)]

    def word_half(operands, skip, cols, assemble):
        outs = [shaped((slots, cols), BF), shaped((model_width, cols), BF)]
        specs = [pl.BlockSpec((slots, width), lambda i: (0, i)), pl.BlockSpec((model_width, width), lambda i: (0, i))]
        kept = z_shapes if assemble else []
        return pl.pallas_call(
            functools.partial(logit_kernel, assemble),
            grid=(cols // width,),
            in_specs=[SCALARS]
            + [whole(a) for a in (*operands, info)]
            + [pl.BlockSpec((model_width, width), lambda i: (0, skip // width + i))],
            out_specs=specs + [whole(k) for k in kept],
            out_shape=outs + kept,
            compiler_params=pltpu.CompilerParams(vmem_limit_bytes=LIMIT),
            cost_estimate=pl.CostEstimate(
                flops=4 * slots * model_width * cols, bytes_accessed=12 << 20, transcendentals=slots * cols
            ),
        )(pos, *operands, info, embedding)

    grads_low, blocks_low, z_cols, z_rows = word_half(z_all, 0, low_words, True)
    sum_low = lax.psum_scatter(blocks_low, "z", scatter_dimension=0, tiled=True)
    grads_high, blocks_high = word_half((z_cols, z_rows), low_words, voc_dev - low_words, False)
    sum_high = lax.psum_scatter(blocks_high, "z", scatter_dimension=0, tiled=True)
    logit_grads = (grads_low, grads_high)

    feature_theirs = flipped(feature_part(logit_grads, embedding, 1 - ci), "c", 1)
    feature_both = feature_part(logit_grads, embedding, ci, feature_theirs)
    feature_got = exchanged(feature_both, "y")
    pre_grads, slot_theirs = slot_part(projection, 1 - ci, got=feature_got, slope=slope)
    slot_both = slot_part(projection, ci, pre=pre_grads, added=flipped(slot_theirs, "c", 1))
    slot_both, sum_low = lax.optimization_barrier((slot_both, sum_low))
    slot_got = exchanged(slot_both, "y")
    slot_grads = jnp.sum(slot_got.astype(F32), axis=0).astype(BF)
    out_shape = shaped(projection.shape, BF)
    grad_projection = pl.pallas_call(
        projection_kernel,
        grid=(1,),
        in_specs=[SCALARS] + [whole(a) for a in (*rows_in, pre_grads)],
        out_specs=whole(out_shape),
        out_shape=out_shape,
        compiler_params=pltpu.CompilerParams(vmem_limit_bytes=LIMIT),
        cost_estimate=pl.CostEstimate(
            flops=2 * slots * model_width * col_count, bytes_accessed=4 << 20, transcendentals=0
        ),
    )(pos, *rows_in, pre_grads)

    pad = jnp.zeros((8 - 3 * comp_dev, col_count), BF)
    prior_pieces = jnp.concatenate([*in_three(prior_own[:comp_dev]), pad], axis=0)
    slot_grads = slot_grads.reshape(comp_dev, owners, capacity, col_count).transpose(1, 0, 2, 3)
    slot_grads = slot_grads.reshape(owners, per_owner, col_count)
    to_return = jnp.concatenate(
        [slot_grads, jnp.broadcast_to(prior_pieces, (owners, *prior_pieces.shape))], axis=1
    )
    returned = exchanged(to_return, ZX)
    route_grads = lax.dot_general(
        dispatch_tokens,
        returned[:, :per_owner].reshape(slot_count, col_count),
        (((0,), (0,)), ((), ())),
        preferred_element_type=F32,
    )
    pieces = returned[:, per_owner : per_owner + 3 * comp_dev].astype(F32)
    pieces = pieces.reshape(owners, 3, comp_dev, col_count)
    grad_prior = (pieces[:, 0] + (pieces[:, 1] + pieces[:, 2])).reshape(experts_all, col_count).T
    grad_hidden = route_grads + prior_back

    sum_low, returned = lax.optimization_barrier((sum_low, returned))
    got_low = exchanged(sum_low.reshape(4, 64, -1), "x")
    sum_high, got_low = lax.optimization_barrier((sum_high, got_low))
    got_high = exchanged(sum_high.reshape(4, 64, -1), "x")
    halves = [jnp.sum(got.astype(F32), axis=0) for got in (got_low, got_high)]
    grad_embedding = jnp.concatenate(halves, axis=1).astype(BF)
    return (grad_hidden, grad_prior, grad_projection, grad_embedding)


def solution(mesh):
    finer = Mesh(mesh.devices.reshape(8, 4, 4, 2), ALL)
    in_specs = (
        P(ZX, None),
        P(ZX, None),
        P(ZX),
        P(ZX, None),
        P(ZX, None),
        P(YC, None),
        P(ZX, None, YC),
        P(None, YC),
    )
    out_specs = (P(ZX, YC), P(YC, None), P(ZX, None, YC), P(ZX, YC))
    return jax.shard_map(
        shards, mesh=finer, in_specs=in_specs, out_specs=out_specs, check_vma=False
    )
```

```python
import functools

import jax
import jax.numpy as jnp
from jax import lax
from jax.experimental import pallas as pl
from jax.experimental.pallas import tpu as pltpu
from jax.sharding import Mesh
from jax.sharding import PartitionSpec as P

ZX = ("z", "x")
YC = ("y", "c")
ALL = ("z", "x", "y", "c")
BF = jnp.bfloat16
F32 = jnp.float32
SCALARS = pl.BlockSpec(memory_space=pltpu.SMEM)


def shifted(value, axis, by):
    n = lax.axis_size(axis)
    return lax.ppermute(value, axis, [(i, (i + by) % n) for i in range(n)])


def flipped(value, axis, bit):
    n = lax.axis_size(axis)
    return lax.ppermute(value, axis, [(i, i ^ bit) for i in range(n)])


def pick(value, index, dim):
    return lax.dynamic_index_in_dim(value, index, dim, keepdims=False)


def gathered(value):
    half = value.shape[0] // 2
    below = shifted(value, "y", 1)
    above = shifted(value, "y", -1)
    far_low = shifted(below[:half], "y", 1)
    far_high = shifted(above[half:], "y", -1)
    near = jnp.stack([value, above, below])
    far = jnp.concatenate([far_low, far_high], axis=0)
    return near, far, flipped(near, "c", 1), flipped(far, "c", 1)


def exchanged(value, axis):
    return lax.all_to_all(value, axis, 0, 0, tiled=True)


def summed_along_z(blocks):
    return lax.psum_scatter(blocks, "z", scatter_dimension=0, tiled=True)


def piece_rows(refs, k, rows):
    span = slice(k * rows, (k + 1) * rows)
    for side in range(2):
        near, far = refs[2 * side : 2 * side + 2]
        yield 0, side, near[0, span, :]
        yield 1, side, near[1, span, :]
        yield 3, side, near[2, span, :]
        yield 2, side, far[span, :]


def half_rows(refs, k, rows, cols):
    for side in range(2):
        for y in range(4):
            yield y, side, refs[side][k * rows : (k + 1) * rows, y * cols : (y + 1) * cols]


def core_start(pos, y, side, cols):
    c = pos[1] if side == 0 else 1 - pos[1]
    return pl.multiple_of((y * 2 + c) * cols, cols)


def block_start(pos, dist, side, cols):
    y = lax.rem(pos[0] + dist, 4)
    c = pos[1] if side == 0 else 1 - pos[1]
    return pl.multiple_of((y * 2 + c) * cols, cols)


def prep_kernel(pos, hidden, routes, targets, lse, tlp, send, table):
    tokens = hidden.shape[0]
    slots = table.shape[0]
    cap = slots // tokens
    ids = lax.broadcasted_iota(jnp.int32, (tokens, tokens), 0)
    token = lax.broadcasted_iota(jnp.int32, (tokens, tokens), 1)
    chosen = [(ids == routes[j : j + 1, :]).astype(F32) for j in range(4)]
    mask = chosen[0] + chosen[1] + (chosen[2] + chosen[3])
    rank = jnp.dot(mask.astype(BF), (ids < token).astype(BF), preferred_element_type=F32)
    place = (mask * (rank + 1.0)).astype(BF)
    slot = lax.broadcasted_iota(jnp.int32, (slots, tokens), 0)
    comp = lax.broadcasted_iota(jnp.int32, (slots, tokens), 1)
    spread = (lax.div(slot, cap) == comp).astype(BF)
    number = jnp.dot(spread, place, preferred_element_type=F32)
    hits = (number == (lax.rem(slot, cap) + 1).astype(F32)).astype(BF)
    table[...] = hits
    at = lax.broadcasted_iota(jnp.int32, (128, tokens), 0)
    t = targets[...]
    numbers = jnp.where(at == 0, lax.div(t, 128).astype(F32), jnp.where(at == 1, lax.rem(t, 128).astype(F32), 0.0))
    for j in range(4):
        numbers = jnp.where(at == 2 + j, (routes[j : j + 1, :] + 1).astype(F32), numbers)
        for base, ref in ((6, lse), (18, tlp)):
            value = ref[j : j + 1, :]
            high = value.astype(BF).astype(F32)
            middle = (value - high).astype(BF).astype(F32)
            numbers = jnp.where(at == base + j, high, numbers)
            numbers = jnp.where(at == base + 4 + j, middle, numbers)
            numbers = jnp.where(at == base + 8 + j, value - high - middle, numbers)
    for y in range(4):
        columns = hidden[:, pl.ds(core_start(pos, y, 0, 256), 256)]
        rows_out = jnp.dot(hits, columns, preferred_element_type=F32)
        send[:, y * 256 : (y + 1) * 256] = rows_out.astype(BF)
    picked = lax.dot_general(
        hits, numbers.astype(BF), (((1,), (1,)), ((), ())), preferred_element_type=F32
    )
    send[:, 1024:] = picked.astype(BF)


def posterior_of(prior, meta, me):
    ids = lax.broadcasted_iota(jnp.int32, prior.shape, 0).astype(F32) + 1.0
    route = [meta[2 + j : 3 + j] for j in range(4)]
    lse = [meta[6 + j : 7 + j] + (meta[10 + j : 11 + j] + meta[14 + j : 15 + j]) for j in range(4)]
    tlp = [meta[18 + j : 19 + j] + (meta[22 + j : 23 + j] + meta[26 + j : 27 + j]) for j in range(4)]
    chosen = [jnp.sum(jnp.where(ids == route[j], prior, 0.0), axis=0, keepdims=True) for j in range(4)]

    def softmax(values):
        top = functools.reduce(jnp.maximum, values)
        powers = [jnp.exp(v - top) for v in values]
        total = sum(powers[1:], powers[0])
        return [p / total for p in powers], [v - top - jnp.log(total) for v in values]

    gate, log_gate = softmax(chosen)
    post, _ = softmax([log_gate[j] + tlp[j] for j in range(4)])
    mine = [(route[j] == me).astype(F32) for j in range(4)]

    def own(values):
        return sum([mine[j] * values[j] for j in range(1, 4)], mine[0] * values[0])

    target = meta[0:1] * 128.0 + meta[1:2]
    return own(lse), own(post), target, own([gate[j] - post[j] for j in range(4)])


def activation_kernel(pos, mine, other, proj, prior, slope, z, info, sums):
    comps, _, cols = proj.shape
    rows = slope.shape[0] // comps
    row = lax.broadcasted_iota(jnp.int32, (info.shape[1], rows), 0)
    for k in range(comps):
        span = slice(k * rows, (k + 1) * rows)
        total = jnp.zeros((rows, cols), F32)
        logits = jnp.zeros((rows, prior.shape[1]), F32)
        for y, side, x in half_rows((mine, other), k, rows, cols):
            place = pl.ds(core_start(pos, y, side, cols), cols)
            total += jnp.dot(x, proj[k, place, :], preferred_element_type=F32)
            logits += jnp.dot(x, prior[place, :], preferred_element_type=F32)
        t = jnp.tanh(total)
        slope[span, :] = 1.0 - t * t
        z[span, :] = t.astype(BF)
        me = (pos[3] * comps + k + 1).astype(F32)
        lse, post, target, grad = posterior_of(logits.T, mine[span, 4 * cols :].astype(F32).T, me)
        columns = jnp.where(row == 0, lse, jnp.where(row == 1, post, jnp.where(row == 2, target, grad))).T
        info[span, :] = columns
        sums[k : k + 1, :] = jnp.sum(mine[span, pl.ds(pl.multiple_of(pos[0] * cols, cols), cols)].astype(F32) * columns[:, 3:4], axis=0, keepdims=True)


def projection_kernel(pos, mine, other, pre, out):
    comps, _, cols = out.shape
    rows = pre.shape[0] // comps
    for k in range(comps):
        g = pre[k * rows : (k + 1) * rows, :]
        for y, side, x in half_rows((mine, other), k, rows, cols):
            value = lax.dot_general(x, g, (((0,), (0,)), ((), ())), preferred_element_type=F32)
            out[k, pl.ds(core_start(pos, y, side, cols), cols), :] = value.astype(BF)


def logit_kernel(assemble, skip, pos, *refs):
    if assemble:
        near, far, near_o, far_o, info, emb, lg, blocks, z, z_rows = refs
        rows, cols = far.shape

        @pl.when(pl.program_id(0) == 0)
        def _():
            for dist, side, x in piece_rows((near, far, near_o, far_o), 0, rows):
                start = block_start(pos, dist, side, cols)
                z[:, pl.ds(start, cols)] = x
                z_rows[pl.ds(start, cols), :] = x.T

    else:
        z, z_rows, info, emb, lg, blocks = refs
    step = pl.program_id(0)
    width = emb.shape[1]
    logits = jnp.dot(z[...], emb[...], preferred_element_type=F32)
    first = pos[2] + step * width + skip
    words = first + lax.broadcasted_iota(jnp.int32, logits.shape, 1)
    hit = (info[:, 2:3].astype(jnp.int32) == words).astype(F32)
    grads = (info[:, 1:2] * (jnp.exp(logits - info[:, 0:1]) - hit)).astype(BF)
    lg[...] = grads
    half = blocks.shape[0] // 4
    for i in range(4):
        span = slice(i * half, (i + 1) * half)
        blocks[span, :] = jnp.dot(z_rows[span, :], grads, preferred_element_type=F32).astype(BF)


def feature_kernel(count, added, core, *refs):
    lgs, emb, out = refs[:count], refs[count], refs[-1]
    value, at = 0.0, 0
    for lg in lgs:
        words = lg.shape[1]
        value += lax.dot_general(
            lg[...], emb[0, :, at : at + words], (((1,), (1,)), ((), ())), preferred_element_type=F32
        )
        at += words
    if added:
        value = value + refs[count + 1][0]
    out[0] = value.astype(BF)


def feature_part(lgs, emb, core, added=None):
    slots, words = lgs[0].shape[0], emb.shape[1]
    out = pl.BlockSpec((1, slots, 256), lambda i, n: (i, 0, 0))
    more = [] if added is None else [added]
    return pl.pallas_call(
        functools.partial(feature_kernel, len(lgs), added is not None),
        grid_spec=pltpu.PrefetchScalarGridSpec(
            num_scalar_prefetch=1,
            grid=(4,),
            in_specs=[pl.BlockSpec(lg.shape, lambda i, n: (0, 0)) for lg in lgs]
            + [pl.BlockSpec((1, 256, words), lambda i, n: (2 * i + n[0], 0, 0))]
            + [out] * len(more),
            out_specs=out,
        ),
        out_shape=jax.ShapeDtypeStruct((4, slots, 256), BF),
        compiler_params=pltpu.CompilerParams(vmem_limit_bytes=60 << 20),
        cost_estimate=pl.CostEstimate(
            flops=2 * slots * words * 1024, bytes_accessed=7 << 20, transcendentals=0
        ),
    )(core.reshape(1).astype(jnp.int32), *lgs, emb.reshape(8, 256, words), *more)


def slot_kernel(first, core, *refs):
    if first:
        got, slope, proj, pre, out = refs

        @pl.when(pl.program_id(0) == 0)
        def _():
            total = got[0].astype(F32) + got[1].astype(F32)
            total = total + (got[2].astype(F32) + got[3].astype(F32))
            pre[...] = (total * slope[...]).astype(BF)

    else:
        pre, proj, added, out = refs
    comps = proj.shape[0]
    rows = pre.shape[0] // comps
    for k in range(comps):
        span = slice(k * rows, (k + 1) * rows)
        value = lax.dot_general(
            pre[span, :], proj[k, 0], (((1,), (1,)), ((), ())), preferred_element_type=F32
        )
        if not first:
            value = value + added[0, span, :]
        out[0, span, :] = value.astype(BF)


def slot_part(proj, core, got=None, slope=None, pre=None, added=None):
    comps, _, cols = proj.shape
    slots = (slope if pre is None else pre).shape[0]
    out = pl.BlockSpec((1, slots, cols), lambda i, n: (i, 0, 0))
    rows = pl.BlockSpec((slots, cols), lambda i, n: (0, 0))
    weights = pl.BlockSpec((comps, 1, cols, cols), lambda i, n: (0, 2 * i + n[0], 0, 0))
    view = proj.reshape(comps, 8, cols, cols)
    shape, pre_shape = jax.ShapeDtypeStruct((4, slots, cols), BF), jax.ShapeDtypeStruct((slots, cols), BF)
    if pre is None:
        operands = (got, slope, view)
        specs = [pl.BlockSpec((4, slots, cols), lambda i, n: (0, 0, 0)), rows, weights]
        outs, shapes = [rows, out], [pre_shape, shape]
    else:
        operands, specs, outs, shapes = (pre, view, added), [rows, weights, out], out, shape
    return pl.pallas_call(
        functools.partial(slot_kernel, pre is None),
        grid_spec=pltpu.PrefetchScalarGridSpec(
            num_scalar_prefetch=1, grid=(4,), in_specs=specs, out_specs=outs
        ),
        out_shape=shapes,
        compiler_params=pltpu.CompilerParams(vmem_limit_bytes=60 << 20),
        cost_estimate=pl.CostEstimate(
            flops=2 * slots * cols * 1024, bytes_accessed=3 << 20, transcendentals=0
        ),
    )(core.reshape(1).astype(jnp.int32), *operands)


def whole(a):
    return pl.BlockSpec(a.shape, lambda *_: (0,) * len(a.shape))


def shaped(shape, dtype):
    return jax.ShapeDtypeStruct(shape, dtype)


def in_three(value):
    high = lax.reduce_precision(value, 8, 7)
    middle = lax.reduce_precision(value - high, 8, 7)
    return high.astype(BF), middle.astype(BF), (value - high - middle).astype(BF)


def shards(hidden, routes, targets, saved_lse, target_logprob, prior_weight, projection, embedding):
    highest = lax.Precision.HIGHEST
    tok_dev, model_width = hidden.shape
    route_count = routes.shape[1]
    comp_dev, _, col_count = projection.shape
    voc_dev = embedding.shape[1]
    owners = lax.axis_size(ZX)
    experts_all = comp_dev * owners
    capacity = max(2, (2 * tok_dev * route_count + experts_all - 1) // experts_all)
    slot_count = owners * comp_dev * capacity
    slot_rows = owners * capacity
    slots = comp_dev * slot_rows
    zi, xi, yi, ci = (lax.axis_index(a) for a in ALL)
    vocab_index = yi * 2 + ci
    pos = jnp.stack([yi, ci, vocab_index * voc_dev, zi * 4 + xi]).astype(jnp.int32)
    comp_ids = jnp.arange(experts_all, dtype=jnp.int32)
    per_owner = comp_dev * capacity
    sent_width = 4 * col_count + 128
    operands = (hidden, routes.T, targets[None, :], saved_lse.T, target_logprob.T)
    results = [shaped((slot_count, sent_width), BF), shaped((slot_count, tok_dev), BF)]
    send_rows, dispatch_tokens = pl.pallas_call(
        prep_kernel,
        grid=(1,),
        in_specs=[SCALARS] + [whole(a) for a in operands],
        out_specs=[whole(r) for r in results],
        out_shape=results,
        compiler_params=pltpu.CompilerParams(vmem_limit_bytes=60 << 20),
        cost_estimate=pl.CostEstimate(
            flops=2 * slot_count * tok_dev * sent_width, bytes_accessed=2 << 20, transcendentals=0
        ),
    )(pos, *operands)
    got_rows = exchanged(send_rows.reshape(owners, per_owner, sent_width), ZX)

    pair = jnp.stack([prior_weight, flipped(prior_weight, "c", 1)])
    pair = jnp.where(ci == 0, pair, pair[::-1])
    two = jnp.stack([pair, flipped(pair, "y", 1)])
    two = jnp.where(yi % 2 == 0, two, two[::-1])
    four = jnp.stack([two, flipped(two, "y", 2)])
    four = jnp.where(yi < 2, four, four[::-1])
    prior_all = four.reshape(model_width, experts_all)
    prior_wide = jnp.pad(prior_all, ((0, 0), (0, 128 - experts_all)))
    prior_logits = jnp.dot(hidden, prior_all, preferred_element_type=F32)
    picked = (routes[:, :, None] == comp_ids[None, None, :]).astype(F32)
    selected = jnp.sum(picked * prior_logits[:, None, :], axis=2)
    gate_weights = jax.nn.softmax(selected, axis=-1)
    posterior = jax.nn.softmax(jax.nn.log_softmax(selected, axis=-1) + target_logprob, axis=-1)
    prior_grads = jnp.sum((gate_weights - posterior)[:, :, None] * picked, axis=1)
    prior_back = lax.dot_general(
        prior_grads, prior_weight.astype(F32), (((1,), (1,)), ((), ())), precision=highest
    )
    got_rows, prior_wide, prior_back = lax.optimization_barrier((got_rows, prior_wide, prior_back))

    got_rows = got_rows.reshape(owners, comp_dev, capacity, -1).transpose(1, 0, 2, 3)
    got_rows = got_rows.reshape(slots, -1)
    rows_in = (got_rows, flipped(got_rows, "c", 1))
    operands = (*rows_in, projection, prior_wide)
    results = [
        shaped((slots, col_count), F32),
        shaped((slots, col_count), BF),
        shaped((slots, 128), F32),
        shaped((8, col_count), F32),
    ]
    slope, z_own, info, prior_own = pl.pallas_call(
        activation_kernel,
        grid=(1,),
        in_specs=[SCALARS] + [whole(a) for a in operands],
        out_specs=[whole(r) for r in results],
        out_shape=results,
        compiler_params=pltpu.CompilerParams(vmem_limit_bytes=48 << 20),
        cost_estimate=pl.CostEstimate(
            flops=2 * slots * model_width * col_count, bytes_accessed=6 << 20, transcendentals=slots * col_count
        ),
    )(pos, *operands)
    z_all = gathered(z_own)

    width = 512
    z_shapes = [shaped((slots, model_width), BF), shaped((model_width, slots), BF)]

    def word_part(operands, skip, cols, assemble):
        outs = [shaped((slots, cols), BF), shaped((model_width, cols), BF)]
        specs = [pl.BlockSpec((slots, width), lambda i: (0, i)), pl.BlockSpec((model_width, width), lambda i: (0, i))]
        kept = z_shapes if assemble else []
        return pl.pallas_call(
            functools.partial(logit_kernel, assemble, skip),
            grid=(cols // width,),
            in_specs=[SCALARS]
            + [whole(a) for a in (*operands, info)]
            + [pl.BlockSpec((model_width, width), lambda i: (0, skip // width + i))],
            out_specs=specs + [whole(k) for k in kept],
            out_shape=outs + kept,
            compiler_params=pltpu.CompilerParams(vmem_limit_bytes=(50 if assemble else 60) << 20),
            cost_estimate=pl.CostEstimate(
                flops=4 * slots * model_width * cols, bytes_accessed=12 << 20, transcendentals=slots * cols
            ),
        )(pos, *operands, info, embedding)

    cuts = (0, width, voc_dev - width, voc_dev)
    first_grads, first_blocks, z_cols, z_rows = word_part(z_all, cuts[0], cuts[1] - cuts[0], True)
    logit_grads, sums = [first_grads], [summed_along_z(first_blocks)]
    for start, stop in zip(cuts[1:], cuts[2:]):
        grads, blocks = word_part((z_cols, z_rows), start, stop - start, False)
        logit_grads.append(grads)
        sums.append(summed_along_z(blocks))

    feature_theirs = flipped(feature_part(logit_grads, embedding, 1 - ci), "c", 1)
    feature_both = feature_part(logit_grads, embedding, ci, feature_theirs)
    feature_got = exchanged(feature_both, "y")
    pre_grads, slot_theirs = slot_part(projection, 1 - ci, got=feature_got, slope=slope)
    slot_both = slot_part(projection, ci, pre=pre_grads, added=flipped(slot_theirs, "c", 1))
    slot_both, sums[0] = lax.optimization_barrier((slot_both, sums[0]))
    slot_got = exchanged(slot_both, "y")
    slot_grads = jnp.sum(slot_got.astype(F32), axis=0).astype(BF)
    out_shape = shaped(projection.shape, BF)
    grad_projection = pl.pallas_call(
        projection_kernel,
        grid=(1,),
        in_specs=[SCALARS] + [whole(a) for a in (*rows_in, pre_grads)],
        out_specs=whole(out_shape),
        out_shape=out_shape,
        compiler_params=pltpu.CompilerParams(vmem_limit_bytes=60 << 20),
        cost_estimate=pl.CostEstimate(
            flops=2 * slots * model_width * col_count, bytes_accessed=4 << 20, transcendentals=0
        ),
    )(pos, *rows_in, pre_grads)

    pad = jnp.zeros((8 - 3 * comp_dev, col_count), BF)
    prior_pieces = jnp.concatenate([*in_three(prior_own[:comp_dev]), pad], axis=0)
    slot_grads = slot_grads.reshape(comp_dev, owners, capacity, col_count).transpose(1, 0, 2, 3)
    slot_grads = slot_grads.reshape(owners, per_owner, col_count)
    to_return = jnp.concatenate(
        [slot_grads, jnp.broadcast_to(prior_pieces, (owners, *prior_pieces.shape))], axis=1
    )
    returned = exchanged(to_return, ZX)
    route_grads = lax.dot_general(
        dispatch_tokens,
        returned[:, :per_owner].reshape(slot_count, col_count),
        (((0,), (0,)), ((), ())),
        preferred_element_type=F32,
    )
    pieces = returned[:, per_owner : per_owner + 3 * comp_dev].astype(F32)
    pieces = pieces.reshape(owners, 3, comp_dev, col_count)
    grad_prior = (pieces[:, 0] + (pieces[:, 1] + pieces[:, 2])).reshape(experts_all, col_count).T
    grad_hidden = route_grads + prior_back

    early = jnp.concatenate(sums[:-1], axis=1)
    early, returned = lax.optimization_barrier((early, returned))
    got_early = exchanged(early.reshape(4, 64, -1), "x")
    late, got_early = lax.optimization_barrier((sums[-1], got_early))
    got_late = exchanged(late.reshape(4, 64, -1), "x")
    parts = [jnp.sum(got.astype(F32), axis=0) for got in (got_early, got_late)]
    grad_embedding = jnp.concatenate(parts, axis=1).astype(BF)
    return (grad_hidden, grad_prior, grad_projection, grad_embedding)


def solution(mesh):
    finer = Mesh(mesh.devices.reshape(8, 4, 4, 2), ALL)
    in_specs = (
        P(ZX, None),
        P(ZX, None),
        P(ZX),
        P(ZX, None),
        P(ZX, None),
        P(YC, None),
        P(ZX, None, YC),
        P(None, YC),
    )
    out_specs = (P(ZX, YC), P(YC, None), P(ZX, None, YC), P(ZX, YC))
    return jax.shard_map(
        shards, mesh=finer, in_specs=in_specs, out_specs=out_specs, check_vma=False
    )
```

```python
import functools

import jax
import jax.numpy as jnp
from jax import lax
from jax.experimental import pallas as pl
from jax.experimental.pallas import tpu as pltpu
from jax.sharding import Mesh
from jax.sharding import PartitionSpec as P

ZX = ("z", "x")
YC = ("y", "c")
ALL = ("z", "x", "y", "c")
BF = jnp.bfloat16
F32 = jnp.float32
SCALARS = pl.BlockSpec(memory_space=pltpu.SMEM)


def shifted(value, axis, by):
    n = lax.axis_size(axis)
    return lax.ppermute(value, axis, [(i, (i + by) % n) for i in range(n)])


def flipped(value, axis, bit):
    n = lax.axis_size(axis)
    return lax.ppermute(value, axis, [(i, i ^ bit) for i in range(n)])


def pick(value, index, dim):
    return lax.dynamic_index_in_dim(value, index, dim, keepdims=False)


def gathered(value):
    half = value.shape[0] // 2
    below = shifted(value, "y", 1)
    above = shifted(value, "y", -1)
    far_low = shifted(below[:half], "y", 1)
    far_high = shifted(above[half:], "y", -1)
    near = jnp.stack([value, above, below])
    far = jnp.concatenate([far_low, far_high], axis=0)
    return near, far, flipped(near, "c", 1), flipped(far, "c", 1)


def exchanged(value, axis):
    return lax.all_to_all(value, axis, 0, 0, tiled=True)


def summed_along_z(blocks):
    return lax.psum_scatter(blocks, "z", scatter_dimension=0, tiled=True)


def piece_rows(refs, k, rows):
    span = slice(k * rows, (k + 1) * rows)
    for side in range(2):
        near, far = refs[2 * side : 2 * side + 2]
        yield 0, side, near[0, span, :]
        yield 1, side, near[1, span, :]
        yield 3, side, near[2, span, :]
        yield 2, side, far[span, :]


def half_rows(refs, k, rows, cols):
    for side in range(2):
        for y in range(4):
            yield y, side, refs[side][k * rows : (k + 1) * rows, y * cols : (y + 1) * cols]


def core_start(pos, y, side, cols):
    c = pos[1] if side == 0 else 1 - pos[1]
    return pl.multiple_of((y * 2 + c) * cols, cols)


def block_start(pos, dist, side, cols):
    y = lax.rem(pos[0] + dist, 4)
    c = pos[1] if side == 0 else 1 - pos[1]
    return pl.multiple_of((y * 2 + c) * cols, cols)


def prep_kernel(pos, hidden, routes, targets, lse, tlp, send, table):
    tokens = hidden.shape[0]
    slots = table.shape[0]
    cap = slots // tokens
    ids = lax.broadcasted_iota(jnp.int32, (tokens, tokens), 0)
    token = lax.broadcasted_iota(jnp.int32, (tokens, tokens), 1)
    chosen = [(ids == routes[j : j + 1, :]).astype(F32) for j in range(4)]
    mask = chosen[0] + chosen[1] + (chosen[2] + chosen[3])
    rank = jnp.dot(mask.astype(BF), (ids < token).astype(BF), preferred_element_type=F32)
    place = (mask * (rank + 1.0)).astype(BF)
    slot = lax.broadcasted_iota(jnp.int32, (slots, tokens), 0)
    comp = lax.broadcasted_iota(jnp.int32, (slots, tokens), 1)
    spread = (lax.div(slot, cap) == comp).astype(BF)
    number = jnp.dot(spread, place, preferred_element_type=F32)
    hits = (number == (lax.rem(slot, cap) + 1).astype(F32)).astype(BF)
    table[...] = hits
    at = lax.broadcasted_iota(jnp.int32, (128, tokens), 0)
    t = targets[...]
    numbers = jnp.where(at == 0, lax.div(t, 128).astype(F32), jnp.where(at == 1, lax.rem(t, 128).astype(F32), 0.0))
    for j in range(4):
        numbers = jnp.where(at == 2 + j, (routes[j : j + 1, :] + 1).astype(F32), numbers)
        for base, ref in ((6, lse), (18, tlp)):
            value = ref[j : j + 1, :]
            high = value.astype(BF).astype(F32)
            middle = (value - high).astype(BF).astype(F32)
            numbers = jnp.where(at == base + j, high, numbers)
            numbers = jnp.where(at == base + 4 + j, middle, numbers)
            numbers = jnp.where(at == base + 8 + j, value - high - middle, numbers)
    for y in range(4):
        columns = hidden[:, pl.ds(core_start(pos, y, 0, 256), 256)]
        rows_out = jnp.dot(hits, columns, preferred_element_type=F32)
        send[:, y * 256 : (y + 1) * 256] = rows_out.astype(BF)
    picked = lax.dot_general(
        hits, numbers.astype(BF), (((1,), (1,)), ((), ())), preferred_element_type=F32
    )
    send[:, 1024:] = picked.astype(BF)


def posterior_of(prior, meta, me):
    ids = lax.broadcasted_iota(jnp.int32, prior.shape, 0).astype(F32) + 1.0
    route = [meta[2 + j : 3 + j] for j in range(4)]
    lse = [meta[6 + j : 7 + j] + (meta[10 + j : 11 + j] + meta[14 + j : 15 + j]) for j in range(4)]
    tlp = [meta[18 + j : 19 + j] + (meta[22 + j : 23 + j] + meta[26 + j : 27 + j]) for j in range(4)]
    chosen = [jnp.sum(jnp.where(ids == route[j], prior, 0.0), axis=0, keepdims=True) for j in range(4)]

    def softmax(values):
        top = functools.reduce(jnp.maximum, values)
        powers = [jnp.exp(v - top) for v in values]
        total = sum(powers[1:], powers[0])
        return [p / total for p in powers], [v - top - jnp.log(total) for v in values]

    gate, log_gate = softmax(chosen)
    post, _ = softmax([log_gate[j] + tlp[j] for j in range(4)])
    mine = [(route[j] == me).astype(F32) for j in range(4)]

    def own(values):
        return sum([mine[j] * values[j] for j in range(1, 4)], mine[0] * values[0])

    target = meta[0:1] * 128.0 + meta[1:2]
    return own(lse), own(post), target, own([gate[j] - post[j] for j in range(4)])


def activation_kernel(pos, mine, other, proj, prior, slope, z, info, sums):
    comps, _, cols = proj.shape
    rows = slope.shape[0] // comps
    row = lax.broadcasted_iota(jnp.int32, (info.shape[1], rows), 0)
    for k in range(comps):
        span = slice(k * rows, (k + 1) * rows)
        total = jnp.zeros((rows, cols), F32)
        logits = jnp.zeros((rows, prior.shape[1]), F32)
        for y, side, x in half_rows((mine, other), k, rows, cols):
            place = pl.ds(core_start(pos, y, side, cols), cols)
            total += jnp.dot(x, proj[k, place, :], preferred_element_type=F32)
            logits += jnp.dot(x, prior[place, :], preferred_element_type=F32)
        t = jnp.tanh(total)
        slope[span, :] = 1.0 - t * t
        z[span, :] = t.astype(BF)
        me = (pos[3] * comps + k + 1).astype(F32)
        lse, post, target, grad = posterior_of(logits.T, mine[span, 4 * cols :].astype(F32).T, me)
        columns = jnp.where(row == 0, lse, jnp.where(row == 1, post, jnp.where(row == 2, target, grad))).T
        info[span, :] = columns
        sums[k : k + 1, :] = jnp.sum(mine[span, pl.ds(pl.multiple_of(pos[0] * cols, cols), cols)].astype(F32) * columns[:, 3:4], axis=0, keepdims=True)


def projection_kernel(pos, mine, other, pre, out):
    comps, _, cols = out.shape
    rows = pre.shape[0] // comps
    for k in range(comps):
        g = pre[k * rows : (k + 1) * rows, :]
        for y, side, x in half_rows((mine, other), k, rows, cols):
            value = lax.dot_general(x, g, (((0,), (0,)), ((), ())), preferred_element_type=F32)
            out[k, pl.ds(core_start(pos, y, side, cols), cols), :] = value.astype(BF)


def logit_kernel(pos, near, far, near_o, far_o, info, emb, lg, blocks, z, z_rows):
    step = pl.program_id(0)
    rows, cols = far.shape
    width = emb.shape[1]

    @pl.when(step == 0)
    def _():
        for dist, side, x in piece_rows((near, far, near_o, far_o), 0, rows):
            start = block_start(pos, dist, side, cols)
            z[:, pl.ds(start, cols)] = x
            z_rows[pl.ds(start, cols), :] = x.T

    logits = jnp.dot(z[...], emb[...], preferred_element_type=F32)
    words = pos[2] + step * width + lax.broadcasted_iota(jnp.int32, logits.shape, 1)
    hit = (info[:, 2:3].astype(jnp.int32) == words).astype(F32)
    grads = (info[:, 1:2] * (jnp.exp(logits - info[:, 0:1]) - hit)).astype(BF)
    lg[...] = grads
    part = blocks.shape[0] // 4
    for i in range(4):
        span = slice(i * part, (i + 1) * part)
        blocks[span, :] = jnp.dot(z_rows[span, :], grads, preferred_element_type=F32).astype(BF)


def feature_kernel(count, added, core, *refs):
    lgs, emb, out = refs[:count], refs[count], refs[-1]
    value, at = 0.0, 0
    for lg in lgs:
        words = lg.shape[1]
        value += lax.dot_general(
            lg[...], emb[0, :, at : at + words], (((1,), (1,)), ((), ())), preferred_element_type=F32
        )
        at += words
    if added:
        value = value + refs[count + 1][0]
    out[0] = value.astype(BF)


def feature_part(lgs, emb, core, added=None):
    slots, words = lgs[0].shape[0], emb.shape[1]
    out = pl.BlockSpec((1, slots, 256), lambda i, n: (i, 0, 0))
    more = [] if added is None else [added]
    return pl.pallas_call(
        functools.partial(feature_kernel, len(lgs), added is not None),
        grid_spec=pltpu.PrefetchScalarGridSpec(
            num_scalar_prefetch=1,
            grid=(4,),
            in_specs=[pl.BlockSpec(lg.shape, lambda i, n: (0, 0)) for lg in lgs]
            + [pl.BlockSpec((1, 256, words), lambda i, n: (2 * i + n[0], 0, 0))]
            + [out] * len(more),
            out_specs=out,
        ),
        out_shape=jax.ShapeDtypeStruct((4, slots, 256), BF),
        compiler_params=pltpu.CompilerParams(vmem_limit_bytes=48 << 20),
        cost_estimate=pl.CostEstimate(
            flops=2 * slots * words * 1024, bytes_accessed=7 << 20, transcendentals=0
        ),
    )(core.reshape(1).astype(jnp.int32), *lgs, emb.reshape(8, 256, words), *more)


def slot_kernel(first, core, *refs):
    if first:
        got, slope, proj, pre, out = refs

        @pl.when(pl.program_id(0) == 0)
        def _():
            total = got[0].astype(F32) + got[1].astype(F32)
            total = total + (got[2].astype(F32) + got[3].astype(F32))
            pre[...] = (total * slope[...]).astype(BF)

    else:
        pre, proj, added, out = refs
    comps = proj.shape[0]
    rows = pre.shape[0] // comps
    for k in range(comps):
        span = slice(k * rows, (k + 1) * rows)
        value = lax.dot_general(
            pre[span, :], proj[k, 0], (((1,), (1,)), ((), ())), preferred_element_type=F32
        )
        if not first:
            value = value + added[0, span, :]
        out[0, span, :] = value.astype(BF)


def slot_part(proj, core, got=None, slope=None, pre=None, added=None):
    comps, _, cols = proj.shape
    slots = (slope if pre is None else pre).shape[0]
    out = pl.BlockSpec((1, slots, cols), lambda i, n: (i, 0, 0))
    rows = pl.BlockSpec((slots, cols), lambda i, n: (0, 0))
    weights = pl.BlockSpec((comps, 1, cols, cols), lambda i, n: (0, 2 * i + n[0], 0, 0))
    view = proj.reshape(comps, 8, cols, cols)
    shape, pre_shape = jax.ShapeDtypeStruct((4, slots, cols), BF), jax.ShapeDtypeStruct((slots, cols), BF)
    if pre is None:
        operands = (got, slope, view)
        specs = [pl.BlockSpec((4, slots, cols), lambda i, n: (0, 0, 0)), rows, weights]
        outs, shapes = [rows, out], [pre_shape, shape]
    else:
        operands, specs, outs, shapes = (pre, view, added), [rows, weights, out], out, shape
    return pl.pallas_call(
        functools.partial(slot_kernel, pre is None),
        grid_spec=pltpu.PrefetchScalarGridSpec(
            num_scalar_prefetch=1, grid=(4,), in_specs=specs, out_specs=outs
        ),
        out_shape=shapes,
        compiler_params=pltpu.CompilerParams(vmem_limit_bytes=48 << 20),
        cost_estimate=pl.CostEstimate(
            flops=2 * slots * cols * 1024, bytes_accessed=3 << 20, transcendentals=0
        ),
    )(core.reshape(1).astype(jnp.int32), *operands)


def whole(a):
    return pl.BlockSpec(a.shape, lambda *_: (0,) * len(a.shape))


def shaped(shape, dtype):
    return jax.ShapeDtypeStruct(shape, dtype)


def in_three(value):
    high = lax.reduce_precision(value, 8, 7)
    middle = lax.reduce_precision(value - high, 8, 7)
    return high.astype(BF), middle.astype(BF), (value - high - middle).astype(BF)


def shards(hidden, routes, targets, saved_lse, target_logprob, prior_weight, projection, embedding):
    highest = lax.Precision.HIGHEST
    tok_dev, model_width = hidden.shape
    route_count = routes.shape[1]
    comp_dev, _, col_count = projection.shape
    voc_dev = embedding.shape[1]
    owners = lax.axis_size(ZX)
    experts_all = comp_dev * owners
    capacity = max(2, (2 * tok_dev * route_count + experts_all - 1) // experts_all)
    slot_count = owners * comp_dev * capacity
    slot_rows = owners * capacity
    slots = comp_dev * slot_rows
    zi, xi, yi, ci = (lax.axis_index(a) for a in ALL)
    vocab_index = yi * 2 + ci
    pos = jnp.stack([yi, ci, vocab_index * voc_dev, zi * 4 + xi]).astype(jnp.int32)
    comp_ids = jnp.arange(experts_all, dtype=jnp.int32)
    per_owner = comp_dev * capacity
    sent_width = 4 * col_count + 128
    operands = (hidden, routes.T, targets[None, :], saved_lse.T, target_logprob.T)
    results = [shaped((slot_count, sent_width), BF), shaped((slot_count, tok_dev), BF)]
    send_rows, dispatch_tokens = pl.pallas_call(
        prep_kernel,
        grid=(1,),
        in_specs=[SCALARS] + [whole(a) for a in operands],
        out_specs=[whole(r) for r in results],
        out_shape=results,
        compiler_params=pltpu.CompilerParams(vmem_limit_bytes=60 << 20),
        cost_estimate=pl.CostEstimate(
            flops=2 * slot_count * tok_dev * sent_width, bytes_accessed=2 << 20, transcendentals=0
        ),
    )(pos, *operands)
    got_rows = exchanged(send_rows.reshape(owners, per_owner, sent_width), ZX)

    pair = jnp.stack([prior_weight, flipped(prior_weight, "c", 1)])
    pair = jnp.where(ci == 0, pair, pair[::-1])
    two = jnp.stack([pair, flipped(pair, "y", 1)])
    two = jnp.where(yi % 2 == 0, two, two[::-1])
    four = jnp.stack([two, flipped(two, "y", 2)])
    four = jnp.where(yi < 2, four, four[::-1])
    prior_all = four.reshape(model_width, experts_all)
    prior_wide = jnp.pad(prior_all, ((0, 0), (0, 128 - experts_all)))
    prior_logits = jnp.dot(hidden, prior_all, preferred_element_type=F32)
    picked = (routes[:, :, None] == comp_ids[None, None, :]).astype(F32)
    selected = jnp.sum(picked * prior_logits[:, None, :], axis=2)
    gate_weights = jax.nn.softmax(selected, axis=-1)
    posterior = jax.nn.softmax(jax.nn.log_softmax(selected, axis=-1) + target_logprob, axis=-1)
    prior_grads = jnp.sum((gate_weights - posterior)[:, :, None] * picked, axis=1)
    prior_back = lax.dot_general(
        prior_grads, prior_weight.astype(F32), (((1,), (1,)), ((), ())), precision=highest
    )
    got_rows, prior_wide, prior_back = lax.optimization_barrier((got_rows, prior_wide, prior_back))

    got_rows = got_rows.reshape(owners, comp_dev, capacity, -1).transpose(1, 0, 2, 3)
    got_rows = got_rows.reshape(slots, -1)
    rows_in = (got_rows, flipped(got_rows, "c", 1))
    operands = (*rows_in, projection, prior_wide)
    results = [
        shaped((slots, col_count), F32),
        shaped((slots, col_count), BF),
        shaped((slots, 128), F32),
        shaped((8, col_count), F32),
    ]
    slope, z_own, info, prior_own = pl.pallas_call(
        activation_kernel,
        grid=(1,),
        in_specs=[SCALARS] + [whole(a) for a in operands],
        out_specs=[whole(r) for r in results],
        out_shape=results,
        compiler_params=pltpu.CompilerParams(vmem_limit_bytes=48 << 20),
        cost_estimate=pl.CostEstimate(
            flops=2 * slots * model_width * col_count, bytes_accessed=6 << 20, transcendentals=slots * col_count
        ),
    )(pos, *operands)
    z_all = gathered(z_own)

    width = 512
    grads, blocks = pl.pallas_call(
        logit_kernel,
        grid=(voc_dev // width,),
        in_specs=[SCALARS]
        + [whole(a) for a in (*z_all, info)]
        + [pl.BlockSpec((model_width, width), lambda i: (0, i))],
        out_specs=[
            pl.BlockSpec((slots, width), lambda i: (0, i)),
            pl.BlockSpec((model_width, width), lambda i: (0, i)),
        ],
        out_shape=[shaped((slots, voc_dev), BF), shaped((model_width, voc_dev), BF)],
        scratch_shapes=[pltpu.VMEM((slots, model_width), BF), pltpu.VMEM((model_width, slots), BF)],
        compiler_params=pltpu.CompilerParams(vmem_limit_bytes=50 << 20),
        cost_estimate=pl.CostEstimate(
            flops=4 * slots * model_width * voc_dev, bytes_accessed=24 << 20, transcendentals=slots * voc_dev
        ),
    )(pos, *z_all, info, embedding)
    logit_grads = (grads,)
    z_sum = summed_along_z(blocks)

    feature_theirs = flipped(feature_part(logit_grads, embedding, 1 - ci), "c", 1)
    feature_both = feature_part(logit_grads, embedding, ci, feature_theirs)
    feature_got = exchanged(feature_both, "y")
    pre_grads, slot_theirs = slot_part(projection, 1 - ci, got=feature_got, slope=slope)
    slot_both = slot_part(projection, ci, pre=pre_grads, added=flipped(slot_theirs, "c", 1))
    slot_got = exchanged(slot_both, "y")
    slot_grads = jnp.sum(slot_got.astype(F32), axis=0).astype(BF)
    out_shape = shaped(projection.shape, BF)
    grad_projection = pl.pallas_call(
        projection_kernel,
        grid=(1,),
        in_specs=[SCALARS] + [whole(a) for a in (*rows_in, pre_grads)],
        out_specs=whole(out_shape),
        out_shape=out_shape,
        compiler_params=pltpu.CompilerParams(vmem_limit_bytes=48 << 20),
        cost_estimate=pl.CostEstimate(
            flops=2 * slots * model_width * col_count, bytes_accessed=4 << 20, transcendentals=0
        ),
    )(pos, *rows_in, pre_grads)

    pad = jnp.zeros((8 - 3 * comp_dev, col_count), BF)
    prior_pieces = jnp.concatenate([*in_three(prior_own[:comp_dev]), pad], axis=0)
    slot_grads = slot_grads.reshape(comp_dev, owners, capacity, col_count).transpose(1, 0, 2, 3)
    slot_grads = slot_grads.reshape(owners, per_owner, col_count)
    to_return = jnp.concatenate(
        [slot_grads, jnp.broadcast_to(prior_pieces, (owners, *prior_pieces.shape))], axis=1
    )
    returned = exchanged(to_return, ZX)
    route_grads = lax.dot_general(
        dispatch_tokens,
        returned[:, :per_owner].reshape(slot_count, col_count),
        (((0,), (0,)), ((), ())),
        preferred_element_type=F32,
    )
    pieces = returned[:, per_owner : per_owner + 3 * comp_dev].astype(F32)
    pieces = pieces.reshape(owners, 3, comp_dev, col_count)
    grad_prior = (pieces[:, 0] + (pieces[:, 1] + pieces[:, 2])).reshape(experts_all, col_count).T
    grad_hidden = route_grads + prior_back

    z_sum, returned = lax.optimization_barrier((z_sum, returned))
    got = exchanged(z_sum.reshape(4, 64, -1), "x")
    grad_embedding = jnp.sum(got.astype(F32), axis=0).astype(BF)
    return (grad_hidden, grad_prior, grad_projection, grad_embedding)


def solution(mesh):
    finer = Mesh(mesh.devices.reshape(8, 4, 4, 2), ALL)
    in_specs = (
        P(ZX, None),
        P(ZX, None),
        P(ZX),
        P(ZX, None),
        P(ZX, None),
        P(YC, None),
        P(ZX, None, YC),
        P(None, YC),
    )
    out_specs = (P(ZX, YC), P(YC, None), P(ZX, None, YC), P(ZX, YC))
    return jax.shard_map(
        shards, mesh=finer, in_specs=in_specs, out_specs=out_specs, check_vma=False
    )
```

```python
import functools

import jax
import jax.numpy as jnp
from jax import lax
from jax.experimental import pallas as pl
from jax.experimental.pallas import tpu as pltpu
from jax.sharding import Mesh
from jax.sharding import PartitionSpec as P

ZX = ("z", "x")
YC = ("y", "c")
ALL = ("z", "x", "y", "c")
BF = jnp.bfloat16
F32 = jnp.float32
SCALARS = pl.BlockSpec(memory_space=pltpu.SMEM)


def shifted(value, axis, by):
    n = lax.axis_size(axis)
    return lax.ppermute(value, axis, [(i, (i + by) % n) for i in range(n)])


def flipped(value, axis, bit):
    n = lax.axis_size(axis)
    return lax.ppermute(value, axis, [(i, i ^ bit) for i in range(n)])


def pick(value, index, dim):
    return lax.dynamic_index_in_dim(value, index, dim, keepdims=False)


def gathered(value):
    half = value.shape[0] // 2
    below = shifted(value, "y", 1)
    above = shifted(value, "y", -1)
    far_low = shifted(below[:half], "y", 1)
    far_high = shifted(above[half:], "y", -1)
    near = jnp.stack([value, above, below])
    far = jnp.concatenate([far_low, far_high], axis=0)
    return near, far, flipped(near, "c", 1), flipped(far, "c", 1)


def exchanged(value, axis):
    return lax.all_to_all(value, axis, 0, 0, tiled=True)


def summed_along_z(blocks):
    return lax.psum_scatter(blocks, "z", scatter_dimension=0, tiled=True)


def piece_rows(refs, k, rows):
    span = slice(k * rows, (k + 1) * rows)
    for side in range(2):
        near, far = refs[2 * side : 2 * side + 2]
        yield 0, side, near[0, span, :]
        yield 1, side, near[1, span, :]
        yield 3, side, near[2, span, :]
        yield 2, side, far[span, :]


def component_rows(ref, k, columns):
    owners, slots, _ = ref.shape
    part = ref[:, k * (slots // 2) : (k + 1) * (slots // 2), columns]
    return part.reshape(owners * slots // 2, part.shape[2])


def half_rows(refs, k, cols):
    for side in range(2):
        for y in range(4):
            yield y, side, component_rows(refs[side], k, slice(y * cols, (y + 1) * cols))


def core_start(pos, y, side, cols):
    c = pos[1] if side == 0 else 1 - pos[1]
    return pl.multiple_of((y * 2 + c) * cols, cols)


def block_start(pos, dist, side, cols):
    y = lax.rem(pos[0] + dist, 4)
    c = pos[1] if side == 0 else 1 - pos[1]
    return pl.multiple_of((y * 2 + c) * cols, cols)


def prep_kernel(pos, hidden, routes, targets, lse, tlp, send, table):
    tokens = hidden.shape[0]
    slots = table.shape[0]
    cap = slots // tokens
    ids = lax.broadcasted_iota(jnp.int32, (tokens, tokens), 0)
    token = lax.broadcasted_iota(jnp.int32, (tokens, tokens), 1)
    chosen = [(ids == routes[j : j + 1, :]).astype(F32) for j in range(4)]
    mask = chosen[0] + chosen[1] + (chosen[2] + chosen[3])
    rank = jnp.dot(mask.astype(BF), (ids < token).astype(BF), preferred_element_type=F32)
    place = (mask * (rank + 1.0)).astype(BF)
    slot = lax.broadcasted_iota(jnp.int32, (slots, tokens), 0)
    comp = lax.broadcasted_iota(jnp.int32, (slots, tokens), 1)
    spread = (lax.div(slot, cap) == comp).astype(BF)
    number = jnp.dot(spread, place, preferred_element_type=F32)
    hits = (number == (lax.rem(slot, cap) + 1).astype(F32)).astype(BF)
    table[...] = hits
    at = lax.broadcasted_iota(jnp.int32, (128, tokens), 0)
    t = targets[...]
    numbers = jnp.where(at == 0, lax.div(t, 128).astype(F32), jnp.where(at == 1, lax.rem(t, 128).astype(F32), 0.0))
    for j in range(4):
        numbers = jnp.where(at == 2 + j, (routes[j : j + 1, :] + 1).astype(F32), numbers)
        for base, ref in ((6, lse), (18, tlp)):
            value = ref[j : j + 1, :]
            high = value.astype(BF).astype(F32)
            middle = (value - high).astype(BF).astype(F32)
            numbers = jnp.where(at == base + j, high, numbers)
            numbers = jnp.where(at == base + 4 + j, middle, numbers)
            numbers = jnp.where(at == base + 8 + j, value - high - middle, numbers)
    for y in range(4):
        columns = hidden[:, pl.ds(core_start(pos, y, 0, 256), 256)]
        rows_out = jnp.dot(hits, columns, preferred_element_type=F32)
        send[:, y * 256 : (y + 1) * 256] = rows_out.astype(BF)
    picked = lax.dot_general(
        hits, numbers.astype(BF), (((1,), (1,)), ((), ())), preferred_element_type=F32
    )
    send[:, 1024:] = picked.astype(BF)


def posterior_of(prior, meta, me):
    ids = lax.broadcasted_iota(jnp.int32, prior.shape, 0).astype(F32) + 1.0
    route = [meta[2 + j : 3 + j] for j in range(4)]
    lse = [meta[6 + j : 7 + j] + (meta[10 + j : 11 + j] + meta[14 + j : 15 + j]) for j in range(4)]
    tlp = [meta[18 + j : 19 + j] + (meta[22 + j : 23 + j] + meta[26 + j : 27 + j]) for j in range(4)]
    chosen = [jnp.sum(jnp.where(ids == route[j], prior, 0.0), axis=0, keepdims=True) for j in range(4)]

    def softmax(values):
        top = functools.reduce(jnp.maximum, values)
        powers = [jnp.exp(v - top) for v in values]
        total = sum(powers[1:], powers[0])
        return [p / total for p in powers], [v - top - jnp.log(total) for v in values]

    gate, log_gate = softmax(chosen)
    post, _ = softmax([log_gate[j] + tlp[j] for j in range(4)])
    mine = [(route[j] == me).astype(F32) for j in range(4)]

    def own(values):
        return sum([mine[j] * values[j] for j in range(1, 4)], mine[0] * values[0])

    target = meta[0:1] * 128.0 + meta[1:2]
    return own(lse), own(post), target, own([gate[j] - post[j] for j in range(4)])


def activation_kernel(pos, mine, other, proj, prior, slope, z, info, sums):
    comps, _, cols = proj.shape
    rows = slope.shape[0] // comps
    row = lax.broadcasted_iota(jnp.int32, (info.shape[1], rows), 0)
    for k in range(comps):
        span = slice(k * rows, (k + 1) * rows)
        total = jnp.zeros((rows, cols), F32)
        logits = jnp.zeros((rows, prior.shape[1]), F32)
        for y, side, x in half_rows((mine, other), k, cols):
            place = pl.ds(core_start(pos, y, side, cols), cols)
            total += jnp.dot(x, proj[k, place, :], preferred_element_type=F32)
            logits += jnp.dot(x, prior[place, :], preferred_element_type=F32)
        t = jnp.tanh(total)
        slope[span, :] = 1.0 - t * t
        z[span, :] = t.astype(BF)
        me = (pos[3] * comps + k + 1).astype(F32)
        lse, post, target, grad = posterior_of(logits.T, component_rows(mine, k, slice(4 * cols, 4 * cols + 128)).astype(F32).T, me)
        columns = jnp.where(row == 0, lse, jnp.where(row == 1, post, jnp.where(row == 2, target, grad))).T
        info[span, :] = columns
        sums[k : k + 1, :] = jnp.sum(component_rows(mine, k, pl.ds(pl.multiple_of(pos[0] * cols, cols), cols)).astype(F32) * columns[:, 3:4], axis=0, keepdims=True)


def projection_kernel(pos, mine, other, pre, out):
    comps, _, cols = out.shape
    rows = pre.shape[0] // comps
    for k in range(comps):
        g = pre[k * rows : (k + 1) * rows, :]
        for y, side, x in half_rows((mine, other), k, cols):
            value = lax.dot_general(x, g, (((0,), (0,)), ((), ())), preferred_element_type=F32)
            out[k, pl.ds(core_start(pos, y, side, cols), cols), :] = value.astype(BF)


def logit_kernel(pos, near, far, near_o, far_o, info, emb, lg, blocks, z, z_rows):
    step = pl.program_id(0)
    rows, cols = far.shape
    width = emb.shape[1]

    @pl.when(step == 0)
    def _():
        for dist, side, x in piece_rows((near, far, near_o, far_o), 0, rows):
            start = block_start(pos, dist, side, cols)
            z[:, pl.ds(start, cols)] = x
            z_rows[pl.ds(start, cols), :] = x.T

    logits = jnp.dot(z[...], emb[...], preferred_element_type=F32)
    words = pos[2] + step * width + lax.broadcasted_iota(jnp.int32, logits.shape, 1)
    hit = (info[:, 2:3].astype(jnp.int32) == words).astype(F32)
    grads = (info[:, 1:2] * (jnp.exp(logits - info[:, 0:1]) - hit)).astype(BF)
    lg[...] = grads
    part = blocks.shape[0] // 4
    for i in range(4):
        span = slice(i * part, (i + 1) * part)
        blocks[span, :] = jnp.dot(z_rows[span, :], grads, preferred_element_type=F32).astype(BF)


def feature_kernel(count, added, core, *refs):
    lgs, emb, out = refs[:count], refs[count], refs[-1]
    value, at = 0.0, 0
    for lg in lgs:
        words = lg.shape[1]
        value += lax.dot_general(
            lg[...], emb[0, :, at : at + words], (((1,), (1,)), ((), ())), preferred_element_type=F32
        )
        at += words
    if added:
        value = value + refs[count + 1][0]
    out[0] = value.astype(BF)


def feature_part(lgs, emb, core, added=None):
    slots, words = lgs[0].shape[0], emb.shape[1]
    out = pl.BlockSpec((1, slots, 256), lambda i, n: (i, 0, 0))
    more = [] if added is None else [added]
    return pl.pallas_call(
        functools.partial(feature_kernel, len(lgs), added is not None),
        grid_spec=pltpu.PrefetchScalarGridSpec(
            num_scalar_prefetch=1,
            grid=(4,),
            in_specs=[pl.BlockSpec(lg.shape, lambda i, n: (0, 0)) for lg in lgs]
            + [pl.BlockSpec((1, 256, words), lambda i, n: (2 * i + n[0], 0, 0))]
            + [out] * len(more),
            out_specs=out,
        ),
        out_shape=jax.ShapeDtypeStruct((4, slots, 256), BF),
        compiler_params=pltpu.CompilerParams(vmem_limit_bytes=48 << 20),
        cost_estimate=pl.CostEstimate(
            flops=2 * slots * words * 1024, bytes_accessed=7 << 20, transcendentals=0
        ),
    )(core.reshape(1).astype(jnp.int32), *lgs, emb.reshape(8, 256, words), *more)


def sum_kernel(got, out):
    low = got[0].astype(F32) + got[1].astype(F32)
    out[...] = (low + (got[2].astype(F32) + got[3].astype(F32))).astype(BF)


def slot_kernel(first, core, *refs):
    if first:
        got, slope, proj, pre, out = refs

        @pl.when(pl.program_id(0) == 0)
        def _():
            total = got[0].astype(F32) + got[1].astype(F32)
            total = total + (got[2].astype(F32) + got[3].astype(F32))
            pre[...] = (total * slope[...]).astype(BF)

    else:
        pre, proj, added, out = refs
    comps = proj.shape[0]
    rows = pre.shape[0] // comps
    for k in range(comps):
        span = slice(k * rows, (k + 1) * rows)
        value = lax.dot_general(
            pre[span, :], proj[k, 0], (((1,), (1,)), ((), ())), preferred_element_type=F32
        )
        if not first:
            value = value + added[0, span, :]
        out[0, span, :] = value.astype(BF)


def slot_part(proj, core, got=None, slope=None, pre=None, added=None):
    comps, _, cols = proj.shape
    slots = (slope if pre is None else pre).shape[0]
    out = pl.BlockSpec((1, slots, cols), lambda i, n: (i, 0, 0))
    rows = pl.BlockSpec((slots, cols), lambda i, n: (0, 0))
    weights = pl.BlockSpec((comps, 1, cols, cols), lambda i, n: (0, 2 * i + n[0], 0, 0))
    view = proj.reshape(comps, 8, cols, cols)
    shape, pre_shape = jax.ShapeDtypeStruct((4, slots, cols), BF), jax.ShapeDtypeStruct((slots, cols), BF)
    if pre is None:
        operands = (got, slope, view)
        specs = [pl.BlockSpec((4, slots, cols), lambda i, n: (0, 0, 0)), rows, weights]
        outs, shapes = [rows, out], [pre_shape, shape]
    else:
        operands, specs, outs, shapes = (pre, view, added), [rows, weights, out], out, shape
    return pl.pallas_call(
        functools.partial(slot_kernel, pre is None),
        grid_spec=pltpu.PrefetchScalarGridSpec(
            num_scalar_prefetch=1, grid=(4,), in_specs=specs, out_specs=outs
        ),
        out_shape=shapes,
        compiler_params=pltpu.CompilerParams(vmem_limit_bytes=48 << 20),
        cost_estimate=pl.CostEstimate(
            flops=2 * slots * cols * 1024, bytes_accessed=3 << 20, transcendentals=0
        ),
    )(core.reshape(1).astype(jnp.int32), *operands)


def whole(a):
    return pl.BlockSpec(a.shape, lambda *_: (0,) * len(a.shape))


def shaped(shape, dtype):
    return jax.ShapeDtypeStruct(shape, dtype)


def in_three(value):
    high = lax.reduce_precision(value, 8, 7)
    middle = lax.reduce_precision(value - high, 8, 7)
    return high.astype(BF), middle.astype(BF), (value - high - middle).astype(BF)


def shards(hidden, routes, targets, saved_lse, target_logprob, prior_weight, projection, embedding):
    highest = lax.Precision.HIGHEST
    tok_dev, model_width = hidden.shape
    route_count = routes.shape[1]
    comp_dev, _, col_count = projection.shape
    voc_dev = embedding.shape[1]
    owners = lax.axis_size(ZX)
    experts_all = comp_dev * owners
    capacity = max(2, (2 * tok_dev * route_count + experts_all - 1) // experts_all)
    slot_count = owners * comp_dev * capacity
    slot_rows = owners * capacity
    slots = comp_dev * slot_rows
    zi, xi, yi, ci = (lax.axis_index(a) for a in ALL)
    vocab_index = yi * 2 + ci
    pos = jnp.stack([yi, ci, vocab_index * voc_dev, zi * 4 + xi]).astype(jnp.int32)
    comp_ids = jnp.arange(experts_all, dtype=jnp.int32)
    per_owner = comp_dev * capacity
    sent_width = 4 * col_count + 128
    operands = (hidden, routes.T, targets[None, :], saved_lse.T, target_logprob.T)
    results = [shaped((slot_count, sent_width), BF), shaped((slot_count, tok_dev), BF)]
    send_rows, dispatch_tokens = pl.pallas_call(
        prep_kernel,
        grid=(1,),
        in_specs=[SCALARS] + [whole(a) for a in operands],
        out_specs=[whole(r) for r in results],
        out_shape=results,
        compiler_params=pltpu.CompilerParams(vmem_limit_bytes=60 << 20),
        cost_estimate=pl.CostEstimate(
            flops=2 * slot_count * tok_dev * sent_width, bytes_accessed=2 << 20, transcendentals=0
        ),
    )(pos, *operands)
    got_rows = exchanged(send_rows.reshape(owners, per_owner, sent_width), ZX)

    pair = jnp.stack([prior_weight, flipped(prior_weight, "c", 1)])
    pair = jnp.where(ci == 0, pair, pair[::-1])
    two = jnp.stack([pair, flipped(pair, "y", 1)])
    two = jnp.where(yi % 2 == 0, two, two[::-1])
    four = jnp.stack([two, flipped(two, "y", 2)])
    four = jnp.where(yi < 2, four, four[::-1])
    prior_all = four.reshape(model_width, experts_all)
    prior_wide = jnp.pad(prior_all, ((0, 0), (0, 128 - experts_all)))
    prior_logits = jnp.dot(hidden, prior_all, preferred_element_type=F32)
    picked = (routes[:, :, None] == comp_ids[None, None, :]).astype(F32)
    selected = jnp.sum(picked * prior_logits[:, None, :], axis=2)
    gate_weights = jax.nn.softmax(selected, axis=-1)
    posterior = jax.nn.softmax(jax.nn.log_softmax(selected, axis=-1) + target_logprob, axis=-1)
    prior_grads = jnp.sum((gate_weights - posterior)[:, :, None] * picked, axis=1)
    prior_back = lax.dot_general(
        prior_grads, prior_weight.astype(F32), (((1,), (1,)), ((), ())), precision=highest
    )
    got_rows, prior_wide, prior_back = lax.optimization_barrier((got_rows, prior_wide, prior_back))

    rows_in = (got_rows, flipped(got_rows, "c", 1))
    operands = (*rows_in, projection, prior_wide)
    results = [
        shaped((slots, col_count), F32),
        shaped((slots, col_count), BF),
        shaped((slots, 128), F32),
        shaped((8, col_count), F32),
    ]
    slope, z_own, info, prior_own = pl.pallas_call(
        activation_kernel,
        grid=(1,),
        in_specs=[SCALARS] + [whole(a) for a in operands],
        out_specs=[whole(r) for r in results],
        out_shape=results,
        compiler_params=pltpu.CompilerParams(vmem_limit_bytes=48 << 20),
        cost_estimate=pl.CostEstimate(
            flops=2 * slots * model_width * col_count, bytes_accessed=6 << 20, transcendentals=slots * col_count
        ),
    )(pos, *operands)
    z_all = gathered(z_own)

    width = 512
    grads, blocks = pl.pallas_call(
        logit_kernel,
        grid=(voc_dev // width,),
        in_specs=[SCALARS]
        + [whole(a) for a in (*z_all, info)]
        + [pl.BlockSpec((model_width, width), lambda i: (0, i))],
        out_specs=[
            pl.BlockSpec((slots, width), lambda i: (0, i)),
            pl.BlockSpec((model_width, width), lambda i: (0, i)),
        ],
        out_shape=[shaped((slots, voc_dev), BF), shaped((model_width, voc_dev), BF)],
        scratch_shapes=[pltpu.VMEM((slots, model_width), BF), pltpu.VMEM((model_width, slots), BF)],
        compiler_params=pltpu.CompilerParams(vmem_limit_bytes=50 << 20),
        cost_estimate=pl.CostEstimate(
            flops=4 * slots * model_width * voc_dev, bytes_accessed=24 << 20, transcendentals=slots * voc_dev
        ),
    )(pos, *z_all, info, embedding)
    logit_grads = (grads,)
    z_sum = summed_along_z(blocks)

    feature_theirs = flipped(feature_part(logit_grads, embedding, 1 - ci), "c", 1)
    feature_both = feature_part(logit_grads, embedding, ci, feature_theirs)
    feature_got = exchanged(feature_both, "y")
    pre_grads, slot_theirs = slot_part(projection, 1 - ci, got=feature_got, slope=slope)
    slot_both = slot_part(projection, ci, pre=pre_grads, added=flipped(slot_theirs, "c", 1))
    slot_got = exchanged(slot_both, "y")
    slot_grads = jnp.sum(slot_got.astype(F32), axis=0).astype(BF)
    out_shape = shaped(projection.shape, BF)
    grad_projection = pl.pallas_call(
        projection_kernel,
        grid=(1,),
        in_specs=[SCALARS] + [whole(a) for a in (*rows_in, pre_grads)],
        out_specs=whole(out_shape),
        out_shape=out_shape,
        compiler_params=pltpu.CompilerParams(vmem_limit_bytes=48 << 20),
        cost_estimate=pl.CostEstimate(
            flops=2 * slots * model_width * col_count, bytes_accessed=4 << 20, transcendentals=0
        ),
    )(pos, *rows_in, pre_grads)

    pad = jnp.zeros((8 - 3 * comp_dev, col_count), BF)
    prior_pieces = jnp.concatenate([*in_three(prior_own[:comp_dev]), pad], axis=0)
    slot_grads = slot_grads.reshape(comp_dev, owners, capacity, col_count).transpose(1, 0, 2, 3)
    slot_grads = slot_grads.reshape(owners, per_owner, col_count)
    to_return = jnp.concatenate(
        [slot_grads, jnp.broadcast_to(prior_pieces, (owners, *prior_pieces.shape))], axis=1
    )
    returned = exchanged(to_return, ZX)
    route_grads = lax.dot_general(
        dispatch_tokens,
        returned[:, :per_owner].reshape(slot_count, col_count),
        (((0,), (0,)), ((), ())),
        preferred_element_type=F32,
    )
    pieces = returned[:, per_owner : per_owner + 3 * comp_dev].astype(F32)
    pieces = pieces.reshape(owners, 3, comp_dev, col_count)
    grad_prior = (pieces[:, 0] + (pieces[:, 1] + pieces[:, 2])).reshape(experts_all, col_count).T
    grad_hidden = route_grads + prior_back

    z_sum, returned = lax.optimization_barrier((z_sum, returned))
    got = exchanged(z_sum.reshape(4, 64, -1), "x")
    summed = shaped(got.shape[1:], BF)
    grad_embedding = pl.pallas_call(
        sum_kernel,
        grid=(4,),
        in_specs=[pl.BlockSpec((4, 64, voc_dev // 4), lambda i: (0, 0, i))],
        out_specs=pl.BlockSpec((64, voc_dev // 4), lambda i: (0, i)),
        out_shape=summed,
        compiler_params=pltpu.CompilerParams(vmem_limit_bytes=48 << 20),
        cost_estimate=pl.CostEstimate(flops=4 * 64 * voc_dev, bytes_accessed=640 * voc_dev, transcendentals=0),
    )(got)
    return (grad_hidden, grad_prior, grad_projection, grad_embedding)


def solution(mesh):
    finer = Mesh(mesh.devices.reshape(8, 4, 4, 2), ALL)
    in_specs = (
        P(ZX, None),
        P(ZX, None),
        P(ZX),
        P(ZX, None),
        P(ZX, None),
        P(YC, None),
        P(ZX, None, YC),
        P(None, YC),
    )
    out_specs = (P(ZX, YC), P(YC, None), P(ZX, None, YC), P(ZX, YC))
    return jax.shard_map(
        shards, mesh=finer, in_specs=in_specs, out_specs=out_specs, check_vma=False
    )
```

```python
import functools

import jax
import jax.numpy as jnp
from jax import lax
from jax.experimental import pallas as pl
from jax.experimental.pallas import tpu as pltpu
from jax.sharding import Mesh
from jax.sharding import PartitionSpec as P

ZX = ("z", "x")
YC = ("y", "c")
ALL = ("z", "x", "y", "c")
BF = jnp.bfloat16
F32 = jnp.float32
SCALARS = pl.BlockSpec(memory_space=pltpu.SMEM)


def shifted(value, axis, by):
    n = lax.axis_size(axis)
    return lax.ppermute(value, axis, [(i, (i + by) % n) for i in range(n)])


def flipped(value, axis, bit):
    n = lax.axis_size(axis)
    return lax.ppermute(value, axis, [(i, i ^ bit) for i in range(n)])


def pick(value, index, dim):
    return lax.dynamic_index_in_dim(value, index, dim, keepdims=False)


def gathered(value):
    half = value.shape[0] // 2
    below = shifted(value, "y", 1)
    above = shifted(value, "y", -1)
    far_low = shifted(below[:half], "y", 1)
    far_high = shifted(above[half:], "y", -1)
    near = jnp.stack([value, above, below])
    far = jnp.concatenate([far_low, far_high], axis=0)
    return near, far, flipped(near, "c", 1), flipped(far, "c", 1)


def exchanged(value, axis):
    return lax.all_to_all(value, axis, 0, 0, tiled=True)


def summed_along_z(blocks):
    return lax.psum_scatter(blocks, "z", scatter_dimension=0, tiled=True)


def piece_rows(refs, k, rows):
    span = slice(k * rows, (k + 1) * rows)
    for side in range(2):
        near, far = refs[2 * side : 2 * side + 2]
        yield 0, side, near[0, span, :]
        yield 1, side, near[1, span, :]
        yield 3, side, near[2, span, :]
        yield 2, side, far[span, :]


def component_rows(ref, k, columns):
    owners, slots, _ = ref.shape
    part = ref[:, k * (slots // 2) : (k + 1) * (slots // 2), columns]
    return part.reshape(owners * slots // 2, part.shape[2])


def half_rows(refs, k, cols):
    for side in range(2):
        for y in range(4):
            yield y, side, component_rows(refs[side], k, slice(y * cols, (y + 1) * cols))


def core_start(pos, y, side, cols):
    c = pos[1] if side == 0 else 1 - pos[1]
    return pl.multiple_of((y * 2 + c) * cols, cols)


def block_start(pos, dist, side, cols):
    y = lax.rem(pos[0] + dist, 4)
    c = pos[1] if side == 0 else 1 - pos[1]
    return pl.multiple_of((y * 2 + c) * cols, cols)


def prep_kernel(hidden, routes, targets, lse, tlp, send, table):
    tokens = hidden.shape[0]
    slots = table.shape[0]
    cap = slots // tokens
    ids = lax.broadcasted_iota(jnp.int32, (tokens, tokens), 0)
    token = lax.broadcasted_iota(jnp.int32, (tokens, tokens), 1)
    chosen = [(ids == routes[j : j + 1, :]).astype(F32) for j in range(4)]
    mask = chosen[0] + chosen[1] + (chosen[2] + chosen[3])
    rank = jnp.dot(mask.astype(BF), (ids < token).astype(BF), preferred_element_type=F32)
    place = (mask * (rank + 1.0)).astype(BF)
    slot = lax.broadcasted_iota(jnp.int32, (slots, tokens), 0)
    comp = lax.broadcasted_iota(jnp.int32, (slots, tokens), 1)
    spread = (lax.div(slot, cap) == comp).astype(BF)
    number = jnp.dot(spread, place, preferred_element_type=F32)
    hits = (number == (lax.rem(slot, cap) + 1).astype(F32)).astype(BF)
    table[...] = hits
    at = lax.broadcasted_iota(jnp.int32, (128, tokens), 0)
    t = targets[...]
    numbers = jnp.where(at == 0, lax.div(t, 128).astype(F32), jnp.where(at == 1, lax.rem(t, 128).astype(F32), 0.0))
    for j in range(4):
        numbers = jnp.where(at == 2 + j, (routes[j : j + 1, :] + 1).astype(F32), numbers)
        for base, ref in ((6, lse), (18, tlp)):
            value = ref[j : j + 1, :]
            high = value.astype(BF).astype(F32)
            middle = (value - high).astype(BF).astype(F32)
            numbers = jnp.where(at == base + j, high, numbers)
            numbers = jnp.where(at == base + 4 + j, middle, numbers)
            numbers = jnp.where(at == base + 8 + j, value - high - middle, numbers)
    core = lax.axis_index("c")
    for y in range(4):
        columns = hidden[:, pl.ds(pl.multiple_of((y * 2 + core) * 256, 256), 256)]
        rows_out = jnp.dot(hits, columns, preferred_element_type=F32)
        send[:, y * 256 : (y + 1) * 256] = rows_out.astype(BF)
    picked = lax.dot_general(
        hits, numbers.astype(BF), (((1,), (1,)), ((), ())), preferred_element_type=F32
    )
    send[:, 1024:] = picked.astype(BF)


def posterior_of(prior, meta, me):
    ids = lax.broadcasted_iota(jnp.int32, prior.shape, 0).astype(F32) + 1.0
    route = [meta[2 + j : 3 + j] for j in range(4)]
    lse = [meta[6 + j : 7 + j] + (meta[10 + j : 11 + j] + meta[14 + j : 15 + j]) for j in range(4)]
    tlp = [meta[18 + j : 19 + j] + (meta[22 + j : 23 + j] + meta[26 + j : 27 + j]) for j in range(4)]
    chosen = [jnp.sum(jnp.where(ids == route[j], prior, 0.0), axis=0, keepdims=True) for j in range(4)]

    def softmax(values):
        top = functools.reduce(jnp.maximum, values)
        powers = [jnp.exp(v - top) for v in values]
        total = sum(powers[1:], powers[0])
        return [p / total for p in powers], [v - top - jnp.log(total) for v in values]

    gate, log_gate = softmax(chosen)
    post, _ = softmax([log_gate[j] + tlp[j] for j in range(4)])
    mine = [(route[j] == me).astype(F32) for j in range(4)]

    def own(values):
        return sum([mine[j] * values[j] for j in range(1, 4)], mine[0] * values[0])

    target = meta[0:1] * 128.0 + meta[1:2]
    return own(lse), own(post), target, own([gate[j] - post[j] for j in range(4)])


def activation_kernel(pos, mine, other, proj, prior, slope, z, info, sums):
    comps, _, cols = proj.shape
    rows = slope.shape[0] // comps
    row = lax.broadcasted_iota(jnp.int32, (info.shape[1], rows), 0)
    for k in range(comps):
        span = slice(k * rows, (k + 1) * rows)
        total = jnp.zeros((rows, cols), F32)
        logits = jnp.zeros((rows, prior.shape[1]), F32)
        for y, side, x in half_rows((mine, other), k, cols):
            place = pl.ds(core_start(pos, y, side, cols), cols)
            total += jnp.dot(x, proj[k, place, :], preferred_element_type=F32)
            logits += jnp.dot(x, prior[place, :], preferred_element_type=F32)
        t = jnp.tanh(total)
        slope[span, :] = 1.0 - t * t
        z[span, :] = t.astype(BF)
        me = (pos[3] * comps + k + 1).astype(F32)
        lse, post, target, grad = posterior_of(logits.T, component_rows(mine, k, slice(4 * cols, 4 * cols + 128)).astype(F32).T, me)
        columns = jnp.where(row == 0, lse, jnp.where(row == 1, post, jnp.where(row == 2, target, grad))).T
        info[span, :] = columns
        sums[k : k + 1, :] = jnp.sum(component_rows(mine, k, pl.ds(pl.multiple_of(pos[0] * cols, cols), cols)).astype(F32) * columns[:, 3:4], axis=0, keepdims=True)


def projection_kernel(pos, mine, other, pre, out):
    comps, _, cols = out.shape
    rows = pre.shape[0] // comps
    for k in range(comps):
        g = pre[k * rows : (k + 1) * rows, :]
        for y, side, x in half_rows((mine, other), k, cols):
            value = lax.dot_general(x, g, (((0,), (0,)), ((), ())), preferred_element_type=F32)
            out[k, pl.ds(core_start(pos, y, side, cols), cols), :] = value.astype(BF)


def logit_kernel(pos, near, far, near_o, far_o, info, emb, lg, blocks, z, z_rows):
    step = pl.program_id(0)
    rows, cols = far.shape
    width = emb.shape[1]

    @pl.when(step == 0)
    def _():
        for dist, side, x in piece_rows((near, far, near_o, far_o), 0, rows):
            start = block_start(pos, dist, side, cols)
            z[:, pl.ds(start, cols)] = x
            z_rows[pl.ds(start, cols), :] = x.T

    logits = jnp.dot(z[...], emb[...], preferred_element_type=F32)
    words = pos[2] + step * width + lax.broadcasted_iota(jnp.int32, logits.shape, 1)
    hit = (info[:, 2:3].astype(jnp.int32) == words).astype(F32)
    grads = (info[:, 1:2] * (jnp.exp(logits - info[:, 0:1]) - hit)).astype(BF)
    lg[...] = grads
    part = blocks.shape[0] // 4
    for i in range(4):
        span = slice(i * part, (i + 1) * part)
        blocks[span, :] = jnp.dot(z_rows[span, :], grads, preferred_element_type=F32).astype(BF)


def feature_kernel(count, added, core, *refs):
    lgs, emb, out = refs[:count], refs[count], refs[-1]
    value, at = 0.0, 0
    for lg in lgs:
        words = lg.shape[1]
        value += lax.dot_general(
            lg[...], emb[0, :, at : at + words], (((1,), (1,)), ((), ())), preferred_element_type=F32
        )
        at += words
    if added:
        value = value + refs[count + 1][0]
    out[0] = value.astype(BF)


def feature_part(lgs, emb, core, added=None):
    slots, words = lgs[0].shape[0], emb.shape[1]
    out = pl.BlockSpec((1, slots, 256), lambda i, n: (i, 0, 0))
    more = [] if added is None else [added]
    return pl.pallas_call(
        functools.partial(feature_kernel, len(lgs), added is not None),
        grid_spec=pltpu.PrefetchScalarGridSpec(
            num_scalar_prefetch=1,
            grid=(4,),
            in_specs=[pl.BlockSpec(lg.shape, lambda i, n: (0, 0)) for lg in lgs]
            + [pl.BlockSpec((1, 256, words), lambda i, n: (2 * i + n[0], 0, 0))]
            + [out] * len(more),
            out_specs=out,
        ),
        out_shape=jax.ShapeDtypeStruct((4, slots, 256), BF),
        compiler_params=pltpu.CompilerParams(vmem_limit_bytes=48 << 20),
        cost_estimate=pl.CostEstimate(
            flops=2 * slots * words * 1024, bytes_accessed=7 << 20, transcendentals=0
        ),
    )(core.reshape(1).astype(jnp.int32), *lgs, emb.reshape(8, 256, words), *more)


def sum_kernel(got, out):
    low = got[0].astype(F32) + got[1].astype(F32)
    out[...] = (low + (got[2].astype(F32) + got[3].astype(F32))).astype(BF)


def slot_kernel(first, core, *refs):
    if first:
        got, slope, proj, pre, out = refs

        @pl.when(pl.program_id(0) == 0)
        def _():
            total = got[0].astype(F32) + got[1].astype(F32)
            total = total + (got[2].astype(F32) + got[3].astype(F32))
            pre[...] = (total * slope[...]).astype(BF)

    else:
        pre, proj, added, out = refs
    comps = proj.shape[0]
    rows = pre.shape[0] // comps
    for k in range(comps):
        span = slice(k * rows, (k + 1) * rows)
        value = lax.dot_general(
            pre[span, :], proj[k, 0], (((1,), (1,)), ((), ())), preferred_element_type=F32
        )
        if not first:
            value = value + added[0, span, :]
        out[0, span, :] = value.astype(BF)


def slot_part(proj, core, got=None, slope=None, pre=None, added=None):
    comps, _, cols = proj.shape
    slots = (slope if pre is None else pre).shape[0]
    out = pl.BlockSpec((1, slots, cols), lambda i, n: (i, 0, 0))
    rows = pl.BlockSpec((slots, cols), lambda i, n: (0, 0))
    weights = pl.BlockSpec((comps, 1, cols, cols), lambda i, n: (0, 2 * i + n[0], 0, 0))
    view = proj.reshape(comps, 8, cols, cols)
    shape, pre_shape = jax.ShapeDtypeStruct((4, slots, cols), BF), jax.ShapeDtypeStruct((slots, cols), BF)
    if pre is None:
        operands = (got, slope, view)
        specs = [pl.BlockSpec((4, slots, cols), lambda i, n: (0, 0, 0)), rows, weights]
        outs, shapes = [rows, out], [pre_shape, shape]
    else:
        operands, specs, outs, shapes = (pre, view, added), [rows, weights, out], out, shape
    return pl.pallas_call(
        functools.partial(slot_kernel, pre is None),
        grid_spec=pltpu.PrefetchScalarGridSpec(
            num_scalar_prefetch=1, grid=(4,), in_specs=specs, out_specs=outs
        ),
        out_shape=shapes,
        compiler_params=pltpu.CompilerParams(vmem_limit_bytes=48 << 20),
        cost_estimate=pl.CostEstimate(
            flops=2 * slots * cols * 1024, bytes_accessed=3 << 20, transcendentals=0
        ),
    )(core.reshape(1).astype(jnp.int32), *operands)


def whole(a):
    return pl.BlockSpec(a.shape, lambda *_: (0,) * len(a.shape))


def shaped(shape, dtype):
    return jax.ShapeDtypeStruct(shape, dtype)


def in_three(value):
    high = lax.reduce_precision(value, 8, 7)
    middle = lax.reduce_precision(value - high, 8, 7)
    return high.astype(BF), middle.astype(BF), (value - high - middle).astype(BF)


def shards(hidden, routes, targets, saved_lse, target_logprob, prior_weight, projection, embedding):
    highest = lax.Precision.HIGHEST
    tok_dev, model_width = hidden.shape
    route_count = routes.shape[1]
    comp_dev, _, col_count = projection.shape
    voc_dev = embedding.shape[1]
    owners = lax.axis_size(ZX)
    experts_all = comp_dev * owners
    capacity = max(2, (2 * tok_dev * route_count + experts_all - 1) // experts_all)
    slot_count = owners * comp_dev * capacity
    slot_rows = owners * capacity
    slots = comp_dev * slot_rows
    zi, xi, yi, ci = (lax.axis_index(a) for a in ALL)
    vocab_index = yi * 2 + ci
    pos = jnp.stack([yi, ci, vocab_index * voc_dev, zi * 4 + xi]).astype(jnp.int32)
    comp_ids = jnp.arange(experts_all, dtype=jnp.int32)
    per_owner = comp_dev * capacity
    sent_width = 4 * col_count + 128
    operands = (hidden, routes.T, targets[None, :], saved_lse.T, target_logprob.T)
    results = [shaped((slot_count, sent_width), BF), shaped((slot_count, tok_dev), BF)]
    send_rows, dispatch_tokens = pl.pallas_call(
        prep_kernel,
        grid=(1,),
        in_specs=[whole(a) for a in operands],
        out_specs=[whole(r) for r in results],
        out_shape=results,
        compiler_params=pltpu.CompilerParams(vmem_limit_bytes=60 << 20),
        cost_estimate=pl.CostEstimate(
            flops=2 * slot_count * tok_dev * sent_width, bytes_accessed=2 << 20, transcendentals=0
        ),
    )(*operands)
    got_rows = exchanged(send_rows.reshape(owners, per_owner, sent_width), ZX)

    pair = jnp.stack([prior_weight, flipped(prior_weight, "c", 1)])
    pair = jnp.where(ci == 0, pair, pair[::-1])
    two = jnp.stack([pair, flipped(pair, "y", 1)])
    two = jnp.where(yi % 2 == 0, two, two[::-1])
    four = jnp.stack([two, flipped(two, "y", 2)])
    four = jnp.where(yi < 2, four, four[::-1])
    prior_all = four.reshape(model_width, experts_all)
    prior_wide = jnp.pad(prior_all, ((0, 0), (0, 128 - experts_all)))
    prior_logits = jnp.dot(hidden, prior_all, preferred_element_type=F32)
    picked = (routes[:, :, None] == comp_ids[None, None, :]).astype(F32)
    selected = jnp.sum(picked * prior_logits[:, None, :], axis=2)
    gate_weights = jax.nn.softmax(selected, axis=-1)
    posterior = jax.nn.softmax(jax.nn.log_softmax(selected, axis=-1) + target_logprob, axis=-1)
    prior_grads = jnp.sum((gate_weights - posterior)[:, :, None] * picked, axis=1)
    prior_back = lax.dot_general(
        prior_grads, prior_weight.astype(F32), (((1,), (1,)), ((), ())), precision=highest
    )
    got_rows, prior_wide, prior_back = lax.optimization_barrier((got_rows, prior_wide, prior_back))

    rows_in = (got_rows, flipped(got_rows, "c", 1))
    operands = (*rows_in, projection, prior_wide)
    results = [
        shaped((slots, col_count), F32),
        shaped((slots, col_count), BF),
        shaped((slots, 128), F32),
        shaped((8, col_count), F32),
    ]
    slope, z_own, info, prior_own = pl.pallas_call(
        activation_kernel,
        grid=(1,),
        in_specs=[SCALARS] + [whole(a) for a in operands],
        out_specs=[whole(r) for r in results],
        out_shape=results,
        compiler_params=pltpu.CompilerParams(vmem_limit_bytes=48 << 20),
        cost_estimate=pl.CostEstimate(
            flops=2 * slots * model_width * col_count, bytes_accessed=6 << 20, transcendentals=slots * col_count
        ),
    )(pos, *operands)
    z_all = gathered(z_own)

    width = 512
    grads, blocks = pl.pallas_call(
        logit_kernel,
        grid=(voc_dev // width,),
        in_specs=[SCALARS]
        + [whole(a) for a in (*z_all, info)]
        + [pl.BlockSpec((model_width, width), lambda i: (0, i))],
        out_specs=[
            pl.BlockSpec((slots, width), lambda i: (0, i)),
            pl.BlockSpec((model_width, width), lambda i: (0, i)),
        ],
        out_shape=[shaped((slots, voc_dev), BF), shaped((model_width, voc_dev), BF)],
        scratch_shapes=[pltpu.VMEM((slots, model_width), BF), pltpu.VMEM((model_width, slots), BF)],
        compiler_params=pltpu.CompilerParams(vmem_limit_bytes=50 << 20),
        cost_estimate=pl.CostEstimate(
            flops=4 * slots * model_width * voc_dev, bytes_accessed=24 << 20, transcendentals=slots * voc_dev
        ),
    )(pos, *z_all, info, embedding)
    logit_grads = (grads,)
    z_sum = summed_along_z(blocks)

    feature_theirs = flipped(feature_part(logit_grads, embedding, 1 - ci), "c", 1)
    feature_both = feature_part(logit_grads, embedding, ci, feature_theirs)
    feature_got = exchanged(feature_both, "y")
    pre_grads, slot_theirs = slot_part(projection, 1 - ci, got=feature_got, slope=slope)
    slot_both = slot_part(projection, ci, pre=pre_grads, added=flipped(slot_theirs, "c", 1))
    slot_got = exchanged(slot_both, "y")
    slot_grads = jnp.sum(slot_got.astype(F32), axis=0).astype(BF)
    out_shape = shaped(projection.shape, BF)
    grad_projection = pl.pallas_call(
        projection_kernel,
        grid=(1,),
        in_specs=[SCALARS] + [whole(a) for a in (*rows_in, pre_grads)],
        out_specs=whole(out_shape),
        out_shape=out_shape,
        compiler_params=pltpu.CompilerParams(vmem_limit_bytes=48 << 20),
        cost_estimate=pl.CostEstimate(
            flops=2 * slots * model_width * col_count, bytes_accessed=4 << 20, transcendentals=0
        ),
    )(pos, *rows_in, pre_grads)

    pad = jnp.zeros((8 - 3 * comp_dev, col_count), BF)
    prior_pieces = jnp.concatenate([*in_three(prior_own[:comp_dev]), pad], axis=0)
    slot_grads = slot_grads.reshape(comp_dev, owners, capacity, col_count).transpose(1, 0, 2, 3)
    slot_grads = slot_grads.reshape(owners, per_owner, col_count)
    to_return = jnp.concatenate(
        [slot_grads, jnp.broadcast_to(prior_pieces, (owners, *prior_pieces.shape))], axis=1
    )
    returned = exchanged(to_return, ZX)
    route_grads = lax.dot_general(
        dispatch_tokens,
        returned[:, :per_owner].reshape(slot_count, col_count),
        (((0,), (0,)), ((), ())),
        preferred_element_type=F32,
    )
    pieces = returned[:, per_owner : per_owner + 3 * comp_dev].astype(F32)
    pieces = pieces.reshape(owners, 3, comp_dev, col_count)
    grad_prior = (pieces[:, 0] + (pieces[:, 1] + pieces[:, 2])).reshape(experts_all, col_count).T
    grad_hidden = route_grads + prior_back

    z_sum, returned = lax.optimization_barrier((z_sum, returned))
    got = exchanged(z_sum.reshape(4, 64, -1), "x")
    summed = shaped(got.shape[1:], BF)
    grad_embedding = pl.pallas_call(
        sum_kernel,
        grid=(2,),
        in_specs=[pl.BlockSpec((4, 64, voc_dev // 2), lambda i: (0, 0, i))],
        out_specs=pl.BlockSpec((64, voc_dev // 2), lambda i: (0, i)),
        out_shape=summed,
        compiler_params=pltpu.CompilerParams(vmem_limit_bytes=48 << 20),
        cost_estimate=pl.CostEstimate(flops=4 * 64 * voc_dev, bytes_accessed=640 * voc_dev, transcendentals=0),
    )(got)
    return (grad_hidden, grad_prior, grad_projection, grad_embedding)


def solution(mesh):
    finer = Mesh(mesh.devices.reshape(8, 4, 4, 2), ALL)
    in_specs = (
        P(ZX, None),
        P(ZX, None),
        P(ZX),
        P(ZX, None),
        P(ZX, None),
        P(YC, None),
        P(ZX, None, YC),
        P(None, YC),
    )
    out_specs = (P(ZX, YC), P(YC, None), P(ZX, None, YC), P(ZX, YC))
    return jax.shard_map(
        shards, mesh=finer, in_specs=in_specs, out_specs=out_specs, check_vma=False
    )
```
